128 devices in a mesh: blk: 16 (over y_hi, x, core), kv: 8 (over z, y_lo).
Axes of the slice: x: 4, y: 4 (y_hi: 2, y_lo: 2; y = y_hi * 2 + y_lo), z: 4, core: 2. Of those that a mesh axis runs over, the one named last changes fastest.
Arguments:
- tokens: bfloat16 [8192, 2560], P('blk'), may hold values from -6 to 6
- attn_gain: float32 [2560], replicated, may hold values from 0.1 to 1.9
- mlp_gain: float32 [2560], replicated, may hold values from 0.1 to 1.9
- w_query: float32 [2560, 2560], P(('blk', 'kv')), may hold values from -0.375 to 0.375
- w_key: float32 [2560, 640], P(('blk', 'kv')), may hold values from -0.125 to 0.125
- w_value: float32 [2560, 640], P(('blk', 'kv')), may hold values from -0.125 to 0.125
- w_gate: float32 [2560, 6912], P(('blk', 'kv')), may hold values from -0.125 to 0.125
- w_up: float32 [2560, 6912], P(('blk', 'kv')), may hold values from -0.125 to 0.125
- w_out: bfloat16 [2560, 2560], P('kv'), may hold values from -0.125 to 0.125
- w_down: bfloat16 [6912, 2560], P('kv'), may hold values from -0.078125 to 0.078125
- cache: bfloat16 [2, 128, 8, 80, 128], P(None, 'blk', 'kv'), may hold values from -300 to 300
- slot_prompt: int32 [128], replicated, may hold values from 0 to 15, as said below
- prefix_len: int32 [16], replicated, may hold values from 1 to 4096, as said below
- new_len: int32 [16], replicated, may hold values from 256 to 512, as said below
Outputs:
- mixed: bfloat16 [8192, 2560], P('blk', 'kv')
The draws below stay inside these ranges and needn't reach their ends.
Inputs may be any that keep to these rules, and one draw needn't show every extreme that they name: `slot_prompt`: the 8 slots of one index of blk hold at most 2 blocks of one prompt. One prompt, drawn afresh, has exactly 2 blocks on every index of blk; the other 6 slots of an index hold blocks of distinct prompts; every prompt has at least one block. `prefix_len`: A prompt with c slots has a prefix longer than (c - 1) * 128 and at most c * 128. Rows i >= new_len[p] of prompt p are padding.
All inputs are finite; a program needn't handle non-finite values.
Results may differ from the reference program's by a relative error of at most 0.019.
The reference program's roundings to bfloat16 on the way (of `normed`, `attended`, `middle`, `normed_mid` and `hidden`) count: a program that leaves them out, or rounds other values in their place, can miss the bound.
Values may be sent and summed in bfloat16 or wider, within the bound.
A program may use at most 128 MiB of HBM per device.

```python
import math
import jax
import jax.numpy as jnp
from jax import lax

D = 2560
HEADS = 32
KV_HEADS = 8
HD = 80
FF = 6912
WINDOW = 4096
SINKS = 4
NEW = 512
BLOCK = 128
SLOTS = 8
CAP = 2
PROMPTS = 16
TOKENS = 8192
PREFIX_BLOCKS = 32


def slot_layout(key):
    base_key = jax.random.fold_in(key, 1234)
    pick_key, order_key, offset_key, shuffle_key, tail_key = jax.random.split(base_key, 5)
    heavy = jax.random.randint(pick_key, (), 0, PROMPTS)
    others = jax.random.permutation(order_key, PROMPTS - 1)
    offset_value = jax.random.randint(offset_key, (), 0, PROMPTS - 1)
    source = jnp.arange(PROMPTS, dtype=jnp.int32)[:, None]
    within = jnp.arange(SLOTS, dtype=jnp.int32)[None, :]
    cyclic = (source * (SLOTS - CAP) + within - CAP + offset_value) % (PROMPTS - 1)
    other_prompt = others[cyclic]
    other_prompt = other_prompt + (other_prompt >= heavy).astype(jnp.int32)
    table = jnp.where(within < CAP, heavy, other_prompt).astype(jnp.int32)
    shuffles = jax.vmap(lambda subkey: jax.random.permutation(subkey, SLOTS))(jax.random.split(shuffle_key, PROMPTS))
    table = jnp.take_along_axis(table, shuffles, axis=1).reshape(-1)
    counts = jnp.sum((table[:, None] == jnp.arange(PROMPTS, dtype=jnp.int32)[None, :]).astype(jnp.int32), axis=0)
    tails = jax.random.randint(tail_key, (PROMPTS,), 1, BLOCK + 1)
    tails = jnp.where(jnp.arange(PROMPTS, dtype=jnp.int32) == heavy, BLOCK, tails)
    lengths = (counts - 1) * BLOCK + tails
    return (table.astype(jnp.int32), lengths.astype(jnp.int32))


def draw_slot_prompt(key, part):
    return slot_layout(key)[0]


def draw_prefix_len(key, part):
    return slot_layout(key)[1]


def draw_new_len(key, part):
    length_key, pick_key = jax.random.split(jax.random.fold_in(key, 99))
    drawn = jax.random.randint(length_key, (PROMPTS,), NEW // 2, NEW + 1)
    longest = jax.random.randint(pick_key, (), 0, PROMPTS)
    return jnp.where(jnp.arange(PROMPTS, dtype=jnp.int32) == longest, NEW, drawn).astype(jnp.int32)


def draw_cache(key, part):
    full_shape = (2, PROMPTS * SLOTS, KV_HEADS, HD, BLOCK)
    noise_key = jax.random.fold_in(jax.random.fold_in(key, 5), 0)
    values = jnp.clip(jax.random.normal(noise_key, full_shape, dtype=jnp.float32), -5.0, 5.0)
    return values.astype(jnp.bfloat16)


def shard_levels(rng, extent, cuts, low, largest):
    gain = 1.0
    for dim, blocks in cuts:
        draws = jax.random.uniform(jax.random.fold_in(jax.random.fold_in(rng, 6), dim), (blocks,), jnp.float32, low / len(cuts), largest / len(cuts))
        gain = gain * jnp.repeat(jnp.exp(draws), extent[dim] // blocks).reshape((-1,) + (1,) * (len(extent) - 1 - dim))
    return gain


def bell_draw(own_key, extent, scale, reach, cuts=(), held_as=jnp.bfloat16):
    array = scale * jax.random.normal(own_key, extent, jnp.float32)
    if cuts:
        array = array * shard_levels(own_key, extent, cuts, -0.22, 0.18)
    return jnp.clip(array, -reach, reach).astype(held_as)


def setup_inputs(seed: int = 0) -> dict:
    seeds = jax.random.split(jax.random.key(seed), 15)
    tokens = bell_draw(seeds[0], (TOKENS, D), 1.0, 6.0, ((0, 16),))
    attn_gain = jnp.clip(1.0 + 0.18 * jax.random.normal(seeds[1], (D,), jnp.float32), 0.1, 1.9)
    mlp_gain = jnp.clip(1.0 + 0.18 * jax.random.normal(seeds[2], (D,), jnp.float32), 0.1, 1.9)
    w_query = bell_draw(seeds[3], (D, HEADS * HD), (D // 9) ** -0.5, 0.375, ((0, 128),), jnp.float32)
    w_key = bell_draw(seeds[4], (D, KV_HEADS * HD), D ** -0.5, 0.125, ((0, 128),), jnp.float32)
    w_value = bell_draw(seeds[5], (D, KV_HEADS * HD), D ** -0.5, 0.125, ((0, 128),), jnp.float32)
    w_gate = bell_draw(seeds[6], (D, FF), D ** -0.5, 0.125, ((0, 128),), jnp.float32)
    w_up = bell_draw(seeds[7], (D, FF), D ** -0.5, 0.125, ((0, 128),), jnp.float32)
    w_out = bell_draw(seeds[8], (HEADS * HD, D), (HEADS * HD) ** -0.5, 0.125, ((0, 8),))
    w_down = bell_draw(seeds[9], (FF, D), FF ** -0.5, 0.078125, ((0, 8),))
    cache = draw_cache(jax.random.fold_in(seeds[14], 71), 0)
    slot_prompt = draw_slot_prompt(jax.random.fold_in(seeds[14], 71), 0)
    prefix_len = draw_prefix_len(jax.random.fold_in(seeds[14], 71), 0)
    new_len = draw_new_len(jax.random.fold_in(seeds[14], 71), 0)
    return {"tokens": tokens, "attn_gain": attn_gain, "mlp_gain": mlp_gain, "w_query": w_query, "w_key": w_key, "w_value": w_value, "w_gate": w_gate, "w_up": w_up, "w_out": w_out, "w_down": w_down, "cache": cache, "slot_prompt": slot_prompt, "prefix_len": prefix_len, "new_len": new_len}


FLOOR_SCORE = -1e+30
EPSILON = 1e-05
ROPE_BASE = 10000.0

def rms_scale(row_data, gain_vec):
    values = row_data.astype(jnp.float32)
    mean_square = lax.optimization_barrier(jnp.mean(values * values, axis=-1, keepdims=True))
    return (values * lax.rsqrt(mean_square + EPSILON) * gain_vec).astype(jnp.bfloat16)

def rotate(values, positions):
    head_width = values.shape[-1]
    half_width = head_width // 2
    frequency = ROPE_BASE ** (-2.0 * jnp.arange(half_width, dtype=jnp.float32) / head_width)
    angles = positions.astype(jnp.float32)[:, None] * frequency[None, :]
    cosine = jnp.cos(angles)[:, None, :]
    sine_wave = jnp.sin(angles)[:, None, :]
    first_half = values[..., :half_width]
    second_half = values[..., half_width:]
    return jnp.concatenate([first_half * cosine - second_half * sine_wave, second_half * cosine + first_half * sine_wave], axis=-1)

def slot_ranks(slot_prompt, prompts, slots):
    onehot = (slot_prompt[:, None] == jnp.arange(prompts, dtype=jnp.int32)[None, :]).astype(jnp.int32)
    running = jnp.cumsum(onehot, axis=0)
    global_rank = lax.optimization_barrier(jnp.sum(onehot * (running - 1), axis=1))
    local_count = jnp.cumsum(onehot.reshape(-1, slots, prompts), axis=1).reshape(-1, prompts)
    local_rank = lax.optimization_barrier(jnp.sum(onehot * (local_count - 1), axis=1))
    return (global_rank.astype(jnp.int32), local_rank.astype(jnp.int32))

def visible(query_pos, key_pos):
    distance = query_pos - key_pos
    return (distance >= 0) & ((distance < WINDOW) | (key_pos < SINKS))

def reference(tokens, attn_gain, mlp_gain, w_query, w_key, w_value, w_gate, w_up, w_out, w_down, cache, slot_prompt, prefix_len, new_len):
    per_group = HEADS // KV_HEADS
    score_scale = 1.0 / math.sqrt(HD)
    normed = rms_scale(tokens, attn_gain)
    new_ids = jnp.arange(NEW, dtype=jnp.int32)
    positions = (prefix_len[:, None] + new_ids[None, :]).reshape(-1)
    query_all = jnp.dot(normed, w_query.astype(jnp.bfloat16), preferred_element_type=jnp.float32)
    query_all = rotate(query_all.reshape(TOKENS, HEADS, HD), positions).astype(jnp.bfloat16)
    key_all = jnp.dot(normed, w_key.astype(jnp.bfloat16), preferred_element_type=jnp.float32)
    key_all = rotate(key_all.reshape(TOKENS, KV_HEADS, HD), positions).astype(jnp.bfloat16)
    value_all = jnp.dot(normed, w_value.astype(jnp.bfloat16), preferred_element_type=jnp.float32)
    value_all = value_all.astype(jnp.bfloat16).reshape(TOKENS, KV_HEADS, HD)
    global_rank, local_rank = slot_ranks(slot_prompt, PROMPTS, SLOTS)
    slot_ids = jnp.arange(PROMPTS * SLOTS, dtype=jnp.int32)
    matched = (slot_prompt[None, None, :] == jnp.arange(PROMPTS, dtype=jnp.int32)[:, None, None]) & (global_rank[None, None, :] == jnp.arange(PREFIX_BLOCKS, dtype=jnp.int32)[None, :, None])
    table = lax.optimization_barrier(jnp.sum(jnp.where(matched, slot_ids[None, None, :], 0), axis=2)).astype(jnp.int32)
    cached_span = PREFIX_BLOCKS * BLOCK
    cached_ids = jnp.arange(cached_span, dtype=jnp.int32)

    def one_prompt(prompt):
        first_row = prompt * NEW
        row_block = lax.dynamic_slice_in_dim(query_all, first_row, NEW, 0)
        own_keys = lax.dynamic_slice_in_dim(key_all, first_row, NEW, 0)
        own_values = lax.dynamic_slice_in_dim(value_all, first_row, NEW, 0)
        picked = jnp.take(cache, table[prompt], axis=1)
        picked = jnp.transpose(picked, (0, 1, 4, 2, 3)).reshape(2, cached_span, KV_HEADS, HD)
        all_keys = jnp.concatenate([picked[0], own_keys], axis=0)
        all_values = jnp.concatenate([picked[1], own_values], axis=0)
        before = prefix_len[prompt]
        key_pos = jnp.concatenate([cached_ids, before + new_ids])
        key_live = jnp.concatenate([cached_ids < before, new_ids < new_len[prompt]])
        query_pos = before + new_ids
        seen_mask = key_live[None, :] & visible(query_pos[:, None], key_pos[None, :])

        def one_head(head_index):
            kv_group = head_index // per_group
            queries = lax.dynamic_index_in_dim(row_block, head_index, 1, keepdims=False)
            keys_here = lax.dynamic_index_in_dim(all_keys, kv_group, 1, keepdims=False)
            values_here = lax.dynamic_index_in_dim(all_values, kv_group, 1, keepdims=False)
            scores = jnp.dot(queries, keys_here.T, preferred_element_type=jnp.float32) * score_scale
            masked = jnp.where(seen_mask, scores, FLOOR_SCORE)
            row_max = lax.optimization_barrier(jnp.max(masked, axis=1, keepdims=True))
            weights = jnp.where(seen_mask, jnp.exp(masked - row_max), 0.0)
            totals = lax.optimization_barrier(jnp.sum(weights, axis=1, keepdims=True))
            return jnp.dot(weights.astype(jnp.bfloat16), values_here, preferred_element_type=jnp.float32) / totals
        head_out = lax.map(one_head, jnp.arange(HEADS, dtype=jnp.int32))
        return jnp.transpose(head_out, (1, 0, 2)).reshape(NEW, HEADS * HD).astype(jnp.bfloat16)
    attended = lax.map(one_prompt, jnp.arange(PROMPTS, dtype=jnp.int32)).reshape(TOKENS, HEADS * HD)
    middle = (tokens.astype(jnp.float32) + jnp.dot(attended, w_out, preferred_element_type=jnp.float32)).astype(jnp.bfloat16)
    normed_mid = rms_scale(middle, mlp_gain)
    gate_proj = jnp.dot(normed_mid, w_gate.astype(jnp.bfloat16), preferred_element_type=jnp.float32)
    up_proj = jnp.dot(normed_mid, w_up.astype(jnp.bfloat16), preferred_element_type=jnp.float32)
    hidden = (jax.nn.silu(gate_proj) * up_proj).astype(jnp.bfloat16)
    mixed = middle.astype(jnp.float32) + jnp.dot(hidden, w_down, preferred_element_type=jnp.float32)
    row_live = (new_ids[None, :] < new_len[:, None]).reshape(-1)
    return jnp.where(row_live[:, None], mixed, 0.0).astype(jnp.bfloat16)
```

```python
import math

import jax
import jax.numpy as jnp
from jax import lax
from jax.sharding import PartitionSpec as P

HEADS = 32
KV_HEADS = 8
HD = 80
WINDOW = 4096
SINKS = 4
BLOCK = 128
CAP = 2


FLOOR_SCORE = -1e30
EPSILON = 1e-05
ROPE_BASE = 10000.0


def rms_scale(row_data, gain_vec):
    values = row_data.astype(jnp.float32)
    mean_square = jnp.mean(values * values, axis=-1, keepdims=True)
    return (values * lax.rsqrt(mean_square + EPSILON) * gain_vec).astype(jnp.bfloat16)


def rotate(values, positions):
    head_width = values.shape[-1]
    half_width = head_width // 2
    frequency = ROPE_BASE ** (-2.0 * jnp.arange(half_width, dtype=jnp.float32) / head_width)
    angles = positions.astype(jnp.float32)[:, None] * frequency[None, :]
    cosine = jnp.cos(angles)[:, None, :]
    sine_wave = jnp.sin(angles)[:, None, :]
    first_half = values[..., :half_width]
    second_half = values[..., half_width:]
    return jnp.concatenate(
        [
            first_half * cosine - second_half * sine_wave,
            second_half * cosine + first_half * sine_wave,
        ],
        axis=-1,
    )


def slot_ranks(slot_prompt, prompts, slots):
    onehot = (slot_prompt[:, None] == jnp.arange(prompts, dtype=jnp.int32)[None, :]).astype(
        jnp.int32
    )
    running = jnp.cumsum(onehot, axis=0)
    global_rank = jnp.sum(onehot * (running - 1), axis=1)
    local_count = jnp.cumsum(onehot.reshape(-1, slots, prompts), axis=1).reshape(-1, prompts)
    local_rank = jnp.sum(onehot * (local_count - 1), axis=1)
    return (global_rank, local_rank)


def visible(query_pos, key_pos):
    distance = query_pos - key_pos
    return (distance >= 0) & ((distance < WINDOW) | (key_pos < SINKS))


def partial_block(scores, seen_mask):
    masked = jnp.where(seen_mask, scores, FLOOR_SCORE)
    row_max = jnp.max(masked, axis=-1)
    weights = jnp.where(seen_mask, jnp.exp(masked - row_max[..., None]), 0.0)
    return (row_max, jnp.sum(weights, axis=-1), weights.astype(jnp.bfloat16))


def combine(first_part, second_part):
    maxima = jnp.maximum(first_part[0], second_part[0])
    scale_first = jnp.exp(first_part[0] - maxima)
    scale_second = jnp.exp(second_part[0] - maxima)
    totals = first_part[1] * scale_first + second_part[1] * scale_second
    outputs = first_part[2] * scale_first[..., None] + second_part[2] * scale_second[..., None]
    return (maxima, totals, outputs)


def pack_groups(matrices, groups):
    rows = matrices[0].shape[0]
    pieces = [
        jnp.transpose(
            matrix.astype(jnp.bfloat16).reshape(rows, groups, matrix.shape[1] // groups), (1, 0, 2)
        )
        for matrix in matrices
    ]
    return jnp.concatenate(pieces, axis=2)


def shards(
    tokens,
    attn_gain,
    mlp_gain,
    w_query,
    w_key,
    w_value,
    w_gate,
    w_up,
    w_out,
    w_down,
    cache,
    slot_prompt,
    prefix_len,
    new_len,
):
    groups = lax.axis_size("kv")
    n_blocks = lax.axis_size("blk")
    blk_index = lax.axis_index("blk")
    kv_index = lax.axis_index("kv")
    packed = pack_groups((w_query, w_key, w_value, w_gate, w_up), groups)
    attn_width = (w_query.shape[1] + w_key.shape[1] + w_value.shape[1]) // groups
    mine = lax.all_to_all(packed, "kv", split_axis=0, concat_axis=0, tiled=True)
    mine = mine.reshape(-1, mine.shape[-1])
    w_qkv = lax.all_gather(mine[:, :attn_width], "blk", axis=0, tiled=True)
    w_pair = lax.all_gather(mine[:, attn_width:], "blk", axis=0, tiled=True)
    query_width = w_query.shape[1] // groups
    key_width = w_key.shape[1] // groups
    kv_local = key_width // HD
    per_group = HEADS // KV_HEADS
    new_rows = tokens.shape[0]
    prompts = prefix_len.shape[0]
    slots = cache.shape[1]
    score_scale = 1.0 / math.sqrt(HD)
    prefix_here = prefix_len[blk_index]
    live_count = new_len[blk_index]
    row_ids = jnp.arange(new_rows, dtype=jnp.int32)
    positions = prefix_here + row_ids
    offsets = jnp.arange(BLOCK, dtype=jnp.int32)
    normed = rms_scale(tokens, attn_gain)
    projected = jnp.dot(normed, w_qkv, preferred_element_type=jnp.float32)
    queries = rotate(projected[:, :query_width].reshape(new_rows, -1, HD), positions).astype(
        jnp.bfloat16
    )
    key_new = rotate(
        projected[:, query_width : query_width + key_width].reshape(new_rows, kv_local, HD),
        positions,
    ).astype(jnp.bfloat16)
    value_new = (
        projected[:, query_width + key_width :].reshape(new_rows, kv_local, HD).astype(jnp.bfloat16)
    )
    grouped_q = queries.reshape(new_rows, kv_local, per_group, HD)
    own_scores = (
        jnp.einsum("qgnd,kgd->gnqk", grouped_q, key_new, preferred_element_type=jnp.float32)
        * score_scale
    )
    own_mask = (row_ids[None, :] < live_count) & visible(positions[:, None], positions[None, :])
    own_max, own_sum, own_weights = partial_block(own_scores, own_mask)
    own_out = jnp.einsum(
        "gnqk,kgd->gnqd", own_weights, value_new, preferred_element_type=jnp.float32
    )
    running = (own_max, own_sum, own_out)
    global_rank, local_rank = slot_ranks(slot_prompt, prompts, slots)
    own_prompts = lax.dynamic_slice_in_dim(slot_prompt, blk_index * slots, slots)
    own_ranks = lax.dynamic_slice_in_dim(local_rank, blk_index * slots, slots)
    placed = own_prompts * CAP + own_ranks
    buffer_ids = jnp.arange(prompts * CAP, dtype=jnp.int32)
    matches = placed[None, :] == buffer_ids[:, None]
    source_slot = jnp.sum(
        jnp.where(matches, jnp.arange(slots, dtype=jnp.int32)[None, :], 0), axis=1
    )
    filled = jnp.any(matches, axis=1)
    outgoing = jnp.where(
        filled[None, :, None, None, None],
        jnp.take(cache, source_slot, axis=1),
        jnp.zeros((), cache.dtype),
    )
    arrived = lax.all_to_all(outgoing, "blk", split_axis=1, concat_axis=1, tiled=True)
    slot_ids = jnp.arange(prompts * slots, dtype=jnp.int32)
    landing = slot_ids // slots * CAP + local_rank
    for_me = slot_prompt == blk_index
    received = (landing[None, :] == buffer_ids[:, None]) & for_me[None, :]
    block_number = jnp.sum(jnp.where(received, global_rank[None, :], 0), axis=1)
    block_live = jnp.any(received, axis=1)
    total_slots = prompts * CAP
    group_slots = min(total_slots, max(1, 512 // BLOCK))
    step_count = total_slots // group_slots
    key_blocks = arrived[0].reshape(step_count, group_slots, kv_local, HD, BLOCK)
    value_blocks = arrived[1].reshape(step_count, group_slots, kv_local, HD, BLOCK)
    numbers = block_number.reshape(step_count, group_slots)
    live_flags = block_live.reshape(step_count, group_slots)

    def prefix_step(running_state, inputs):
        key_part, value_part, number_part, flag_part = inputs
        scores = (
            jnp.einsum("qgnd,sgdt->gnqst", grouped_q, key_part, preferred_element_type=jnp.float32)
            * score_scale
        )
        scores = scores.reshape(kv_local, per_group, new_rows, group_slots * BLOCK)
        key_pos = number_part[:, None] * BLOCK + offsets[None, :]
        key_live = (flag_part[:, None] & (key_pos < prefix_here)).reshape(-1)
        seen_mask = key_live[None, :] & visible(positions[:, None], key_pos.reshape(-1)[None, :])
        block_max, block_sum, weights = partial_block(scores, seen_mask)
        weights = weights.reshape(kv_local, per_group, new_rows, group_slots, BLOCK)
        block_out = jnp.einsum(
            "gnqst,sgdt->gnqd", weights, value_part, preferred_element_type=jnp.float32
        )
        return (combine(running_state, (block_max, block_sum, block_out)), None)

    running = lax.scan(prefix_step, running, (key_blocks, value_blocks, numbers, live_flags))[0]
    totals = running[1]
    outputs = running[2]
    attended = (
        jnp.transpose(outputs / totals[..., None], (2, 0, 1, 3))
        .reshape(new_rows, -1)
        .astype(jnp.bfloat16)
    )
    projected_out = jnp.dot(attended, w_out, preferred_element_type=jnp.float32)
    partial_out, w_pair = lax.optimization_barrier((projected_out.astype(jnp.bfloat16), w_pair))
    summed = lax.psum(partial_out, "kv").astype(jnp.float32)
    middle = (tokens.astype(jnp.float32) + summed).astype(jnp.bfloat16)
    normed_mid = rms_scale(middle, mlp_gain)
    paired = jnp.dot(normed_mid, w_pair, preferred_element_type=jnp.float32)
    hidden_width = w_pair.shape[1] // 2
    hidden = (jax.nn.silu(paired[:, :hidden_width]) * paired[:, hidden_width:]).astype(jnp.bfloat16)
    down_part = jnp.dot(hidden, w_down, preferred_element_type=jnp.float32)
    reduced = lax.psum_scatter(
        down_part.astype(jnp.bfloat16), "kv", scatter_dimension=1, tiled=True
    ).astype(jnp.float32)
    out_width = reduced.shape[1]
    residual = lax.dynamic_slice_in_dim(middle, kv_index * out_width, out_width, 1).astype(
        jnp.float32
    )
    mixed = jnp.where((row_ids < live_count)[:, None], residual + reduced, 0.0)
    return mixed.astype(jnp.bfloat16)


def solution(mesh):
    return jax.shard_map(
        shards,
        mesh=mesh,
        in_specs=(
            P("blk", None),
            P(),
            P(),
            P(("blk", "kv"), None),
            P(("blk", "kv"), None),
            P(("blk", "kv"), None),
            P(("blk", "kv"), None),
            P(("blk", "kv"), None),
            P("kv", None),
            P("kv", None),
            P(None, "blk", "kv", None, None),
            P(),
            P(),
            P(),
        ),
        out_specs=P("blk", "kv"),
        check_vma=False,
    )
```

```python
import functools
import math

import jax
import jax.numpy as jnp
from jax import lax
from jax.experimental import pallas as pl
from jax.experimental.pallas import tpu as pltpu
from jax.sharding import PartitionSpec as P

HEADS = 32
KV_HEADS = 8
HD = 80
WINDOW = 4096
SINKS = 4
BLOCK = 128
CAP = 2


FLOOR_SCORE = -1e30
EPSILON = 1e-05
ROPE_BASE = 10000.0


def rms_scale(row_data, gain_vec):
    values = row_data.astype(jnp.float32)
    mean_square = jnp.mean(values * values, axis=-1, keepdims=True)
    return (values * lax.rsqrt(mean_square + EPSILON) * gain_vec).astype(jnp.bfloat16)


def rotate(values, positions):
    head_width = values.shape[-1]
    half_width = head_width // 2
    frequency = ROPE_BASE ** (-2.0 * jnp.arange(half_width, dtype=jnp.float32) / head_width)
    angles = positions.astype(jnp.float32)[:, None] * frequency[None, :]
    cosine = jnp.cos(angles)[:, None, :]
    sine_wave = jnp.sin(angles)[:, None, :]
    first_half = values[..., :half_width]
    second_half = values[..., half_width:]
    return jnp.concatenate(
        [
            first_half * cosine - second_half * sine_wave,
            second_half * cosine + first_half * sine_wave,
        ],
        axis=-1,
    )


def slot_ranks(slot_prompt, prompts, slots):
    onehot = (slot_prompt[:, None] == jnp.arange(prompts, dtype=jnp.int32)[None, :]).astype(
        jnp.int32
    )
    running = jnp.cumsum(onehot, axis=0)
    global_rank = jnp.sum(onehot * (running - 1), axis=1)
    local_count = jnp.cumsum(onehot.reshape(-1, slots, prompts), axis=1).reshape(-1, prompts)
    local_rank = jnp.sum(onehot * (local_count - 1), axis=1)
    return (global_rank, local_rank)


def visible(query_pos, key_pos):
    distance = query_pos - key_pos
    return (distance >= 0) & ((distance < WINDOW) | (key_pos < SINKS))


def partial_block(scores, seen_mask):
    masked = jnp.where(seen_mask, scores, FLOOR_SCORE)
    row_max = jnp.max(masked, axis=-1)
    weights = jnp.where(seen_mask, jnp.exp(masked - row_max[..., None]), 0.0)
    return (row_max, jnp.sum(weights, axis=-1), weights.astype(jnp.bfloat16))


def combine(first_part, second_part):
    maxima = jnp.maximum(first_part[0], second_part[0])
    scale_first = jnp.exp(first_part[0] - maxima)
    scale_second = jnp.exp(second_part[0] - maxima)
    totals = first_part[1] * scale_first + second_part[1] * scale_second
    outputs = first_part[2] * scale_first[..., None] + second_part[2] * scale_second[..., None]
    return (maxima, totals, outputs)


def pack_groups(matrices, groups):
    rows = matrices[0].shape[0]
    pieces = [
        jnp.transpose(
            matrix.astype(jnp.bfloat16).reshape(rows, groups, matrix.shape[1] // groups), (1, 0, 2)
        )
        for matrix in matrices
    ]
    return jnp.concatenate(pieces, axis=2)


MESH = pl.DeviceIdType.MESH
VMEM_SPEC = pl.BlockSpec(memory_space=pltpu.VMEM)


def greet(n, me):
    barrier = pltpu.get_barrier_semaphore()
    for step in range(1, n):
        peer = lax.rem(me + step, n)
        pl.semaphore_signal(barrier, inc=1, device_id={"kv": peer}, device_id_type=MESH)
    pl.semaphore_wait(barrier, n - 1)


def exchange(n, me, piece_ref, landed, send_sem, recv_sem):
    copies = []
    for step in range(1, n):
        peer = lax.rem(me + step, n)
        copy = pltpu.make_async_remote_copy(
            src_ref=piece_ref.at[peer],
            dst_ref=landed.at[step - 1],
            send_sem=send_sem.at[step - 1],
            recv_sem=recv_sem.at[step - 1],
            device_id={"kv": peer},
            device_id_type=MESH,
        )
        copy.start()
        copies.append(copy)
    return copies


def middle_kernel(
    n, piece_ref, token_ref, gain_ref, middle_ref, normed_ref, landed, total, whole,
    send_sem, recv_sem, share_sem, join_sem,
):
    me = lax.axis_index("kv")
    rows = piece_ref.shape[1]
    greet(n, me)
    copies = exchange(n, me, piece_ref, landed, send_sem, recv_sem)
    own = pl.ds(pl.multiple_of(me * rows, rows), rows)
    total[...] = token_ref[own, :].astype(jnp.float32) + piece_ref[me].astype(jnp.float32)
    for step in range(1, n):
        copies[step - 1].wait_recv()
        total[...] += landed[step - 1].astype(jnp.float32)
    whole[0] = total[...].astype(jnp.bfloat16)
    shares = []
    for step in range(1, n):
        peer = lax.rem(me + step, n)
        share = pltpu.make_async_remote_copy(
            src_ref=whole.at[0],
            dst_ref=whole.at[step],
            send_sem=share_sem.at[step - 1],
            recv_sem=join_sem.at[step - 1],
            device_id={"kv": peer},
            device_id_type=MESH,
        )
        share.start()
        shares.append(share)
    for step in range(n):
        if step:
            shares[step - 1].wait_recv()
        owner = lax.rem(me + n - step, n)
        place = pl.ds(pl.multiple_of(owner * rows, rows), rows)
        middle_rows = whole[step]
        middle_ref[place, :] = middle_rows
        values = middle_rows.astype(jnp.float32)
        mean_square = jnp.mean(values * values, axis=-1, keepdims=True)
        normed_ref[place, :] = (
            values * lax.rsqrt(mean_square + EPSILON) * gain_ref[...]
        ).astype(jnp.bfloat16)
    for copy in copies + shares:
        copy.wait_send()


def sum_middle(n, partial_out, tokens, mlp_gain):
    rows, width = tokens.shape
    piece = rows // n
    whole_shape = jax.ShapeDtypeStruct((rows, width), jnp.bfloat16)
    return pl.pallas_call(
        functools.partial(middle_kernel, n),
        name="sum_middle",
        out_shape=(whole_shape, whole_shape),
        in_specs=[VMEM_SPEC] * 3,
        out_specs=(VMEM_SPEC, VMEM_SPEC),
        scratch_shapes=[
            pltpu.VMEM((n - 1, piece, width), jnp.bfloat16),
            pltpu.VMEM((piece, width), jnp.float32),
            pltpu.VMEM((n, piece, width), jnp.bfloat16),
        ]
        + [pltpu.SemaphoreType.DMA((n - 1,))] * 4,
        compiler_params=pltpu.CompilerParams(collective_id=0, has_side_effects=True),
    )(partial_out.reshape(n, piece, width), tokens, mlp_gain.reshape(1, width))


def scatter_kernel(n, piece_ref, out_ref, landed, send_sem, recv_sem):
    me = lax.axis_index("kv")
    greet(n, me)
    copies = exchange(n, me, piece_ref, landed, send_sem, recv_sem)
    out_ref[...] = piece_ref[me].astype(jnp.float32)
    for step in range(1, n):
        copies[step - 1].wait_recv()
        out_ref[...] += landed[step - 1].astype(jnp.float32)
    for copy in copies:
        copy.wait_send()


def sum_scatter(n, pieces):
    shape = pieces.shape[1:]
    return pl.pallas_call(
        functools.partial(scatter_kernel, n),
        name="sum_scatter",
        out_shape=jax.ShapeDtypeStruct(shape, jnp.float32),
        in_specs=[VMEM_SPEC],
        out_specs=VMEM_SPEC,
        scratch_shapes=[pltpu.VMEM((n - 1,) + shape, jnp.bfloat16)]
        + [pltpu.SemaphoreType.DMA((n - 1,))] * 2,
        compiler_params=pltpu.CompilerParams(collective_id=1, has_side_effects=True),
    )(pieces)


def shards(
    tokens,
    attn_gain,
    mlp_gain,
    w_query,
    w_key,
    w_value,
    w_gate,
    w_up,
    w_out,
    w_down,
    cache,
    slot_prompt,
    prefix_len,
    new_len,
):
    groups = lax.axis_size("kv")
    n_blocks = lax.axis_size("blk")
    blk_index = lax.axis_index("blk")
    kv_index = lax.axis_index("kv")
    packed = pack_groups((w_query, w_key, w_value, w_gate, w_up), groups)
    attn_width = (w_query.shape[1] + w_key.shape[1] + w_value.shape[1]) // groups
    mine = lax.all_to_all(packed, "kv", split_axis=0, concat_axis=0, tiled=True)
    mine = mine.reshape(-1, mine.shape[-1])
    w_qkv = lax.all_gather(mine[:, :attn_width], "blk", axis=0, tiled=True)
    w_pair = lax.all_gather(mine[:, attn_width:], "blk", axis=0, tiled=True)
    query_width = w_query.shape[1] // groups
    key_width = w_key.shape[1] // groups
    kv_local = key_width // HD
    per_group = HEADS // KV_HEADS
    new_rows = tokens.shape[0]
    prompts = prefix_len.shape[0]
    slots = cache.shape[1]
    score_scale = 1.0 / math.sqrt(HD)
    prefix_here = prefix_len[blk_index]
    live_count = new_len[blk_index]
    row_ids = jnp.arange(new_rows, dtype=jnp.int32)
    positions = prefix_here + row_ids
    offsets = jnp.arange(BLOCK, dtype=jnp.int32)
    normed = rms_scale(tokens, attn_gain)
    projected = jnp.dot(normed, w_qkv, preferred_element_type=jnp.float32)
    queries = rotate(projected[:, :query_width].reshape(new_rows, -1, HD), positions).astype(
        jnp.bfloat16
    )
    key_new = rotate(
        projected[:, query_width : query_width + key_width].reshape(new_rows, kv_local, HD),
        positions,
    ).astype(jnp.bfloat16)
    value_new = (
        projected[:, query_width + key_width :].reshape(new_rows, kv_local, HD).astype(jnp.bfloat16)
    )
    grouped_q = queries.reshape(new_rows, kv_local, per_group, HD)
    own_scores = (
        jnp.einsum("qgnd,kgd->gnqk", grouped_q, key_new, preferred_element_type=jnp.float32)
        * score_scale
    )
    own_mask = (row_ids[None, :] < live_count) & visible(positions[:, None], positions[None, :])
    own_max, own_sum, own_weights = partial_block(own_scores, own_mask)
    own_out = jnp.einsum(
        "gnqk,kgd->gnqd", own_weights, value_new, preferred_element_type=jnp.float32
    )
    running = (own_max, own_sum, own_out)
    global_rank, local_rank = slot_ranks(slot_prompt, prompts, slots)
    own_prompts = lax.dynamic_slice_in_dim(slot_prompt, blk_index * slots, slots)
    own_ranks = lax.dynamic_slice_in_dim(local_rank, blk_index * slots, slots)
    placed = own_prompts * CAP + own_ranks
    buffer_ids = jnp.arange(prompts * CAP, dtype=jnp.int32)
    matches = placed[None, :] == buffer_ids[:, None]
    source_slot = jnp.sum(
        jnp.where(matches, jnp.arange(slots, dtype=jnp.int32)[None, :], 0), axis=1
    )
    filled = jnp.any(matches, axis=1)
    outgoing = jnp.where(
        filled[None, :, None, None, None],
        jnp.take(cache, source_slot, axis=1),
        jnp.zeros((), cache.dtype),
    )
    arrived = lax.all_to_all(outgoing, "blk", split_axis=1, concat_axis=1, tiled=True)
    slot_ids = jnp.arange(prompts * slots, dtype=jnp.int32)
    landing = slot_ids // slots * CAP + local_rank
    for_me = slot_prompt == blk_index
    received = (landing[None, :] == buffer_ids[:, None]) & for_me[None, :]
    block_number = jnp.sum(jnp.where(received, global_rank[None, :], 0), axis=1)
    block_live = jnp.any(received, axis=1)
    total_slots = prompts * CAP
    group_slots = min(total_slots, max(1, 512 // BLOCK))
    step_count = total_slots // group_slots
    key_blocks = arrived[0].reshape(step_count, group_slots, kv_local, HD, BLOCK)
    value_blocks = arrived[1].reshape(step_count, group_slots, kv_local, HD, BLOCK)
    numbers = block_number.reshape(step_count, group_slots)
    live_flags = block_live.reshape(step_count, group_slots)

    def prefix_step(running_state, inputs):
        key_part, value_part, number_part, flag_part = inputs
        scores = (
            jnp.einsum("qgnd,sgdt->gnqst", grouped_q, key_part, preferred_element_type=jnp.float32)
            * score_scale
        )
        scores = scores.reshape(kv_local, per_group, new_rows, group_slots * BLOCK)
        key_pos = number_part[:, None] * BLOCK + offsets[None, :]
        key_live = (flag_part[:, None] & (key_pos < prefix_here)).reshape(-1)
        seen_mask = key_live[None, :] & visible(positions[:, None], key_pos.reshape(-1)[None, :])
        block_max, block_sum, weights = partial_block(scores, seen_mask)
        weights = weights.reshape(kv_local, per_group, new_rows, group_slots, BLOCK)
        block_out = jnp.einsum(
            "gnqst,sgdt->gnqd", weights, value_part, preferred_element_type=jnp.float32
        )
        return (combine(running_state, (block_max, block_sum, block_out)), None)

    running = lax.scan(prefix_step, running, (key_blocks, value_blocks, numbers, live_flags))[0]
    totals = running[1]
    outputs = running[2]
    attended = (
        jnp.transpose(outputs / totals[..., None], (2, 0, 1, 3))
        .reshape(new_rows, -1)
        .astype(jnp.bfloat16)
    )
    projected_out = jnp.dot(attended, w_out, preferred_element_type=jnp.float32)
    partial_out, w_pair = lax.optimization_barrier((projected_out.astype(jnp.bfloat16), w_pair))
    middle, normed_mid = sum_middle(groups, partial_out, tokens, mlp_gain)
    paired = jnp.dot(normed_mid, w_pair, preferred_element_type=jnp.float32)
    hidden_width = w_pair.shape[1] // 2
    hidden = (jax.nn.silu(paired[:, :hidden_width]) * paired[:, hidden_width:]).astype(jnp.bfloat16)
    down_part = lax.dot_general(
        w_down, hidden, (((0,), (1,)), ((), ())), preferred_element_type=jnp.float32
    ).astype(jnp.bfloat16)
    reduced = sum_scatter(groups, down_part.reshape(groups, -1, new_rows)).T
    out_width = reduced.shape[1]
    residual = lax.dynamic_slice_in_dim(middle, kv_index * out_width, out_width, 1).astype(
        jnp.float32
    )
    mixed = jnp.where((row_ids < live_count)[:, None], residual + reduced, 0.0)
    return mixed.astype(jnp.bfloat16)


def solution(mesh):
    return jax.shard_map(
        shards,
        mesh=mesh,
        in_specs=(
            P("blk", None),
            P(),
            P(),
            P(("blk", "kv"), None),
            P(("blk", "kv"), None),
            P(("blk", "kv"), None),
            P(("blk", "kv"), None),
            P(("blk", "kv"), None),
            P("kv", None),
            P("kv", None),
            P(None, "blk", "kv", None, None),
            P(),
            P(),
            P(),
        ),
        out_specs=P("blk", "kv"),
        check_vma=False,
    )
```

```python
import functools
import math

import jax
import jax.numpy as jnp
from jax import lax
from jax.experimental import pallas as pl
from jax.experimental.pallas import tpu as pltpu
from jax.sharding import PartitionSpec as P

HEADS = 32
KV_HEADS = 8
HD = 80
WINDOW = 4096
SINKS = 4
BLOCK = 128
CAP = 2


FLOOR_SCORE = -1e30
EPSILON = 1e-05
ROPE_BASE = 10000.0


def rms_scale(row_data, gain_vec):
    values = row_data.astype(jnp.float32)
    mean_square = jnp.mean(values * values, axis=-1, keepdims=True)
    return (values * lax.rsqrt(mean_square + EPSILON) * gain_vec).astype(jnp.bfloat16)


def rotate(values, positions):
    head_width = values.shape[-1]
    half_width = head_width // 2
    frequency = ROPE_BASE ** (-2.0 * jnp.arange(half_width, dtype=jnp.float32) / head_width)
    angles = positions.astype(jnp.float32)[:, None] * frequency[None, :]
    cosine = jnp.cos(angles)[:, None, :]
    sine_wave = jnp.sin(angles)[:, None, :]
    first_half = values[..., :half_width]
    second_half = values[..., half_width:]
    return jnp.concatenate(
        [
            first_half * cosine - second_half * sine_wave,
            second_half * cosine + first_half * sine_wave,
        ],
        axis=-1,
    )


def slot_ranks(slot_prompt, prompts, slots):
    onehot = (slot_prompt[:, None] == jnp.arange(prompts, dtype=jnp.int32)[None, :]).astype(
        jnp.int32
    )
    running = jnp.cumsum(onehot, axis=0)
    global_rank = jnp.sum(onehot * (running - 1), axis=1)
    local_count = jnp.cumsum(onehot.reshape(-1, slots, prompts), axis=1).reshape(-1, prompts)
    local_rank = jnp.sum(onehot * (local_count - 1), axis=1)
    return (global_rank, local_rank)


def pack_groups(matrices, groups):
    rows = matrices[0].shape[0]
    pieces = [
        jnp.transpose(
            matrix.astype(jnp.bfloat16).reshape(rows, groups, matrix.shape[1] // groups), (1, 0, 2)
        )
        for matrix in matrices
    ]
    return jnp.concatenate(pieces, axis=2)


MESH = pl.DeviceIdType.MESH
VMEM_SPEC = pl.BlockSpec(memory_space=pltpu.VMEM)


LIFT = 1.0 / math.sqrt(HD) * math.log2(math.e)


def attention_kernel(
    scalars, query_ref, own_key_ref, own_value_ref, blocks_ref, out_ref,
    keys, values, score_a, score_b, row_max, summed,
):
    slots, block = blocks_ref.shape[0], blocks_ref.shape[3]
    rows = query_ref.shape[2]
    depth = keys.shape[1]
    wide = values.shape[0]
    chunk = rows
    per_chunk = chunk // block
    chunks = slots // per_chunk
    before, live_rows = scalars[2 * slots], scalars[2 * slots + 1]

    def padded_key(part, limit):
        spots = lax.broadcasted_iota(jnp.int32, (depth - HD, block), 1)
        lines = lax.broadcasted_iota(jnp.int32, (depth - HD, block), 0)
        bias = jnp.where((lines == 0) & (spots >= limit), FLOOR_SCORE, 0.0)
        return jnp.concatenate([part.astype(jnp.float32), bias], axis=0).T.astype(jnp.bfloat16)

    @pl.when(pl.program_id(0) == 0)
    def _():
        ones = jnp.ones((wide - HD, block), jnp.bfloat16)

        def place(slot, carry):
            limit = jnp.where(
                scalars[slots + slot] > 0, before - scalars[slot] * block, 0
            )
            spot = pl.multiple_of(slot * block, block)
            keys[pl.ds(spot, block), :] = padded_key(blocks_ref[slot, 0], limit)
            values[:, pl.ds(spot, block)] = jnp.concatenate([blocks_ref[slot, 1], ones], axis=0)
            return carry

        lax.fori_loop(0, slots, place, 0)
        for part in range(rows // block):
            near = slice(part * block, (part + 1) * block)
            far = slice(slots * block + part * block, slots * block + (part + 1) * block)
            keys[far, :] = padded_key(own_key_ref[:, near], live_rows - part * block)
            values[:, far] = jnp.concatenate([own_value_ref[:, near], ones], axis=0)

    query = jnp.concatenate(
        [
            query_ref[0].astype(jnp.float32),
            jnp.ones((16, rows), jnp.float32),
            jnp.zeros((depth - HD - 16, rows), jnp.float32),
        ],
        axis=0,
    ).astype(jnp.bfloat16)

    def score(index, into):
        spot = pl.multiple_of(index * chunk, chunk)
        into[...] = jnp.dot(keys[pl.ds(spot, chunk), :], query, preferred_element_type=jnp.float32)

    def window(index, into):
        near = before + rows - WINDOW
        needed = False
        for part in range(per_chunk):
            needed |= scalars[index * per_chunk + part] * block < near

        @pl.when(needed)
        def _():
            for part in range(per_chunk):
                lines = slice(part * block, (part + 1) * block)
                place = scalars[index * per_chunk + part] * block + lax.broadcasted_iota(
                    jnp.int32, (block, rows), 0
                )
                away = before - place + lax.broadcasted_iota(jnp.int32, (block, rows), 1)
                seen = (away < WINDOW) | (place < SINKS)
                into[lines, :] = jnp.where(seen, into[lines, :], FLOOR_SCORE)

    def absorb(index, held):
        spot = pl.multiple_of(index * chunk, chunk)
        now = held[...]
        largest = jnp.maximum(row_max[...], jnp.max(now, axis=0, keepdims=True))
        fade = jnp.exp2((row_max[...] - largest) * LIFT)
        weights = jnp.exp2((now - largest) * LIFT).astype(jnp.bfloat16)
        row_max[...] = largest
        summed[...] = summed[...] * fade + jnp.dot(
            values[:, pl.ds(spot, chunk)], weights, preferred_element_type=jnp.float32
        )

    score(chunks, score_b)
    causal = lax.broadcasted_iota(jnp.int32, (rows, rows), 0) <= lax.broadcasted_iota(
        jnp.int32, (rows, rows), 1
    )
    score_b[...] = jnp.where(causal, score_b[...], FLOOR_SCORE)
    row_max[...] = jnp.full_like(row_max, FLOOR_SCORE)
    summed[...] = jnp.zeros_like(summed)
    score(0, score_a)
    absorb(chunks, score_b)
    window(0, score_a)

    def pair(step, carry):
        first = step * 2
        score(first + 1, score_b)
        absorb(first, score_a)
        window(first + 1, score_b)
        later = lax.rem(first + 2, chunks)
        score(later, score_a)
        absorb(first + 1, score_b)
        window(later, score_a)
        return carry

    lax.fori_loop(0, chunks // 2, pair, 0)
    out_ref[0] = (summed[:HD, :] / summed[HD : HD + 1, :]).astype(jnp.bfloat16)


def attend(scalars, query, own_key, own_value, blocks):
    heads, width, rows = query.shape
    slots, block = blocks.shape[0], blocks.shape[3]
    span = slots * block + rows
    whole = pl.BlockSpec(memory_space=pltpu.VMEM)
    return pl.pallas_call(
        attention_kernel,
        name="attend",
        grid=(heads,),
        out_shape=jax.ShapeDtypeStruct((heads, width, rows), jnp.bfloat16),
        in_specs=[
            pl.BlockSpec(memory_space=pltpu.SMEM),
            pl.BlockSpec((1, width, rows), lambda head: (head, 0, 0)),
            whole,
            whole,
            whole,
        ],
        out_specs=pl.BlockSpec((1, width, rows), lambda head: (head, 0, 0)),
        scratch_shapes=[
            pltpu.VMEM((span, 128), jnp.bfloat16),
            pltpu.VMEM((96, span), jnp.bfloat16),
            pltpu.VMEM((rows, rows), jnp.float32),
            pltpu.VMEM((rows, rows), jnp.float32),
            pltpu.VMEM((1, rows), jnp.float32),
            pltpu.VMEM((96, rows), jnp.float32),
        ],
        cost_estimate=pl.CostEstimate(
            flops=4 * heads * rows * span * 128,
            bytes_accessed=span * 4 * width,
            transcendentals=heads * rows * span,
        ),
    )(scalars, query, own_key, own_value, blocks)


def greet(n, me):
    barrier = pltpu.get_barrier_semaphore()
    for step in range(1, n):
        peer = lax.rem(me + step, n)
        pl.semaphore_signal(barrier, inc=1, device_id={"kv": peer}, device_id_type=MESH)
    pl.semaphore_wait(barrier, n - 1)


def exchange(n, me, piece_ref, landed, send_sem, recv_sem):
    copies = []
    for step in range(1, n):
        peer = lax.rem(me + step, n)
        copy = pltpu.make_async_remote_copy(
            src_ref=piece_ref.at[peer],
            dst_ref=landed.at[step - 1],
            send_sem=send_sem.at[step - 1],
            recv_sem=recv_sem.at[step - 1],
            device_id={"kv": peer},
            device_id_type=MESH,
        )
        copy.start()
        copies.append(copy)
    return copies


def middle_kernel(
    n, piece_ref, token_ref, gain_ref, middle_ref, normed_ref, landed, total, whole,
    send_sem, recv_sem, share_sem, join_sem,
):
    me = lax.axis_index("kv")
    rows = piece_ref.shape[1]
    greet(n, me)
    copies = exchange(n, me, piece_ref, landed, send_sem, recv_sem)
    own = pl.ds(pl.multiple_of(me * rows, rows), rows)
    total[...] = token_ref[own, :].astype(jnp.float32) + piece_ref[me].astype(jnp.float32)
    for step in range(1, n):
        copies[step - 1].wait_recv()
        total[...] += landed[step - 1].astype(jnp.float32)
    whole[0] = total[...].astype(jnp.bfloat16)
    shares = []
    for step in range(1, n):
        peer = lax.rem(me + step, n)
        share = pltpu.make_async_remote_copy(
            src_ref=whole.at[0],
            dst_ref=whole.at[step],
            send_sem=share_sem.at[step - 1],
            recv_sem=join_sem.at[step - 1],
            device_id={"kv": peer},
            device_id_type=MESH,
        )
        share.start()
        shares.append(share)
    for step in range(n):
        if step:
            shares[step - 1].wait_recv()
        owner = lax.rem(me + n - step, n)
        place = pl.ds(pl.multiple_of(owner * rows, rows), rows)
        middle_rows = whole[step]
        middle_ref[place, :] = middle_rows
        values = middle_rows.astype(jnp.float32)
        mean_square = jnp.mean(values * values, axis=-1, keepdims=True)
        normed_ref[place, :] = (
            values * lax.rsqrt(mean_square + EPSILON) * gain_ref[...]
        ).astype(jnp.bfloat16)
    for copy in copies + shares:
        copy.wait_send()


def sum_middle(n, partial_out, tokens, mlp_gain):
    rows, width = tokens.shape
    piece = rows // n
    whole_shape = jax.ShapeDtypeStruct((rows, width), jnp.bfloat16)
    return pl.pallas_call(
        functools.partial(middle_kernel, n),
        name="sum_middle",
        cost_estimate=pl.CostEstimate(flops=0, bytes_accessed=200_000_000, transcendentals=0),
        out_shape=(whole_shape, whole_shape),
        in_specs=[VMEM_SPEC] * 3,
        out_specs=(VMEM_SPEC, VMEM_SPEC),
        scratch_shapes=[
            pltpu.VMEM((n - 1, piece, width), jnp.bfloat16),
            pltpu.VMEM((piece, width), jnp.float32),
            pltpu.VMEM((n, piece, width), jnp.bfloat16),
        ]
        + [pltpu.SemaphoreType.DMA((n - 1,))] * 4,
        compiler_params=pltpu.CompilerParams(collective_id=0, has_side_effects=True),
    )(partial_out.reshape(n, piece, width), tokens, mlp_gain.reshape(1, width))


def scatter_kernel(n, piece_ref, out_ref, landed, send_sem, recv_sem):
    me = lax.axis_index("kv")
    greet(n, me)
    copies = exchange(n, me, piece_ref, landed, send_sem, recv_sem)
    out_ref[...] = piece_ref[me].astype(jnp.float32)
    for step in range(1, n):
        copies[step - 1].wait_recv()
        out_ref[...] += landed[step - 1].astype(jnp.float32)
    for copy in copies:
        copy.wait_send()


def sum_scatter(n, pieces):
    shape = pieces.shape[1:]
    return pl.pallas_call(
        functools.partial(scatter_kernel, n),
        name="sum_scatter",
        out_shape=jax.ShapeDtypeStruct(shape, jnp.float32),
        in_specs=[VMEM_SPEC],
        out_specs=VMEM_SPEC,
        scratch_shapes=[pltpu.VMEM((n - 1,) + shape, jnp.bfloat16)]
        + [pltpu.SemaphoreType.DMA((n - 1,))] * 2,
        compiler_params=pltpu.CompilerParams(collective_id=1, has_side_effects=True),
    )(pieces)


def shards(
    tokens,
    attn_gain,
    mlp_gain,
    w_query,
    w_key,
    w_value,
    w_gate,
    w_up,
    w_out,
    w_down,
    cache,
    slot_prompt,
    prefix_len,
    new_len,
):
    groups = lax.axis_size("kv")
    n_blocks = lax.axis_size("blk")
    blk_index = lax.axis_index("blk")
    kv_index = lax.axis_index("kv")
    packed = pack_groups((w_query, w_key, w_value, w_gate, w_up), groups)
    attn_width = (w_query.shape[1] + w_key.shape[1] + w_value.shape[1]) // groups
    mine = lax.all_to_all(packed, "kv", split_axis=0, concat_axis=0, tiled=True)
    mine = mine.reshape(-1, mine.shape[-1])
    w_qkv = lax.all_gather(mine[:, :attn_width], "blk", axis=0, tiled=True)
    w_pair = lax.all_gather(mine[:, attn_width:], "blk", axis=0, tiled=True)
    query_width = w_query.shape[1] // groups
    key_width = w_key.shape[1] // groups
    kv_local = key_width // HD
    new_rows = tokens.shape[0]
    prompts = prefix_len.shape[0]
    slots = cache.shape[1]
    prefix_here = prefix_len[blk_index]
    live_count = new_len[blk_index]
    row_ids = jnp.arange(new_rows, dtype=jnp.int32)
    positions = prefix_here + row_ids
    normed = rms_scale(tokens, attn_gain)
    projected = jnp.dot(normed, w_qkv, preferred_element_type=jnp.float32)
    queries = rotate(projected[:, :query_width].reshape(new_rows, -1, HD), positions).astype(
        jnp.bfloat16
    )
    key_new = rotate(
        projected[:, query_width : query_width + key_width].reshape(new_rows, kv_local, HD),
        positions,
    ).astype(jnp.bfloat16)
    value_new = (
        projected[:, query_width + key_width :].reshape(new_rows, kv_local, HD).astype(jnp.bfloat16)
    )
    global_rank, local_rank = slot_ranks(slot_prompt, prompts, slots)
    own_prompts = lax.dynamic_slice_in_dim(slot_prompt, blk_index * slots, slots)
    own_ranks = lax.dynamic_slice_in_dim(local_rank, blk_index * slots, slots)
    placed = own_prompts * CAP + own_ranks
    buffer_ids = jnp.arange(prompts * CAP, dtype=jnp.int32)
    matches = placed[None, :] == buffer_ids[:, None]
    source_slot = jnp.sum(
        jnp.where(matches, jnp.arange(slots, dtype=jnp.int32)[None, :], 0), axis=1
    )
    filled = jnp.any(matches, axis=1)
    outgoing = jnp.where(
        filled[None, :, None, None, None],
        jnp.take(cache, source_slot, axis=1),
        jnp.zeros((), cache.dtype),
    )
    arrived = lax.all_to_all(outgoing, "blk", split_axis=1, concat_axis=1, tiled=True)
    slot_ids = jnp.arange(prompts * slots, dtype=jnp.int32)
    landing = slot_ids // slots * CAP + local_rank
    for_me = slot_prompt == blk_index
    received = (landing[None, :] == buffer_ids[:, None]) & for_me[None, :]
    block_number = jnp.sum(jnp.where(received, global_rank[None, :], 0), axis=1)
    block_live = jnp.any(received, axis=1)
    blocks = jnp.transpose(arrived, (1, 2, 0, 3, 4)).reshape(prompts * CAP, 2, HD, BLOCK)
    scalars = jnp.concatenate(
        [block_number, block_live.astype(jnp.int32), jnp.stack([prefix_here, live_count])]
    )
    attended = attend(
        scalars,
        jnp.transpose(queries, (1, 2, 0)),
        key_new.reshape(new_rows, HD).T,
        value_new.reshape(new_rows, HD).T,
        blocks,
    ).reshape(-1, new_rows)
    projected_out = lax.dot_general(
        attended, w_out, (((0,), (0,)), ((), ())), preferred_element_type=jnp.float32
    )
    partial_out = projected_out.astype(jnp.bfloat16)
    middle, normed_mid = sum_middle(groups, partial_out, tokens, mlp_gain)
    paired = jnp.dot(normed_mid, w_pair, preferred_element_type=jnp.float32)
    hidden_width = w_pair.shape[1] // 2
    hidden = (jax.nn.silu(paired[:, :hidden_width]) * paired[:, hidden_width:]).astype(jnp.bfloat16)
    down_part = lax.dot_general(
        w_down, hidden, (((0,), (1,)), ((), ())), preferred_element_type=jnp.float32
    ).astype(jnp.bfloat16)
    reduced = sum_scatter(groups, down_part.reshape(groups, -1, new_rows)).T
    out_width = reduced.shape[1]
    residual = lax.dynamic_slice_in_dim(middle, kv_index * out_width, out_width, 1).astype(
        jnp.float32
    )
    mixed = jnp.where((row_ids < live_count)[:, None], residual + reduced, 0.0)
    return mixed.astype(jnp.bfloat16)


def solution(mesh):
    return jax.shard_map(
        shards,
        mesh=mesh,
        in_specs=(
            P("blk", None),
            P(),
            P(),
            P(("blk", "kv"), None),
            P(("blk", "kv"), None),
            P(("blk", "kv"), None),
            P(("blk", "kv"), None),
            P(("blk", "kv"), None),
            P("kv", None),
            P("kv", None),
            P(None, "blk", "kv", None, None),
            P(),
            P(),
            P(),
        ),
        out_specs=P("blk", "kv"),
        check_vma=False,
    )
```

```python
import functools
import math

import jax
import jax.numpy as jnp
from jax import lax
from jax.experimental import pallas as pl
from jax.experimental.pallas import tpu as pltpu
from jax.sharding import PartitionSpec as P

HEADS = 32
KV_HEADS = 8
HD = 80
WINDOW = 4096
SINKS = 4
BLOCK = 128
CAP = 2


FLOOR_SCORE = -1e30
EPSILON = 1e-05
ROPE_BASE = 10000.0


def rms_scale(row_data, gain_vec):
    values = row_data.astype(jnp.float32)
    mean_square = jnp.mean(values * values, axis=-1, keepdims=True)
    return (values * lax.rsqrt(mean_square + EPSILON) * gain_vec).astype(jnp.bfloat16)


def rotate(values, positions):
    head_width = values.shape[-1]
    half_width = head_width // 2
    frequency = ROPE_BASE ** (-2.0 * jnp.arange(half_width, dtype=jnp.float32) / head_width)
    angles = positions.astype(jnp.float32)[:, None] * frequency[None, :]
    cosine = jnp.cos(angles)[:, None, :]
    sine_wave = jnp.sin(angles)[:, None, :]
    first_half = values[..., :half_width]
    second_half = values[..., half_width:]
    return jnp.concatenate(
        [
            first_half * cosine - second_half * sine_wave,
            second_half * cosine + first_half * sine_wave,
        ],
        axis=-1,
    )


def slot_ranks(slot_prompt, prompts, slots):
    onehot = (slot_prompt[:, None] == jnp.arange(prompts, dtype=jnp.int32)[None, :]).astype(
        jnp.int32
    )
    running = jnp.cumsum(onehot, axis=0)
    global_rank = jnp.sum(onehot * (running - 1), axis=1)
    local_count = jnp.cumsum(onehot.reshape(-1, slots, prompts), axis=1).reshape(-1, prompts)
    local_rank = jnp.sum(onehot * (local_count - 1), axis=1)
    return (global_rank, local_rank)


def pack_groups(matrices, groups):
    rows = matrices[0].shape[0]
    pieces = [
        jnp.transpose(
            matrix.astype(jnp.bfloat16).reshape(rows, groups, matrix.shape[1] // groups), (1, 0, 2)
        )
        for matrix in matrices
    ]
    return jnp.concatenate(pieces, axis=2)


MESH = pl.DeviceIdType.MESH
VMEM_SPEC = pl.BlockSpec(memory_space=pltpu.VMEM)


def fan_out(step_count, make):
    copies = [make(step) for step in range(1, step_count)]
    for copy in copies:
        copy.start()
    return copies


def regroup_kernel(
    n_kv, n_blk, first_ref, second_ref, cache_ref, first_out, second_out, cache_out,
    first_in, second_in, cache_in, whole, stage_a, stage_b,
    first_send, first_recv, second_send, second_recv, cache_send, cache_recv, send, recv,
):
    me_kv, me = lax.axis_index("kv"), lax.axis_index("blk")
    rows = first_ref.shape[1]
    half, line, core = lax.div(me, 8), lax.rem(lax.div(me, 2), 4), lax.rem(me, 2)

    barrier = pltpu.get_barrier_semaphore()
    for axis, count, mine in (("kv", n_kv, me_kv), ("blk", n_blk, me)):
        for step in range(1, count):
            pl.semaphore_signal(
                barrier, inc=1, device_id={axis: lax.rem(mine + step, count)}, device_id_type=MESH
            )
    pl.semaphore_wait(barrier, n_kv + n_blk - 2)

    def swap(source, landing, sent, got):
        def make(step):
            peer = lax.rem(me_kv + step, n_kv)
            return pltpu.make_async_remote_copy(
                src_ref=source.at[peer],
                dst_ref=landing.at[me_kv],
                send_sem=sent.at[step - 1],
                recv_sem=got.at[step - 1],
                device_id={"kv": peer},
                device_id_type=MESH,
            )

        return fan_out(n_kv, make)

    def deal(step):
        peer = lax.rem(me + step, n_blk)
        return pltpu.make_async_remote_copy(
            src_ref=cache_ref.at[peer],
            dst_ref=cache_in.at[step - 1],
            send_sem=cache_send.at[step - 1],
            recv_sem=cache_recv.at[step - 1],
            device_id={"blk": peer},
            device_id_type=MESH,
        )

    firsts = swap(first_ref, first_in, first_send, first_recv)
    seconds = swap(second_ref, second_in, second_send, second_recv)
    deals = fan_out(n_blk, deal)

    first_in[me_kv] = first_ref[me_kv]
    for copy in firsts:
        copy.wait_recv()
    for group in range(n_kv):
        stage_a[group * rows : (group + 1) * rows, :] = first_in[group].astype(jnp.float32)
    whole[0] = stage_a[...].astype(jnp.bfloat16)

    passed = {}

    def pass_on(held, peer, slot):
        copy = pltpu.make_async_remote_copy(
            src_ref=whole.at[held],
            dst_ref=whole.at[slot],
            send_sem=send.at[slot - 1],
            recv_sem=recv.at[slot - 1],
            device_id={"blk": peer},
            device_id_type=MESH,
        )
        copy.start()
        passed[slot] = copy

    def along(step):
        return half * 8 + lax.rem(line + step, 4) * 2 + core

    across = lax.rem(me + 8, n_blk)
    sibling = me + 1 - 2 * core
    pass_on(0, across, 8)
    for step in (1, 3, 2):
        pass_on(0, along(step), 2 * step)
    pass_on(0, sibling, 1)
    passed[8].wait_recv()
    for step in (1, 3, 2):
        pass_on(8, along(step), 8 + 2 * step)
    pass_on(8, sibling, 9)

    second_in[me_kv] = second_ref[me_kv]
    for copy in seconds:
        copy.wait_recv()
    for group in range(n_kv):
        stage_b[group * rows : (group + 1) * rows, :] = second_in[group].astype(jnp.float32)
    second_out[...] = stage_b[...].astype(jnp.bfloat16)

    for base in (0, 8):
        for step in (1, 3, 2):
            slot = base + 2 * step
            passed[slot].wait_recv()
            pass_on(slot, sibling, slot + 1)
    for base in (0, 8):
        for step in range(4):
            for other in range(2):
                slot = base + 2 * step + other
                if other:
                    passed[slot].wait_recv()
                owner = (
                    lax.rem(half + base // 8, 2) * 8
                    + lax.rem(line + 4 - step, 4) * 2
                    + lax.rem(core + other, 2)
                )
                first_out[owner] = whole[slot]
    cache_out[me] = cache_ref[me]
    for step in range(1, n_blk):
        deals[step - 1].wait_recv()
        cache_out[lax.rem(me + n_blk - step, n_blk)] = cache_in[step - 1]
    for copy in firsts + seconds + deals + list(passed.values()):
        copy.wait_send()


def regroup(n_kv, n_blk, first, second, cached):
    rows = first.shape[1]
    tall = n_kv * rows
    first_width, second_width = first.shape[2], second.shape[2]
    half = jnp.bfloat16
    dma = pltpu.SemaphoreType.DMA
    return pl.pallas_call(
        functools.partial(regroup_kernel, n_kv, n_blk),
        name="regroup",
        out_shape=(
            jax.ShapeDtypeStruct((n_blk, tall, first_width), half),
            jax.ShapeDtypeStruct((tall, second_width), half),
            jax.ShapeDtypeStruct(cached.shape, half),
        ),
        in_specs=[VMEM_SPEC] * 3,
        out_specs=(VMEM_SPEC,) * 3,
        scratch_shapes=[
            pltpu.VMEM(first.shape, half),
            pltpu.VMEM(second.shape, half),
            pltpu.VMEM((n_blk - 1,) + cached.shape[1:], half),
            pltpu.VMEM((n_blk, tall, first_width), half),
            pltpu.VMEM((tall, first_width), jnp.float32),
            pltpu.VMEM((tall, second_width), jnp.float32),
        ]
        + [dma((n_kv - 1,))] * 4
        + [dma((n_blk - 1,))] * 4,
        compiler_params=pltpu.CompilerParams(collective_id=2, has_side_effects=True),
    )(first, second, cached)


LIFT = 1.0 / math.sqrt(HD) * math.log2(math.e)


def attention_kernel(
    scalars, query_ref, own_key_ref, own_value_ref, blocks_ref, out_ref,
    keys, values, score_a, score_b, row_max, summed,
):
    slots, block = blocks_ref.shape[0], blocks_ref.shape[3]
    rows = query_ref.shape[2]
    depth = keys.shape[1]
    wide = values.shape[0]
    chunk = rows
    per_chunk = chunk // block
    chunks = slots // per_chunk
    before, live_rows = scalars[2 * slots], scalars[2 * slots + 1]

    def padded_key(part, limit):
        spots = lax.broadcasted_iota(jnp.int32, (depth - HD, block), 1)
        lines = lax.broadcasted_iota(jnp.int32, (depth - HD, block), 0)
        bias = jnp.where((lines == 0) & (spots >= limit), FLOOR_SCORE, 0.0)
        return jnp.concatenate([part.astype(jnp.float32), bias], axis=0).T.astype(jnp.bfloat16)

    @pl.when(pl.program_id(0) == 0)
    def _():
        ones = jnp.ones((wide - HD, block), jnp.bfloat16)

        def place(slot, carry):
            limit = jnp.where(
                scalars[slots + slot] > 0, before - scalars[slot] * block, 0
            )
            spot = pl.multiple_of(slot * block, block)
            keys[pl.ds(spot, block), :] = padded_key(blocks_ref[slot, 0], limit)
            values[:, pl.ds(spot, block)] = jnp.concatenate([blocks_ref[slot, 1], ones], axis=0)
            return carry

        lax.fori_loop(0, slots, place, 0)
        for part in range(rows // block):
            near = slice(part * block, (part + 1) * block)
            far = slice(slots * block + part * block, slots * block + (part + 1) * block)
            keys[far, :] = padded_key(own_key_ref[:, near], live_rows - part * block)
            values[:, far] = jnp.concatenate([own_value_ref[:, near], ones], axis=0)

    query = jnp.concatenate(
        [
            query_ref[0].astype(jnp.float32),
            jnp.ones((16, rows), jnp.float32),
            jnp.zeros((depth - HD - 16, rows), jnp.float32),
        ],
        axis=0,
    ).astype(jnp.bfloat16)

    def score(index, into):
        spot = pl.multiple_of(index * chunk, chunk)
        into[...] = jnp.dot(keys[pl.ds(spot, chunk), :], query, preferred_element_type=jnp.float32)

    def window(index, into):
        near = before + rows - WINDOW
        needed = False
        for part in range(per_chunk):
            needed |= scalars[index * per_chunk + part] * block < near

        @pl.when(needed)
        def _():
            for part in range(per_chunk):
                lines = slice(part * block, (part + 1) * block)
                place = scalars[index * per_chunk + part] * block + lax.broadcasted_iota(
                    jnp.int32, (block, rows), 0
                )
                away = before - place + lax.broadcasted_iota(jnp.int32, (block, rows), 1)
                seen = (away < WINDOW) | (place < SINKS)
                into[lines, :] = jnp.where(seen, into[lines, :], FLOOR_SCORE)

    def absorb(index, held):
        spot = pl.multiple_of(index * chunk, chunk)
        now = held[...]
        largest = jnp.maximum(row_max[...], jnp.max(now, axis=0, keepdims=True))
        fade = jnp.exp2((row_max[...] - largest) * LIFT)
        weights = jnp.exp2((now - largest) * LIFT).astype(jnp.bfloat16)
        row_max[...] = largest
        summed[...] = summed[...] * fade + jnp.dot(
            values[:, pl.ds(spot, chunk)], weights, preferred_element_type=jnp.float32
        )

    score(chunks, score_b)
    causal = lax.broadcasted_iota(jnp.int32, (rows, rows), 0) <= lax.broadcasted_iota(
        jnp.int32, (rows, rows), 1
    )
    score_b[...] = jnp.where(causal, score_b[...], FLOOR_SCORE)
    row_max[...] = jnp.full_like(row_max, FLOOR_SCORE)
    summed[...] = jnp.zeros_like(summed)
    score(0, score_a)
    absorb(chunks, score_b)
    window(0, score_a)

    def pair(step, carry):
        first = step * 2
        score(first + 1, score_b)
        absorb(first, score_a)
        window(first + 1, score_b)
        later = lax.rem(first + 2, chunks)
        score(later, score_a)
        absorb(first + 1, score_b)
        window(later, score_a)
        return carry

    lax.fori_loop(0, chunks // 2, pair, 0)
    out_ref[0] = (summed[:HD, :] / summed[HD : HD + 1, :]).astype(jnp.bfloat16)


def attend(scalars, query, own_key, own_value, blocks):
    heads, width, rows = query.shape
    slots, block = blocks.shape[0], blocks.shape[3]
    span = slots * block + rows
    whole = pl.BlockSpec(memory_space=pltpu.VMEM)
    return pl.pallas_call(
        attention_kernel,
        name="attend",
        grid=(heads,),
        out_shape=jax.ShapeDtypeStruct((heads, width, rows), jnp.bfloat16),
        in_specs=[
            pl.BlockSpec(memory_space=pltpu.SMEM),
            pl.BlockSpec((1, width, rows), lambda head: (head, 0, 0)),
            whole,
            whole,
            whole,
        ],
        out_specs=pl.BlockSpec((1, width, rows), lambda head: (head, 0, 0)),
        scratch_shapes=[
            pltpu.VMEM((span, 128), jnp.bfloat16),
            pltpu.VMEM((96, span), jnp.bfloat16),
            pltpu.VMEM((rows, rows), jnp.float32),
            pltpu.VMEM((rows, rows), jnp.float32),
            pltpu.VMEM((1, rows), jnp.float32),
            pltpu.VMEM((96, rows), jnp.float32),
        ],
        cost_estimate=pl.CostEstimate(
            flops=4 * heads * rows * span * 128,
            bytes_accessed=span * 4 * width,
            transcendentals=heads * rows * span,
        ),
    )(scalars, query, own_key, own_value, blocks)


def greet(n, me):
    barrier = pltpu.get_barrier_semaphore()
    for step in range(1, n):
        peer = lax.rem(me + step, n)
        pl.semaphore_signal(barrier, inc=1, device_id={"kv": peer}, device_id_type=MESH)
    pl.semaphore_wait(barrier, n - 1)


def exchange(n, me, piece_ref, landed, send_sem, recv_sem):
    copies = []
    for step in range(1, n):
        peer = lax.rem(me + step, n)
        copy = pltpu.make_async_remote_copy(
            src_ref=piece_ref.at[peer],
            dst_ref=landed.at[step - 1],
            send_sem=send_sem.at[step - 1],
            recv_sem=recv_sem.at[step - 1],
            device_id={"kv": peer},
            device_id_type=MESH,
        )
        copy.start()
        copies.append(copy)
    return copies


def middle_kernel(
    n, piece_ref, token_ref, gain_ref, middle_ref, normed_ref, landed, total, whole,
    send_sem, recv_sem, share_sem, join_sem,
):
    me = lax.axis_index("kv")
    rows = piece_ref.shape[1]
    greet(n, me)
    copies = exchange(n, me, piece_ref, landed, send_sem, recv_sem)
    own = pl.ds(pl.multiple_of(me * rows, rows), rows)
    total[...] = token_ref[own, :].astype(jnp.float32) + piece_ref[me].astype(jnp.float32)
    for step in range(1, n):
        copies[step - 1].wait_recv()
        total[...] += landed[step - 1].astype(jnp.float32)
    whole[0] = total[...].astype(jnp.bfloat16)
    shares = []
    for step in range(1, n):
        peer = lax.rem(me + step, n)
        share = pltpu.make_async_remote_copy(
            src_ref=whole.at[0],
            dst_ref=whole.at[step],
            send_sem=share_sem.at[step - 1],
            recv_sem=join_sem.at[step - 1],
            device_id={"kv": peer},
            device_id_type=MESH,
        )
        share.start()
        shares.append(share)
    for step in range(n):
        if step:
            shares[step - 1].wait_recv()
        owner = lax.rem(me + n - step, n)
        place = pl.ds(pl.multiple_of(owner * rows, rows), rows)
        middle_rows = whole[step]
        middle_ref[place, :] = middle_rows
        values = middle_rows.astype(jnp.float32)
        mean_square = jnp.mean(values * values, axis=-1, keepdims=True)
        normed_ref[place, :] = (
            values * lax.rsqrt(mean_square + EPSILON) * gain_ref[...]
        ).astype(jnp.bfloat16)
    for copy in copies + shares:
        copy.wait_send()


def sum_middle(n, partial_out, tokens, mlp_gain):
    rows, width = tokens.shape
    piece = rows // n
    whole_shape = jax.ShapeDtypeStruct((rows, width), jnp.bfloat16)
    return pl.pallas_call(
        functools.partial(middle_kernel, n),
        name="sum_middle",
        cost_estimate=pl.CostEstimate(flops=0, bytes_accessed=200_000_000, transcendentals=0),
        out_shape=(whole_shape, whole_shape),
        in_specs=[VMEM_SPEC] * 3,
        out_specs=(VMEM_SPEC, VMEM_SPEC),
        scratch_shapes=[
            pltpu.VMEM((n - 1, piece, width), jnp.bfloat16),
            pltpu.VMEM((piece, width), jnp.float32),
            pltpu.VMEM((n, piece, width), jnp.bfloat16),
        ]
        + [pltpu.SemaphoreType.DMA((n - 1,))] * 4,
        compiler_params=pltpu.CompilerParams(collective_id=0, has_side_effects=True),
    )(partial_out.reshape(n, piece, width), tokens, mlp_gain.reshape(1, width))


def scatter_kernel(n, piece_ref, out_ref, landed, send_sem, recv_sem):
    me = lax.axis_index("kv")
    greet(n, me)
    copies = exchange(n, me, piece_ref, landed, send_sem, recv_sem)
    out_ref[...] = piece_ref[me].astype(jnp.float32)
    for step in range(1, n):
        copies[step - 1].wait_recv()
        out_ref[...] += landed[step - 1].astype(jnp.float32)
    for copy in copies:
        copy.wait_send()


def sum_scatter(n, pieces):
    shape = pieces.shape[1:]
    return pl.pallas_call(
        functools.partial(scatter_kernel, n),
        name="sum_scatter",
        out_shape=jax.ShapeDtypeStruct(shape, jnp.float32),
        in_specs=[VMEM_SPEC],
        out_specs=VMEM_SPEC,
        scratch_shapes=[pltpu.VMEM((n - 1,) + shape, jnp.bfloat16)]
        + [pltpu.SemaphoreType.DMA((n - 1,))] * 2,
        compiler_params=pltpu.CompilerParams(collective_id=1, has_side_effects=True),
    )(pieces)


def shards(
    tokens,
    attn_gain,
    mlp_gain,
    w_query,
    w_key,
    w_value,
    w_gate,
    w_up,
    w_out,
    w_down,
    cache,
    slot_prompt,
    prefix_len,
    new_len,
):
    groups = lax.axis_size("kv")
    n_blocks = lax.axis_size("blk")
    blk_index = lax.axis_index("blk")
    kv_index = lax.axis_index("kv")
    query_width = w_query.shape[1] // groups
    key_width = w_key.shape[1] // groups
    kv_local = key_width // HD
    new_rows = tokens.shape[0]
    prompts = prefix_len.shape[0]
    slots = cache.shape[1]
    prefix_here = prefix_len[blk_index]
    live_count = new_len[blk_index]
    row_ids = jnp.arange(new_rows, dtype=jnp.int32)
    positions = prefix_here + row_ids
    global_rank, local_rank = slot_ranks(slot_prompt, prompts, slots)
    own_prompts = lax.dynamic_slice_in_dim(slot_prompt, blk_index * slots, slots)
    own_ranks = lax.dynamic_slice_in_dim(local_rank, blk_index * slots, slots)
    placed = own_prompts * CAP + own_ranks
    buffer_ids = jnp.arange(prompts * CAP, dtype=jnp.int32)
    matches = placed[None, :] == buffer_ids[:, None]
    source_slot = jnp.sum(
        jnp.where(matches, jnp.arange(slots, dtype=jnp.int32)[None, :], 0), axis=1
    )
    by_slot = jnp.transpose(cache.reshape(2, slots, HD, BLOCK), (1, 0, 2, 3))
    outgoing = jnp.take(by_slot, source_slot, axis=0, mode="clip").reshape(prompts, CAP, 2, HD, BLOCK)
    w_first, w_second, arrived = regroup(
        groups,
        n_blocks,
        pack_groups((w_query, w_key, w_value), groups),
        pack_groups((w_gate, w_up), groups),
        outgoing,
    )
    w_qkv = w_first.reshape(-1, w_first.shape[2])
    w_pair = lax.all_gather(w_second, "blk", axis=0, tiled=True)
    normed = rms_scale(tokens, attn_gain)
    projected = jnp.dot(normed, w_qkv, preferred_element_type=jnp.float32)
    queries = rotate(projected[:, :query_width].reshape(new_rows, -1, HD), positions).astype(
        jnp.bfloat16
    )
    key_new = rotate(
        projected[:, query_width : query_width + key_width].reshape(new_rows, kv_local, HD),
        positions,
    ).astype(jnp.bfloat16)
    value_new = (
        projected[:, query_width + key_width :].reshape(new_rows, kv_local, HD).astype(jnp.bfloat16)
    )
    slot_ids = jnp.arange(prompts * slots, dtype=jnp.int32)
    landing = slot_ids // slots * CAP + local_rank
    for_me = slot_prompt == blk_index
    received = (landing[None, :] == buffer_ids[:, None]) & for_me[None, :]
    block_number = jnp.sum(jnp.where(received, global_rank[None, :], 0), axis=1)
    block_live = jnp.any(received, axis=1)
    blocks = arrived.reshape(prompts * CAP, 2, HD, BLOCK)
    scalars = jnp.concatenate(
        [block_number, block_live.astype(jnp.int32), jnp.stack([prefix_here, live_count])]
    )
    attended = attend(
        scalars,
        jnp.transpose(queries, (1, 2, 0)),
        key_new.reshape(new_rows, HD).T,
        value_new.reshape(new_rows, HD).T,
        blocks,
    ).reshape(-1, new_rows)
    projected_out = lax.dot_general(
        attended, w_out, (((0,), (0,)), ((), ())), preferred_element_type=jnp.float32
    )
    partial_out = projected_out.astype(jnp.bfloat16)
    middle, normed_mid = sum_middle(groups, partial_out, tokens, mlp_gain)
    paired = jnp.dot(normed_mid, w_pair, preferred_element_type=jnp.float32)
    hidden_width = w_pair.shape[1] // 2
    hidden = (jax.nn.silu(paired[:, :hidden_width]) * paired[:, hidden_width:]).astype(jnp.bfloat16)
    down_part = lax.dot_general(
        w_down, hidden, (((0,), (1,)), ((), ())), preferred_element_type=jnp.float32
    ).astype(jnp.bfloat16)
    reduced = sum_scatter(groups, down_part.reshape(groups, -1, new_rows)).T
    out_width = reduced.shape[1]
    residual = lax.dynamic_slice_in_dim(middle, kv_index * out_width, out_width, 1).astype(
        jnp.float32
    )
    mixed = jnp.where((row_ids < live_count)[:, None], residual + reduced, 0.0)
    return mixed.astype(jnp.bfloat16)


def solution(mesh):
    return jax.shard_map(
        shards,
        mesh=mesh,
        in_specs=(
            P("blk", None),
            P(),
            P(),
            P(("blk", "kv"), None),
            P(("blk", "kv"), None),
            P(("blk", "kv"), None),
            P(("blk", "kv"), None),
            P(("blk", "kv"), None),
            P("kv", None),
            P("kv", None),
            P(None, "blk", "kv", None, None),
            P(),
            P(),
            P(),
        ),
        out_specs=P("blk", "kv"),
        check_vma=False,
    )
```

```python
import functools
import math

import jax
import jax.numpy as jnp
from jax import lax
from jax.experimental import pallas as pl
from jax.experimental.pallas import tpu as pltpu
from jax.sharding import PartitionSpec as P

HEADS = 32
KV_HEADS = 8
HD = 80
WINDOW = 4096
SINKS = 4
BLOCK = 128
CAP = 2


FLOOR_SCORE = -1e30
EPSILON = 1e-05
ROPE_BASE = 10000.0


def rms_scale(row_data, gain_vec):
    values = row_data.astype(jnp.float32)
    mean_square = jnp.mean(values * values, axis=-1, keepdims=True)
    return (values * lax.rsqrt(mean_square + EPSILON) * gain_vec).astype(jnp.bfloat16)


def rotate(values, positions):
    head_width = values.shape[-1]
    half_width = head_width // 2
    frequency = ROPE_BASE ** (-2.0 * jnp.arange(half_width, dtype=jnp.float32) / head_width)
    angles = positions.astype(jnp.float32)[:, None] * frequency[None, :]
    cosine = jnp.cos(angles)[:, None, :]
    sine_wave = jnp.sin(angles)[:, None, :]
    first_half = values[..., :half_width]
    second_half = values[..., half_width:]
    return jnp.concatenate(
        [
            first_half * cosine - second_half * sine_wave,
            second_half * cosine + first_half * sine_wave,
        ],
        axis=-1,
    )


def slot_ranks(slot_prompt, prompts, slots):
    onehot = (slot_prompt[:, None] == jnp.arange(prompts, dtype=jnp.int32)[None, :]).astype(
        jnp.int32
    )
    running = jnp.cumsum(onehot, axis=0)
    global_rank = jnp.sum(onehot * (running - 1), axis=1)
    local_count = jnp.cumsum(onehot.reshape(-1, slots, prompts), axis=1).reshape(-1, prompts)
    local_rank = jnp.sum(onehot * (local_count - 1), axis=1)
    return (global_rank, local_rank)


def pack_groups(matrices, groups):
    rows = matrices[0].shape[0]
    pieces = [
        jnp.transpose(
            matrix.astype(jnp.bfloat16).reshape(rows, groups, matrix.shape[1] // groups), (1, 0, 2)
        )
        for matrix in matrices
    ]
    return jnp.concatenate(pieces, axis=2)


MESH = pl.DeviceIdType.MESH
VMEM_SPEC = pl.BlockSpec(memory_space=pltpu.VMEM)


def fan_out(step_count, make):
    copies = [make(step) for step in range(1, step_count)]
    for copy in copies:
        copy.start()
    return copies


def regroup_kernel(
    n_kv, n_blk, first_ref, second_ref, cache_ref, first_out, second_out, cache_out,
    first_in, second_in, cache_in, whole, stage_a, stage_b,
    first_send, first_recv, second_send, second_recv, cache_send, cache_recv, send, recv,
):
    me_kv, me = lax.axis_index("kv"), lax.axis_index("blk")
    rows = first_ref.shape[1]
    half, line, core = lax.div(me, 8), lax.rem(lax.div(me, 2), 4), lax.rem(me, 2)

    barrier = pltpu.get_barrier_semaphore()
    for axis, count, mine in (("kv", n_kv, me_kv), ("blk", n_blk, me)):
        for step in range(1, count):
            pl.semaphore_signal(
                barrier, inc=1, device_id={axis: lax.rem(mine + step, count)}, device_id_type=MESH
            )
    pl.semaphore_wait(barrier, n_kv + n_blk - 2)

    def swap(source, landing, sent, got):
        def make(step):
            peer = lax.rem(me_kv + step, n_kv)
            return pltpu.make_async_remote_copy(
                src_ref=source.at[peer],
                dst_ref=landing.at[me_kv],
                send_sem=sent.at[step - 1],
                recv_sem=got.at[step - 1],
                device_id={"kv": peer},
                device_id_type=MESH,
            )

        return fan_out(n_kv, make)

    def deal(step):
        peer = lax.rem(me + step, n_blk)
        return pltpu.make_async_remote_copy(
            src_ref=cache_ref.at[peer],
            dst_ref=cache_in.at[step - 1],
            send_sem=cache_send.at[step - 1],
            recv_sem=cache_recv.at[step - 1],
            device_id={"blk": peer},
            device_id_type=MESH,
        )

    firsts = swap(first_ref, first_in, first_send, first_recv)
    seconds = swap(second_ref, second_in, second_send, second_recv)
    deals = fan_out(n_blk, deal)

    first_in[me_kv] = first_ref[me_kv]
    for copy in firsts:
        copy.wait_recv()
    for group in range(n_kv):
        stage_a[group * rows : (group + 1) * rows, :] = first_in[group].astype(jnp.float32)
    whole[0] = stage_a[...].astype(jnp.bfloat16)

    passed = {}

    def pass_on(held, peer, slot):
        copy = pltpu.make_async_remote_copy(
            src_ref=whole.at[held],
            dst_ref=whole.at[slot],
            send_sem=send.at[slot - 1],
            recv_sem=recv.at[slot - 1],
            device_id={"blk": peer},
            device_id_type=MESH,
        )
        copy.start()
        passed[slot] = copy

    def along(step):
        return half * 8 + lax.rem(line + step, 4) * 2 + core

    across = lax.rem(me + 8, n_blk)
    sibling = me + 1 - 2 * core
    pass_on(0, across, 8)
    for step in (1, 3, 2):
        pass_on(0, along(step), 2 * step)
    pass_on(0, sibling, 1)
    passed[8].wait_recv()
    for step in (1, 3, 2):
        pass_on(8, along(step), 8 + 2 * step)
    pass_on(8, sibling, 9)

    second_in[me_kv] = second_ref[me_kv]
    for copy in seconds:
        copy.wait_recv()
    for group in range(n_kv):
        stage_b[group * rows : (group + 1) * rows, :] = second_in[group].astype(jnp.float32)
    second_out[...] = stage_b[...].astype(jnp.bfloat16)

    for base in (0, 8):
        for step in (1, 3, 2):
            slot = base + 2 * step
            passed[slot].wait_recv()
            pass_on(slot, sibling, slot + 1)
    for base in (0, 8):
        for step in range(4):
            for other in range(2):
                slot = base + 2 * step + other
                if other:
                    passed[slot].wait_recv()
                owner = (
                    lax.rem(half + base // 8, 2) * 8
                    + lax.rem(line + 4 - step, 4) * 2
                    + lax.rem(core + other, 2)
                )
                first_out[owner] = whole[slot]
    cache_out[me] = cache_ref[me]
    for step in range(1, n_blk):
        deals[step - 1].wait_recv()
        cache_out[lax.rem(me + n_blk - step, n_blk)] = cache_in[step - 1]
    for copy in firsts + seconds + deals + list(passed.values()):
        copy.wait_send()


def regroup(n_kv, n_blk, first, second, cached):
    rows = first.shape[1]
    tall = n_kv * rows
    first_width, second_width = first.shape[2], second.shape[2]
    half = jnp.bfloat16
    dma = pltpu.SemaphoreType.DMA
    return pl.pallas_call(
        functools.partial(regroup_kernel, n_kv, n_blk),
        name="regroup",
        out_shape=(
            jax.ShapeDtypeStruct((n_blk, tall, first_width), half),
            jax.ShapeDtypeStruct((tall, second_width), half),
            jax.ShapeDtypeStruct(cached.shape, half),
        ),
        in_specs=[VMEM_SPEC] * 3,
        out_specs=(VMEM_SPEC,) * 3,
        scratch_shapes=[
            pltpu.VMEM(first.shape, half),
            pltpu.VMEM(second.shape, half),
            pltpu.VMEM((n_blk - 1,) + cached.shape[1:], half),
            pltpu.VMEM((n_blk, tall, first_width), half),
            pltpu.VMEM((tall, first_width), jnp.float32),
            pltpu.VMEM((tall, second_width), jnp.float32),
        ]
        + [dma((n_kv - 1,))] * 4
        + [dma((n_blk - 1,))] * 4,
        compiler_params=pltpu.CompilerParams(collective_id=2, has_side_effects=True),
    )(first, second, cached)


LIFT = 1.0 / math.sqrt(HD) * math.log2(math.e)


def attention_kernel(
    scalars, query_ref, own_key_ref, own_value_ref, blocks_ref, out_ref,
    keys, values, score_a, score_b, row_max, summed,
):
    slots, block = blocks_ref.shape[0], blocks_ref.shape[3]
    rows = query_ref.shape[2]
    depth = keys.shape[1]
    wide = values.shape[0]
    chunk = rows
    per_chunk = chunk // block
    chunks = slots // per_chunk
    before, live_rows = scalars[2 * slots], scalars[2 * slots + 1]

    def padded_key(part, limit):
        spots = lax.broadcasted_iota(jnp.int32, (depth - HD, block), 1)
        lines = lax.broadcasted_iota(jnp.int32, (depth - HD, block), 0)
        bias = jnp.where((lines == 0) & (spots >= limit), FLOOR_SCORE, 0.0)
        return jnp.concatenate([part.astype(jnp.float32), bias], axis=0).T.astype(jnp.bfloat16)

    @pl.when(pl.program_id(0) == 0)
    def _():
        ones = jnp.ones((wide - HD, block), jnp.bfloat16)

        def place(slot, carry):
            limit = jnp.where(
                scalars[slots + slot] > 0, before - scalars[slot] * block, 0
            )
            spot = pl.multiple_of(slot * block, block)
            keys[pl.ds(spot, block), :] = padded_key(blocks_ref[slot, 0], limit)
            values[:, pl.ds(spot, block)] = jnp.concatenate([blocks_ref[slot, 1], ones], axis=0)
            return carry

        lax.fori_loop(0, slots, place, 0)
        for part in range(rows // block):
            near = slice(part * block, (part + 1) * block)
            far = slice(slots * block + part * block, slots * block + (part + 1) * block)
            keys[far, :] = padded_key(own_key_ref[:, near], live_rows - part * block)
            values[:, far] = jnp.concatenate([own_value_ref[:, near], ones], axis=0)

    query = jnp.concatenate(
        [
            query_ref[0].astype(jnp.float32),
            jnp.ones((16, rows), jnp.float32),
            jnp.zeros((depth - HD - 16, rows), jnp.float32),
        ],
        axis=0,
    ).astype(jnp.bfloat16)

    def score(index, into):
        spot = pl.multiple_of(index * chunk, chunk)
        into[...] = jnp.dot(keys[pl.ds(spot, chunk), :], query, preferred_element_type=jnp.float32)

    def window(index, into):
        near = before + rows - WINDOW
        needed = False
        for part in range(per_chunk):
            needed |= scalars[index * per_chunk + part] * block < near

        @pl.when(needed)
        def _():
            for part in range(per_chunk):
                lines = slice(part * block, (part + 1) * block)
                place = scalars[index * per_chunk + part] * block + lax.broadcasted_iota(
                    jnp.int32, (block, rows), 0
                )
                away = before - place + lax.broadcasted_iota(jnp.int32, (block, rows), 1)
                seen = (away < WINDOW) | (place < SINKS)
                into[lines, :] = jnp.where(seen, into[lines, :], FLOOR_SCORE)

    def absorb(index, held):
        spot = pl.multiple_of(index * chunk, chunk)
        now = held[...]
        largest = jnp.maximum(row_max[...], jnp.max(now, axis=0, keepdims=True))
        fade = jnp.exp2((row_max[...] - largest) * LIFT)
        weights = jnp.exp2((now - largest) * LIFT).astype(jnp.bfloat16)
        row_max[...] = largest
        summed[...] = summed[...] * fade + jnp.dot(
            values[:, pl.ds(spot, chunk)], weights, preferred_element_type=jnp.float32
        )

    score(chunks, score_b)
    causal = lax.broadcasted_iota(jnp.int32, (rows, rows), 0) <= lax.broadcasted_iota(
        jnp.int32, (rows, rows), 1
    )
    score_b[...] = jnp.where(causal, score_b[...], FLOOR_SCORE)
    row_max[...] = jnp.full_like(row_max, FLOOR_SCORE)
    summed[...] = jnp.zeros_like(summed)
    score(0, score_a)
    absorb(chunks, score_b)
    window(0, score_a)

    def pair(step, carry):
        first = step * 2
        score(first + 1, score_b)
        absorb(first, score_a)
        window(first + 1, score_b)
        later = lax.rem(first + 2, chunks)
        score(later, score_a)
        absorb(first + 1, score_b)
        window(later, score_a)
        return carry

    lax.fori_loop(0, chunks // 2, pair, 0)
    out_ref[0] = (summed[:HD, :] / summed[HD : HD + 1, :]).astype(jnp.bfloat16)


def attend(scalars, query, own_key, own_value, blocks):
    heads, width, rows = query.shape
    slots, block = blocks.shape[0], blocks.shape[3]
    span = slots * block + rows
    whole = pl.BlockSpec(memory_space=pltpu.VMEM)
    return pl.pallas_call(
        attention_kernel,
        name="attend",
        grid=(heads,),
        out_shape=jax.ShapeDtypeStruct((heads, width, rows), jnp.bfloat16),
        in_specs=[
            pl.BlockSpec(memory_space=pltpu.SMEM),
            pl.BlockSpec((1, width, rows), lambda head: (head, 0, 0)),
            whole,
            whole,
            whole,
        ],
        out_specs=pl.BlockSpec((1, width, rows), lambda head: (head, 0, 0)),
        scratch_shapes=[
            pltpu.VMEM((span, 128), jnp.bfloat16),
            pltpu.VMEM((96, span), jnp.bfloat16),
            pltpu.VMEM((rows, rows), jnp.float32),
            pltpu.VMEM((rows, rows), jnp.float32),
            pltpu.VMEM((1, rows), jnp.float32),
            pltpu.VMEM((96, rows), jnp.float32),
        ],
        cost_estimate=pl.CostEstimate(
            flops=4 * heads * rows * span * 128,
            bytes_accessed=span * 4 * width,
            transcendentals=heads * rows * span,
        ),
    )(scalars, query, own_key, own_value, blocks)


def greet(n, me):
    barrier = pltpu.get_barrier_semaphore()
    for step in range(1, n):
        peer = lax.rem(me + step, n)
        pl.semaphore_signal(barrier, inc=1, device_id={"kv": peer}, device_id_type=MESH)
    pl.semaphore_wait(barrier, n - 1)


def exchange(n, me, piece_ref, landed, send_sem, recv_sem):
    copies = []
    for step in range(1, n):
        peer = lax.rem(me + step, n)
        copy = pltpu.make_async_remote_copy(
            src_ref=piece_ref.at[peer],
            dst_ref=landed.at[step - 1],
            send_sem=send_sem.at[step - 1],
            recv_sem=recv_sem.at[step - 1],
            device_id={"kv": peer},
            device_id_type=MESH,
        )
        copy.start()
        copies.append(copy)
    return copies


def middle_kernel(
    n, piece_ref, token_ref, gain_ref, middle_ref, normed_ref, landed, total, whole,
    send_sem, recv_sem, share_sem, join_sem,
):
    me = lax.axis_index("kv")
    rows = piece_ref.shape[1]
    greet(n, me)
    copies = exchange(n, me, piece_ref, landed, send_sem, recv_sem)
    own = pl.ds(pl.multiple_of(me * rows, rows), rows)
    total[...] = token_ref[own, :].astype(jnp.float32) + piece_ref[me].astype(jnp.float32)
    for step in range(1, n):
        copies[step - 1].wait_recv()
        total[...] += landed[step - 1].astype(jnp.float32)
    whole[0] = total[...].astype(jnp.bfloat16)
    shares = []
    for step in range(1, n):
        peer = lax.rem(me + step, n)
        share = pltpu.make_async_remote_copy(
            src_ref=whole.at[0],
            dst_ref=whole.at[step],
            send_sem=share_sem.at[step - 1],
            recv_sem=join_sem.at[step - 1],
            device_id={"kv": peer},
            device_id_type=MESH,
        )
        share.start()
        shares.append(share)
    for step in range(n):
        if step:
            shares[step - 1].wait_recv()
        owner = lax.rem(me + n - step, n)
        place = pl.ds(pl.multiple_of(owner * rows, rows), rows)
        middle_rows = whole[step]
        middle_ref[place, :] = middle_rows
        values = middle_rows.astype(jnp.float32)
        mean_square = jnp.mean(values * values, axis=-1, keepdims=True)
        normed_ref[place, :] = (
            values * lax.rsqrt(mean_square + EPSILON) * gain_ref[...]
        ).astype(jnp.bfloat16)
    for copy in copies + shares:
        copy.wait_send()


def sum_middle(n, partial_out, tokens, mlp_gain):
    rows, width = tokens.shape
    piece = rows // n
    whole_shape = jax.ShapeDtypeStruct((rows, width), jnp.bfloat16)
    return pl.pallas_call(
        functools.partial(middle_kernel, n),
        name="sum_middle",
        cost_estimate=pl.CostEstimate(flops=0, bytes_accessed=200_000_000, transcendentals=0),
        out_shape=(whole_shape, whole_shape),
        in_specs=[VMEM_SPEC] * 3,
        out_specs=(VMEM_SPEC, VMEM_SPEC),
        scratch_shapes=[
            pltpu.VMEM((n - 1, piece, width), jnp.bfloat16),
            pltpu.VMEM((piece, width), jnp.float32),
            pltpu.VMEM((n, piece, width), jnp.bfloat16),
        ]
        + [pltpu.SemaphoreType.DMA((n - 1,))] * 4,
        compiler_params=pltpu.CompilerParams(collective_id=0, has_side_effects=True),
    )(partial_out.reshape(n, piece, width), tokens, mlp_gain.reshape(1, width))


def hidden_kernel(
    n, normed_ref, middle_hbm, pair_hbm, down_hbm, out_ref, pair, down, hidden, terms, landed,
    window, turned, pair_sem, down_sem, window_sem, send_sem, recv_sem,
):
    me = lax.axis_index("kv")
    rows, width = normed_ref.shape
    halves, part = terms.shape[0], terms.shape[2]
    piece = width // n
    tiles = pair.shape[1] // 256
    units = down.shape[0]
    barrier = pltpu.get_barrier_semaphore()
    for step in range(1, n):
        peer = lax.rem(me + step, n)
        pl.semaphore_signal(barrier, inc=1, device_id={"kv": peer}, device_id_type=MESH)

    def bring(tile):
        lanes = pl.ds(pl.multiple_of(tile * 256, 256), 256)
        return pltpu.make_async_copy(pair_hbm.at[:, lanes], pair.at[:, lanes], pair_sem.at[tile])

    for tile in range(tiles):
        bring(tile).start()
    fetch = pltpu.make_async_copy(down_hbm, down, down_sem)
    fetch.start()
    left = lax.div(me * piece, 128) * 128
    view = pltpu.make_async_copy(
        middle_hbm.at[:, pl.ds(pl.multiple_of(left, 128), window.shape[1])], window, window_sem
    )
    view.start()

    copies = []
    for half in range(halves):
        lines = slice(half * part, (half + 1) * part)

        @pl.loop(0, tiles)
        def _(tile):
            if half == 0:
                bring(tile).wait()
            lanes = pl.ds(pl.multiple_of(tile * 256, 256), 256)
            both = jnp.dot(normed_ref[lines, :], pair[:, lanes], preferred_element_type=jnp.float32)
            gate, up = both[:, :128], both[:, 128:]
            hidden[:, pl.ds(pl.multiple_of(tile * 128, 128), 128)] = (
                gate / (1.0 + jnp.exp(-gate)) * up
            ).astype(jnp.bfloat16)

        if half == 0:
            fetch.wait()

        @pl.loop(0, width // 512)
        def _(tile):
            spot = pl.ds(pl.multiple_of(tile * 512, 512), 512)
            term = jnp.dot(
                hidden[:, :units], down[:, spot], preferred_element_type=jnp.float32
            )
            terms[half, spot, :] = term.T.astype(jnp.bfloat16)

        if half == 0:
            pl.semaphore_wait(barrier, n - 1)
        for step in range(1, n):
            peer = lax.rem(me + step, n)
            copy = pltpu.make_async_remote_copy(
                src_ref=terms.at[half, pl.ds(pl.multiple_of(peer * piece, piece), piece)],
                dst_ref=landed.at[half, step - 1],
                send_sem=send_sem.at[half, step - 1],
                recv_sem=recv_sem.at[half, step - 1],
                device_id={"kv": peer},
                device_id_type=MESH,
            )
            copy.start()
            copies.append(copy)
    view.wait()
    turned[...] = window[...].astype(jnp.float32).T
    residual = pl.ds(pl.multiple_of(me * piece - left, 64), piece)
    for half in range(halves):
        lines = slice(half * part, (half + 1) * part)
        own = pl.ds(pl.multiple_of(me * piece, piece), piece)
        out_ref[:, lines] = turned[residual, lines] + terms[half, own, :].astype(jnp.float32)
        for step in range(1, n):
            copies[half * (n - 1) + step - 1].wait_recv()
            out_ref[:, lines] += landed[half, step - 1].astype(jnp.float32)
    for copy in copies:
        copy.wait_send()


def feed_forward(n, normed_mid, middle, w_pair, w_down):
    rows, width = normed_mid.shape
    halves = 2
    part = rows // halves
    piece = width // n
    half = jnp.bfloat16
    dma = pltpu.SemaphoreType.DMA
    any_spec = pl.BlockSpec(memory_space=pl.ANY)
    return pl.pallas_call(
        functools.partial(hidden_kernel, n),
        name="feed_forward",
        out_shape=jax.ShapeDtypeStruct((piece, rows), jnp.float32),
        in_specs=[VMEM_SPEC, any_spec, any_spec, any_spec],
        out_specs=VMEM_SPEC,
        scratch_shapes=[
            pltpu.VMEM(w_pair.shape, half),
            pltpu.VMEM(w_down.shape, half),
            pltpu.VMEM((part, w_pair.shape[1] // 2), half),
            pltpu.VMEM((halves, width, part), half),
            pltpu.VMEM((halves, n - 1, piece, part), half),
            pltpu.VMEM((rows, piece + 64), half),
            pltpu.VMEM((piece + 64, rows), jnp.float32),
            dma((w_pair.shape[1] // 256,)),
            dma,
            dma,
            dma((halves, n - 1)),
            dma((halves, n - 1)),
        ],
        compiler_params=pltpu.CompilerParams(
            collective_id=1, has_side_effects=True, vmem_limit_bytes=56 * 1024 * 1024
        ),
    )(normed_mid, middle, w_pair, w_down)


def pack_pairs(first, second, groups):
    rows, columns = first.shape
    units = columns // groups
    padded = -(-units // 128) * 128
    tiles = [
        jnp.pad(
            matrix.astype(jnp.bfloat16).reshape(rows, groups, units),
            ((0, 0), (0, 0), (0, padded - units)),
        ).reshape(rows, groups, -1, 1, 128)
        for matrix in (first, second)
    ]
    return jnp.transpose(jnp.concatenate(tiles, axis=3), (1, 0, 2, 3, 4)).reshape(groups, rows, -1)


def shards(
    tokens,
    attn_gain,
    mlp_gain,
    w_query,
    w_key,
    w_value,
    w_gate,
    w_up,
    w_out,
    w_down,
    cache,
    slot_prompt,
    prefix_len,
    new_len,
):
    groups = lax.axis_size("kv")
    n_blocks = lax.axis_size("blk")
    blk_index = lax.axis_index("blk")
    kv_index = lax.axis_index("kv")
    query_width = w_query.shape[1] // groups
    key_width = w_key.shape[1] // groups
    kv_local = key_width // HD
    new_rows = tokens.shape[0]
    prompts = prefix_len.shape[0]
    slots = cache.shape[1]
    prefix_here = prefix_len[blk_index]
    live_count = new_len[blk_index]
    row_ids = jnp.arange(new_rows, dtype=jnp.int32)
    positions = prefix_here + row_ids
    global_rank, local_rank = slot_ranks(slot_prompt, prompts, slots)
    own_prompts = lax.dynamic_slice_in_dim(slot_prompt, blk_index * slots, slots)
    own_ranks = lax.dynamic_slice_in_dim(local_rank, blk_index * slots, slots)
    placed = own_prompts * CAP + own_ranks
    buffer_ids = jnp.arange(prompts * CAP, dtype=jnp.int32)
    matches = placed[None, :] == buffer_ids[:, None]
    source_slot = jnp.sum(
        jnp.where(matches, jnp.arange(slots, dtype=jnp.int32)[None, :], 0), axis=1
    )
    by_slot = jnp.transpose(cache.reshape(2, slots, HD, BLOCK), (1, 0, 2, 3))
    outgoing = jnp.take(by_slot, source_slot, axis=0, mode="clip").reshape(prompts, CAP, 2, HD, BLOCK)
    w_first, w_second, arrived = regroup(
        groups,
        n_blocks,
        pack_groups((w_query, w_key, w_value), groups),
        pack_pairs(w_gate, w_up, groups),
        outgoing,
    )
    w_qkv = w_first.reshape(-1, w_first.shape[2])
    w_pair = lax.all_gather(w_second, "blk", axis=0, tiled=True)
    normed = rms_scale(tokens, attn_gain)
    projected = jnp.dot(normed, w_qkv, preferred_element_type=jnp.float32)
    queries = rotate(projected[:, :query_width].reshape(new_rows, -1, HD), positions).astype(
        jnp.bfloat16
    )
    key_new = rotate(
        projected[:, query_width : query_width + key_width].reshape(new_rows, kv_local, HD),
        positions,
    ).astype(jnp.bfloat16)
    value_new = (
        projected[:, query_width + key_width :].reshape(new_rows, kv_local, HD).astype(jnp.bfloat16)
    )
    slot_ids = jnp.arange(prompts * slots, dtype=jnp.int32)
    landing = slot_ids // slots * CAP + local_rank
    for_me = slot_prompt == blk_index
    received = (landing[None, :] == buffer_ids[:, None]) & for_me[None, :]
    block_number = jnp.sum(jnp.where(received, global_rank[None, :], 0), axis=1)
    block_live = jnp.any(received, axis=1)
    blocks = arrived.reshape(prompts * CAP, 2, HD, BLOCK)
    scalars = jnp.concatenate(
        [block_number, block_live.astype(jnp.int32), jnp.stack([prefix_here, live_count])]
    )
    attended = attend(
        scalars,
        jnp.transpose(queries, (1, 2, 0)),
        key_new.reshape(new_rows, HD).T,
        value_new.reshape(new_rows, HD).T,
        blocks,
    ).reshape(-1, new_rows)
    projected_out = lax.dot_general(
        attended, w_out, (((0,), (0,)), ((), ())), preferred_element_type=jnp.float32
    )
    partial_out = projected_out.astype(jnp.bfloat16)
    middle, normed_mid = sum_middle(groups, partial_out, tokens, mlp_gain)
    summed = feed_forward(groups, normed_mid, middle, w_pair, w_down).T
    mixed = jnp.where((row_ids < live_count)[:, None], summed, 0.0)
    return mixed.astype(jnp.bfloat16)


def solution(mesh):
    return jax.shard_map(
        shards,
        mesh=mesh,
        in_specs=(
            P("blk", None),
            P(),
            P(),
            P(("blk", "kv"), None),
            P(("blk", "kv"), None),
            P(("blk", "kv"), None),
            P(("blk", "kv"), None),
            P(("blk", "kv"), None),
            P("kv", None),
            P("kv", None),
            P(None, "blk", "kv", None, None),
            P(),
            P(),
            P(),
        ),
        out_specs=P("blk", "kv"),
        check_vma=False,
    )
```

```python
import functools
import math

import jax
import jax.numpy as jnp
from jax import lax
from jax.experimental import pallas as pl
from jax.experimental.pallas import tpu as pltpu
from jax.sharding import PartitionSpec as P

HEADS = 32
KV_HEADS = 8
HD = 80
WINDOW = 4096
SINKS = 4
BLOCK = 128
CAP = 2


FLOOR_SCORE = -1e30
EPSILON = 1e-05
ROPE_BASE = 10000.0


def rms_scale(row_data, gain_vec):
    values = row_data.astype(jnp.float32)
    mean_square = jnp.mean(values * values, axis=-1, keepdims=True)
    return (values * lax.rsqrt(mean_square + EPSILON) * gain_vec).astype(jnp.bfloat16)


def rotate(values, positions):
    head_width = values.shape[-1]
    half_width = head_width // 2
    frequency = ROPE_BASE ** (-2.0 * jnp.arange(half_width, dtype=jnp.float32) / head_width)
    angles = positions.astype(jnp.float32)[:, None] * frequency[None, :]
    cosine = jnp.cos(angles)[:, None, :]
    sine_wave = jnp.sin(angles)[:, None, :]
    first_half = values[..., :half_width]
    second_half = values[..., half_width:]
    return jnp.concatenate(
        [
            first_half * cosine - second_half * sine_wave,
            second_half * cosine + first_half * sine_wave,
        ],
        axis=-1,
    )


def slot_ranks(slot_prompt, prompts, slots):
    onehot = (slot_prompt[:, None] == jnp.arange(prompts, dtype=jnp.int32)[None, :]).astype(
        jnp.int32
    )
    running = jnp.cumsum(onehot, axis=0)
    global_rank = jnp.sum(onehot * (running - 1), axis=1)
    local_count = jnp.cumsum(onehot.reshape(-1, slots, prompts), axis=1).reshape(-1, prompts)
    local_rank = jnp.sum(onehot * (local_count - 1), axis=1)
    return (global_rank, local_rank)


def pack_groups(matrices, groups):
    rows = matrices[0].shape[0]
    pieces = [
        jnp.transpose(
            matrix.astype(jnp.bfloat16).reshape(rows, groups, matrix.shape[1] // groups), (1, 0, 2)
        )
        for matrix in matrices
    ]
    return jnp.concatenate(pieces, axis=2)


MESH = pl.DeviceIdType.MESH
VMEM_SPEC = pl.BlockSpec(memory_space=pltpu.VMEM)


def fan_out(step_count, make):
    copies = [make(step) for step in range(1, step_count)]
    for copy in copies:
        copy.start()
    return copies


def regroup_kernel(
    n_kv, n_blk, first_ref, second_ref, cache_ref, first_out, second_out, cache_out,
    first_in, second_in, cache_in, whole, stage_a, stage_b,
    first_send, first_recv, second_send, second_recv, cache_send, cache_recv, send, recv,
):
    me_kv, me = lax.axis_index("kv"), lax.axis_index("blk")
    rows = first_ref.shape[1]
    half, line, core = lax.div(me, 8), lax.rem(lax.div(me, 2), 4), lax.rem(me, 2)

    barrier = pltpu.get_barrier_semaphore()
    for axis, count, mine in (("kv", n_kv, me_kv), ("blk", n_blk, me)):
        for step in range(1, count):
            pl.semaphore_signal(
                barrier, inc=1, device_id={axis: lax.rem(mine + step, count)}, device_id_type=MESH
            )
    pl.semaphore_wait(barrier, n_kv + n_blk - 2)

    def swap(source, landing, sent, got):
        def make(step):
            peer = lax.rem(me_kv + step, n_kv)
            return pltpu.make_async_remote_copy(
                src_ref=source.at[peer],
                dst_ref=landing.at[me_kv],
                send_sem=sent.at[step - 1],
                recv_sem=got.at[step - 1],
                device_id={"kv": peer},
                device_id_type=MESH,
            )

        return fan_out(n_kv, make)

    def deal(step):
        peer = lax.rem(me + step, n_blk)
        return pltpu.make_async_remote_copy(
            src_ref=cache_ref.at[peer],
            dst_ref=cache_in.at[step - 1],
            send_sem=cache_send.at[step - 1],
            recv_sem=cache_recv.at[step - 1],
            device_id={"blk": peer},
            device_id_type=MESH,
        )

    firsts = swap(first_ref, first_in, first_send, first_recv)
    first_in[me_kv] = first_ref[me_kv]
    for copy in firsts:
        copy.wait_recv()
    for group in range(n_kv):
        stage_a[group * rows : (group + 1) * rows, :] = first_in[group].astype(jnp.float32)
    whole[0] = stage_a[...].astype(jnp.bfloat16)

    passed = {}

    def pass_on(held, peer, slot):
        copy = pltpu.make_async_remote_copy(
            src_ref=whole.at[held],
            dst_ref=whole.at[slot],
            send_sem=send.at[slot - 1],
            recv_sem=recv.at[slot - 1],
            device_id={"blk": peer},
            device_id_type=MESH,
        )
        copy.start()
        passed[slot] = copy

    def along(step):
        return half * 8 + lax.rem(line + step, 4) * 2 + core

    across = lax.rem(me + 8, n_blk)
    sibling = me + 1 - 2 * core
    pass_on(0, across, 8)
    for step in (1, 3, 2):
        pass_on(0, along(step), 2 * step)
    pass_on(0, sibling, 1)
    seconds = swap(second_ref, second_in, second_send, second_recv)
    passed[8].wait_recv()
    for step in (1, 3, 2):
        pass_on(8, along(step), 8 + 2 * step)
    pass_on(8, sibling, 9)
    deals = fan_out(n_blk, deal)

    for base in (0, 8):
        for step in (1, 3, 2):
            slot = base + 2 * step
            passed[slot].wait_recv()
            pass_on(slot, sibling, slot + 1)
    second_in[me_kv] = second_ref[me_kv]
    for copy in seconds:
        copy.wait_recv()
    for group in range(n_kv):
        stage_b[group * rows : (group + 1) * rows, :] = second_in[group].astype(jnp.float32)
    second_out[...] = stage_b[...].astype(jnp.bfloat16)
    for base in (0, 8):
        for step in range(4):
            for other in range(2):
                slot = base + 2 * step + other
                if other:
                    passed[slot].wait_recv()
                owner = (
                    lax.rem(half + base // 8, 2) * 8
                    + lax.rem(line + 4 - step, 4) * 2
                    + lax.rem(core + other, 2)
                )
                first_out[owner] = whole[slot]
    cache_out[me] = cache_ref[me]
    for step in range(1, n_blk):
        deals[step - 1].wait_recv()
        cache_out[lax.rem(me + n_blk - step, n_blk)] = cache_in[step - 1]
    for copy in firsts + seconds + deals + list(passed.values()):
        copy.wait_send()


def regroup(n_kv, n_blk, first, second, cached):
    rows = first.shape[1]
    tall = n_kv * rows
    first_width, second_width = first.shape[2], second.shape[2]
    half = jnp.bfloat16
    dma = pltpu.SemaphoreType.DMA
    return pl.pallas_call(
        functools.partial(regroup_kernel, n_kv, n_blk),
        name="regroup",
        out_shape=(
            jax.ShapeDtypeStruct((n_blk, tall, first_width), half),
            jax.ShapeDtypeStruct((tall, second_width), half),
            jax.ShapeDtypeStruct(cached.shape, half),
        ),
        in_specs=[VMEM_SPEC] * 3,
        out_specs=(VMEM_SPEC,) * 3,
        scratch_shapes=[
            pltpu.VMEM(first.shape, half),
            pltpu.VMEM(second.shape, half),
            pltpu.VMEM((n_blk - 1,) + cached.shape[1:], half),
            pltpu.VMEM((n_blk, tall, first_width), half),
            pltpu.VMEM((tall, first_width), jnp.float32),
            pltpu.VMEM((tall, second_width), jnp.float32),
        ]
        + [dma((n_kv - 1,))] * 4
        + [dma((n_blk - 1,))] * 4,
        compiler_params=pltpu.CompilerParams(collective_id=2, has_side_effects=True),
    )(first, second, cached)


LIFT = 1.0 / math.sqrt(HD) * math.log2(math.e)


def attention_kernel(
    scalars, query_ref, own_key_ref, own_value_ref, blocks_ref, out_ref,
    keys, values, score_a, score_b, row_max, summed,
):
    slots, block = blocks_ref.shape[0], blocks_ref.shape[3]
    rows = query_ref.shape[2]
    depth = keys.shape[1]
    wide = values.shape[0]
    chunk = rows
    per_chunk = chunk // block
    chunks = slots // per_chunk
    before, live_rows = scalars[2 * slots], scalars[2 * slots + 1]

    def padded_key(part, limit):
        spots = lax.broadcasted_iota(jnp.int32, (depth - HD, block), 1)
        lines = lax.broadcasted_iota(jnp.int32, (depth - HD, block), 0)
        bias = jnp.where((lines == 0) & (spots >= limit), FLOOR_SCORE, 0.0)
        return jnp.concatenate([part.astype(jnp.float32), bias], axis=0).T.astype(jnp.bfloat16)

    @pl.when(pl.program_id(0) == 0)
    def _():
        ones = jnp.ones((wide - HD, block), jnp.bfloat16)

        def place(slot, carry):
            limit = jnp.where(
                scalars[slots + slot] > 0, before - scalars[slot] * block, 0
            )
            spot = pl.multiple_of(slot * block, block)
            keys[pl.ds(spot, block), :] = padded_key(blocks_ref[slot, 0], limit)
            values[:, pl.ds(spot, block)] = jnp.concatenate([blocks_ref[slot, 1], ones], axis=0)
            return carry

        lax.fori_loop(0, slots, place, 0)
        for part in range(rows // block):
            near = slice(part * block, (part + 1) * block)
            far = slice(slots * block + part * block, slots * block + (part + 1) * block)
            keys[far, :] = padded_key(own_key_ref[:, near], live_rows - part * block)
            values[:, far] = jnp.concatenate([own_value_ref[:, near], ones], axis=0)

    query = jnp.concatenate(
        [
            query_ref[0].astype(jnp.float32),
            jnp.ones((16, rows), jnp.float32),
            jnp.zeros((depth - HD - 16, rows), jnp.float32),
        ],
        axis=0,
    ).astype(jnp.bfloat16)

    def score(index, into):
        spot = pl.multiple_of(index * chunk, chunk)
        into[...] = jnp.dot(keys[pl.ds(spot, chunk), :], query, preferred_element_type=jnp.float32)

    def window(index, into):
        near = before + rows - WINDOW
        needed = False
        for part in range(per_chunk):
            needed |= scalars[index * per_chunk + part] * block < near

        @pl.when(needed)
        def _():
            for part in range(per_chunk):
                lines = slice(part * block, (part + 1) * block)
                place = scalars[index * per_chunk + part] * block + lax.broadcasted_iota(
                    jnp.int32, (block, rows), 0
                )
                away = before - place + lax.broadcasted_iota(jnp.int32, (block, rows), 1)
                seen = (away < WINDOW) | (place < SINKS)
                into[lines, :] = jnp.where(seen, into[lines, :], FLOOR_SCORE)

    def absorb(index, held):
        spot = pl.multiple_of(index * chunk, chunk)
        now = held[...]
        largest = jnp.maximum(row_max[...], jnp.max(now, axis=0, keepdims=True))
        fade = jnp.exp2((row_max[...] - largest) * LIFT)
        weights = jnp.exp2((now - largest) * LIFT).astype(jnp.bfloat16)
        row_max[...] = largest
        summed[...] = summed[...] * fade + jnp.dot(
            values[:, pl.ds(spot, chunk)], weights, preferred_element_type=jnp.float32
        )

    score(chunks, score_b)
    causal = lax.broadcasted_iota(jnp.int32, (rows, rows), 0) <= lax.broadcasted_iota(
        jnp.int32, (rows, rows), 1
    )
    score_b[...] = jnp.where(causal, score_b[...], FLOOR_SCORE)
    row_max[...] = jnp.full_like(row_max, FLOOR_SCORE)
    summed[...] = jnp.zeros_like(summed)
    score(0, score_a)
    absorb(chunks, score_b)
    window(0, score_a)

    def pair(step, carry):
        first = step * 2
        score(first + 1, score_b)
        absorb(first, score_a)
        window(first + 1, score_b)
        later = lax.rem(first + 2, chunks)
        score(later, score_a)
        absorb(first + 1, score_b)
        window(later, score_a)
        return carry

    lax.fori_loop(0, chunks // 2, pair, 0)
    out_ref[0] = (summed[:HD, :] / summed[HD : HD + 1, :]).astype(jnp.bfloat16)


def attend(scalars, query, own_key, own_value, blocks):
    heads, width, rows = query.shape
    slots, block = blocks.shape[0], blocks.shape[3]
    span = slots * block + rows
    whole = pl.BlockSpec(memory_space=pltpu.VMEM)
    return pl.pallas_call(
        attention_kernel,
        name="attend",
        grid=(heads,),
        out_shape=jax.ShapeDtypeStruct((heads, width, rows), jnp.bfloat16),
        in_specs=[
            pl.BlockSpec(memory_space=pltpu.SMEM),
            pl.BlockSpec((1, width, rows), lambda head: (head, 0, 0)),
            whole,
            whole,
            whole,
        ],
        out_specs=pl.BlockSpec((1, width, rows), lambda head: (head, 0, 0)),
        scratch_shapes=[
            pltpu.VMEM((span, 128), jnp.bfloat16),
            pltpu.VMEM((96, span), jnp.bfloat16),
            pltpu.VMEM((rows, rows), jnp.float32),
            pltpu.VMEM((rows, rows), jnp.float32),
            pltpu.VMEM((1, rows), jnp.float32),
            pltpu.VMEM((96, rows), jnp.float32),
        ],
        cost_estimate=pl.CostEstimate(
            flops=4 * heads * rows * span * 128,
            bytes_accessed=span * 4 * width,
            transcendentals=heads * rows * span,
        ),
    )(scalars, query, own_key, own_value, blocks)


def greet(n, me):
    barrier = pltpu.get_barrier_semaphore()
    for step in range(1, n):
        peer = lax.rem(me + step, n)
        pl.semaphore_signal(barrier, inc=1, device_id={"kv": peer}, device_id_type=MESH)
    pl.semaphore_wait(barrier, n - 1)


def exchange(n, me, piece_ref, landed, send_sem, recv_sem):
    copies = []
    for step in range(1, n):
        peer = lax.rem(me + step, n)
        copy = pltpu.make_async_remote_copy(
            src_ref=piece_ref.at[peer],
            dst_ref=landed.at[step - 1],
            send_sem=send_sem.at[step - 1],
            recv_sem=recv_sem.at[step - 1],
            device_id={"kv": peer},
            device_id_type=MESH,
        )
        copy.start()
        copies.append(copy)
    return copies


def middle_kernel(
    n, piece_ref, token_ref, gain_ref, middle_ref, normed_ref, landed, total, whole,
    send_sem, recv_sem, share_sem, join_sem,
):
    me = lax.axis_index("kv")
    rows = piece_ref.shape[1]
    greet(n, me)
    copies = exchange(n, me, piece_ref, landed, send_sem, recv_sem)
    own = pl.ds(pl.multiple_of(me * rows, rows), rows)
    total[...] = token_ref[own, :].astype(jnp.float32) + piece_ref[me].astype(jnp.float32)
    for step in range(1, n):
        copies[step - 1].wait_recv()
        total[...] += landed[step - 1].astype(jnp.float32)
    whole[0] = total[...].astype(jnp.bfloat16)
    shares = []
    for step in range(1, n):
        peer = lax.rem(me + step, n)
        share = pltpu.make_async_remote_copy(
            src_ref=whole.at[0],
            dst_ref=whole.at[step],
            send_sem=share_sem.at[step - 1],
            recv_sem=join_sem.at[step - 1],
            device_id={"kv": peer},
            device_id_type=MESH,
        )
        share.start()
        shares.append(share)
    for step in range(n):
        if step:
            shares[step - 1].wait_recv()
        owner = lax.rem(me + n - step, n)
        place = pl.ds(pl.multiple_of(owner * rows, rows), rows)
        middle_rows = whole[step]
        middle_ref[place, :] = middle_rows
        values = middle_rows.astype(jnp.float32)
        mean_square = jnp.mean(values * values, axis=-1, keepdims=True)
        normed_ref[place, :] = (
            values * lax.rsqrt(mean_square + EPSILON) * gain_ref[...]
        ).astype(jnp.bfloat16)
    for copy in copies + shares:
        copy.wait_send()


def sum_middle(n, partial_out, tokens, mlp_gain):
    rows, width = tokens.shape
    piece = rows // n
    whole_shape = jax.ShapeDtypeStruct((rows, width), jnp.bfloat16)
    return pl.pallas_call(
        functools.partial(middle_kernel, n),
        name="sum_middle",
        cost_estimate=pl.CostEstimate(flops=0, bytes_accessed=200_000_000, transcendentals=0),
        out_shape=(whole_shape, whole_shape),
        in_specs=[VMEM_SPEC] * 3,
        out_specs=(VMEM_SPEC, VMEM_SPEC),
        scratch_shapes=[
            pltpu.VMEM((n - 1, piece, width), jnp.bfloat16),
            pltpu.VMEM((piece, width), jnp.float32),
            pltpu.VMEM((n, piece, width), jnp.bfloat16),
        ]
        + [pltpu.SemaphoreType.DMA((n - 1,))] * 4,
        compiler_params=pltpu.CompilerParams(collective_id=0, has_side_effects=True),
    )(partial_out.reshape(n, piece, width), tokens, mlp_gain.reshape(1, width))


def hidden_kernel(
    n, normed_ref, middle_hbm, pair_hbm, down_hbm, out_ref, pair, down, hidden, terms, landed,
    window, turned, pair_sem, down_sem, window_sem, send_sem, recv_sem,
):
    me = lax.axis_index("kv")
    rows, width = normed_ref.shape
    halves, part = terms.shape[0], terms.shape[2]
    piece = width // n
    tiles = pair.shape[1] // 256
    units = down.shape[0]
    barrier = pltpu.get_barrier_semaphore()
    for step in range(1, n):
        peer = lax.rem(me + step, n)
        pl.semaphore_signal(barrier, inc=1, device_id={"kv": peer}, device_id_type=MESH)

    def bring(tile):
        lanes = pl.ds(pl.multiple_of(tile * 256, 256), 256)
        return pltpu.make_async_copy(pair_hbm.at[:, lanes], pair.at[:, lanes], pair_sem.at[tile])

    for tile in range(tiles):
        bring(tile).start()
    fetch = pltpu.make_async_copy(down_hbm, down, down_sem)
    fetch.start()
    left = lax.div(me * piece, 128) * 128
    view = pltpu.make_async_copy(
        middle_hbm.at[:, pl.ds(pl.multiple_of(left, 128), window.shape[1])], window, window_sem
    )
    view.start()

    copies = []
    for half in range(halves):
        lines = slice(half * part, (half + 1) * part)

        @pl.loop(0, tiles)
        def _(tile):
            if half == 0:
                bring(tile).wait()
            lanes = pl.ds(pl.multiple_of(tile * 256, 256), 256)
            both = jnp.dot(normed_ref[lines, :], pair[:, lanes], preferred_element_type=jnp.float32)
            gate, up = both[:, :128], both[:, 128:]
            hidden[:, pl.ds(pl.multiple_of(tile * 128, 128), 128)] = (
                gate / (1.0 + jnp.exp(-gate)) * up
            ).astype(jnp.bfloat16)

        if half == 0:
            fetch.wait()

        @pl.loop(0, width // 512)
        def _(tile):
            spot = pl.ds(pl.multiple_of(tile * 512, 512), 512)
            term = jnp.dot(
                hidden[:, :units], down[:, spot], preferred_element_type=jnp.float32
            )
            terms[half, spot, :] = term.T.astype(jnp.bfloat16)

        if half == 0:
            pl.semaphore_wait(barrier, n - 1)
        for step in range(1, n):
            peer = lax.rem(me + step, n)
            copy = pltpu.make_async_remote_copy(
                src_ref=terms.at[half, pl.ds(pl.multiple_of(peer * piece, piece), piece)],
                dst_ref=landed.at[half, step - 1],
                send_sem=send_sem.at[half, step - 1],
                recv_sem=recv_sem.at[half, step - 1],
                device_id={"kv": peer},
                device_id_type=MESH,
            )
            copy.start()
            copies.append(copy)
    view.wait()
    turned[...] = window[...].astype(jnp.float32).T
    residual = pl.ds(pl.multiple_of(me * piece - left, 64), piece)
    for half in range(halves):
        lines = slice(half * part, (half + 1) * part)
        own = pl.ds(pl.multiple_of(me * piece, piece), piece)
        out_ref[:, lines] = turned[residual, lines] + terms[half, own, :].astype(jnp.float32)
        for step in range(1, n):
            copies[half * (n - 1) + step - 1].wait_recv()
            out_ref[:, lines] += landed[half, step - 1].astype(jnp.float32)
    for copy in copies:
        copy.wait_send()


def feed_forward(n, normed_mid, middle, w_pair, w_down):
    rows, width = normed_mid.shape
    halves = 2
    part = rows // halves
    piece = width // n
    half = jnp.bfloat16
    dma = pltpu.SemaphoreType.DMA
    any_spec = pl.BlockSpec(memory_space=pl.ANY)
    return pl.pallas_call(
        functools.partial(hidden_kernel, n),
        name="feed_forward",
        out_shape=jax.ShapeDtypeStruct((piece, rows), jnp.float32),
        in_specs=[VMEM_SPEC, any_spec, any_spec, any_spec],
        out_specs=VMEM_SPEC,
        scratch_shapes=[
            pltpu.VMEM(w_pair.shape, half),
            pltpu.VMEM(w_down.shape, half),
            pltpu.VMEM((part, w_pair.shape[1] // 2), half),
            pltpu.VMEM((halves, width, part), half),
            pltpu.VMEM((halves, n - 1, piece, part), half),
            pltpu.VMEM((rows, piece + 64), half),
            pltpu.VMEM((piece + 64, rows), jnp.float32),
            dma((w_pair.shape[1] // 256,)),
            dma,
            dma,
            dma((halves, n - 1)),
            dma((halves, n - 1)),
        ],
        compiler_params=pltpu.CompilerParams(
            collective_id=1, has_side_effects=True, vmem_limit_bytes=56 * 1024 * 1024
        ),
    )(normed_mid, middle, w_pair, w_down)


def pack_pairs(first, second, groups):
    rows, columns = first.shape
    units = columns // groups
    padded = -(-units // 128) * 128
    tiles = [
        jnp.pad(
            matrix.astype(jnp.bfloat16).reshape(rows, groups, units),
            ((0, 0), (0, 0), (0, padded - units)),
        ).reshape(rows, groups, -1, 1, 128)
        for matrix in (first, second)
    ]
    return jnp.transpose(jnp.concatenate(tiles, axis=3), (1, 0, 2, 3, 4)).reshape(groups, rows, -1)


def shards(
    tokens,
    attn_gain,
    mlp_gain,
    w_query,
    w_key,
    w_value,
    w_gate,
    w_up,
    w_out,
    w_down,
    cache,
    slot_prompt,
    prefix_len,
    new_len,
):
    groups = lax.axis_size("kv")
    n_blocks = lax.axis_size("blk")
    blk_index = lax.axis_index("blk")
    kv_index = lax.axis_index("kv")
    query_width = w_query.shape[1] // groups
    key_width = w_key.shape[1] // groups
    kv_local = key_width // HD
    new_rows = tokens.shape[0]
    prompts = prefix_len.shape[0]
    slots = cache.shape[1]
    prefix_here = prefix_len[blk_index]
    live_count = new_len[blk_index]
    row_ids = jnp.arange(new_rows, dtype=jnp.int32)
    positions = prefix_here + row_ids
    global_rank, local_rank = slot_ranks(slot_prompt, prompts, slots)
    own_prompts = lax.dynamic_slice_in_dim(slot_prompt, blk_index * slots, slots)
    own_ranks = lax.dynamic_slice_in_dim(local_rank, blk_index * slots, slots)
    placed = own_prompts * CAP + own_ranks
    buffer_ids = jnp.arange(prompts * CAP, dtype=jnp.int32)
    matches = placed[None, :] == buffer_ids[:, None]
    source_slot = jnp.sum(
        jnp.where(matches, jnp.arange(slots, dtype=jnp.int32)[None, :], 0), axis=1
    )
    by_slot = jnp.transpose(cache.reshape(2, slots, HD, BLOCK), (1, 0, 2, 3))
    outgoing = jnp.take(by_slot, source_slot, axis=0, mode="clip").reshape(prompts, CAP, 2, HD, BLOCK)
    w_first, w_second, arrived = regroup(
        groups,
        n_blocks,
        pack_groups((w_query, w_key, w_value), groups),
        pack_pairs(w_gate, w_up, groups),
        outgoing,
    )
    w_qkv = w_first.reshape(-1, w_first.shape[2])
    w_pair = lax.all_gather(w_second, "blk", axis=0, tiled=True)
    normed = rms_scale(tokens, attn_gain)
    projected = jnp.dot(normed, w_qkv, preferred_element_type=jnp.float32)
    queries = rotate(projected[:, :query_width].reshape(new_rows, -1, HD), positions).astype(
        jnp.bfloat16
    )
    key_new = rotate(
        projected[:, query_width : query_width + key_width].reshape(new_rows, kv_local, HD),
        positions,
    ).astype(jnp.bfloat16)
    value_new = (
        projected[:, query_width + key_width :].reshape(new_rows, kv_local, HD).astype(jnp.bfloat16)
    )
    slot_ids = jnp.arange(prompts * slots, dtype=jnp.int32)
    landing = slot_ids // slots * CAP + local_rank
    for_me = slot_prompt == blk_index
    received = (landing[None, :] == buffer_ids[:, None]) & for_me[None, :]
    block_number = jnp.sum(jnp.where(received, global_rank[None, :], 0), axis=1)
    block_live = jnp.any(received, axis=1)
    blocks = arrived.reshape(prompts * CAP, 2, HD, BLOCK)
    scalars = jnp.concatenate(
        [block_number, block_live.astype(jnp.int32), jnp.stack([prefix_here, live_count])]
    )
    attended = attend(
        scalars,
        jnp.transpose(queries, (1, 2, 0)),
        key_new.reshape(new_rows, HD).T,
        value_new.reshape(new_rows, HD).T,
        blocks,
    ).reshape(-1, new_rows)
    projected_out = lax.dot_general(
        attended, w_out, (((0,), (0,)), ((), ())), preferred_element_type=jnp.float32
    )
    partial_out = projected_out.astype(jnp.bfloat16)
    middle, normed_mid = sum_middle(groups, partial_out, tokens, mlp_gain)
    summed = feed_forward(groups, normed_mid, middle, w_pair, w_down).T
    mixed = jnp.where((row_ids < live_count)[:, None], summed, 0.0)
    return mixed.astype(jnp.bfloat16)


def solution(mesh):
    return jax.shard_map(
        shards,
        mesh=mesh,
        in_specs=(
            P("blk", None),
            P(),
            P(),
            P(("blk", "kv"), None),
            P(("blk", "kv"), None),
            P(("blk", "kv"), None),
            P(("blk", "kv"), None),
            P(("blk", "kv"), None),
            P("kv", None),
            P("kv", None),
            P(None, "blk", "kv", None, None),
            P(),
            P(),
            P(),
        ),
        out_specs=P("blk", "kv"),
        check_vma=False,
    )
```

```python
import functools
import math

import jax
import jax.numpy as jnp
from jax import lax
from jax.experimental import pallas as pl
from jax.experimental.pallas import tpu as pltpu
from jax.sharding import PartitionSpec as P

HEADS = 32
KV_HEADS = 8
HD = 80
WINDOW = 4096
SINKS = 4
BLOCK = 128
CAP = 2


FLOOR_SCORE = -1e30
EPSILON = 1e-05
ROPE_BASE = 10000.0


def rms_scale(row_data, gain_vec):
    values = row_data.astype(jnp.float32)
    mean_square = jnp.mean(values * values, axis=-1, keepdims=True)
    return (values * lax.rsqrt(mean_square + EPSILON) * gain_vec).astype(jnp.bfloat16)


def rotate(values, positions):
    head_width = values.shape[-1]
    half_width = head_width // 2
    frequency = ROPE_BASE ** (-2.0 * jnp.arange(half_width, dtype=jnp.float32) / head_width)
    angles = positions.astype(jnp.float32)[:, None] * frequency[None, :]
    cosine = jnp.cos(angles)[:, None, :]
    sine_wave = jnp.sin(angles)[:, None, :]
    first_half = values[..., :half_width]
    second_half = values[..., half_width:]
    return jnp.concatenate(
        [
            first_half * cosine - second_half * sine_wave,
            second_half * cosine + first_half * sine_wave,
        ],
        axis=-1,
    )


def slot_ranks(slot_prompt, prompts, slots):
    onehot = (slot_prompt[:, None] == jnp.arange(prompts, dtype=jnp.int32)[None, :]).astype(
        jnp.int32
    )
    running = jnp.cumsum(onehot, axis=0)
    global_rank = jnp.sum(onehot * (running - 1), axis=1)
    local_count = jnp.cumsum(onehot.reshape(-1, slots, prompts), axis=1).reshape(-1, prompts)
    local_rank = jnp.sum(onehot * (local_count - 1), axis=1)
    return (global_rank, local_rank)


def pack_groups(matrices, groups):
    rows = matrices[0].shape[0]
    pieces = [
        jnp.transpose(
            matrix.astype(jnp.bfloat16).reshape(rows, groups, matrix.shape[1] // groups), (1, 0, 2)
        )
        for matrix in matrices
    ]
    return jnp.concatenate(pieces, axis=2)


MESH = pl.DeviceIdType.MESH
VMEM_SPEC = pl.BlockSpec(memory_space=pltpu.VMEM)


def fan_out(step_count, make):
    copies = [make(step) for step in range(1, step_count)]
    for copy in copies:
        copy.start()
    return copies


def regroup_kernel(
    n_kv, n_blk, first_ref, second_ref, cache_ref, first_out, second_out, cache_out,
    first_in, second_in, cache_in, whole, stage_a, stage_b,
    first_send, first_recv, second_send, second_recv, cache_send, cache_recv, send, recv,
):
    me_kv, me = lax.axis_index("kv"), lax.axis_index("blk")
    rows = first_ref.shape[1]
    half, line, core = lax.div(me, 8), lax.rem(lax.div(me, 2), 4), lax.rem(me, 2)

    barrier = pltpu.get_barrier_semaphore()
    for axis, count, mine in (("kv", n_kv, me_kv), ("blk", n_blk, me)):
        for step in range(1, count):
            pl.semaphore_signal(
                barrier, inc=1, device_id={axis: lax.rem(mine + step, count)}, device_id_type=MESH
            )
    pl.semaphore_wait(barrier, n_kv + n_blk - 2)

    def swap(source, landing, sent, got):
        def make(step):
            peer = lax.rem(me_kv + step, n_kv)
            return pltpu.make_async_remote_copy(
                src_ref=source.at[peer],
                dst_ref=landing.at[me_kv],
                send_sem=sent.at[step - 1],
                recv_sem=got.at[step - 1],
                device_id={"kv": peer},
                device_id_type=MESH,
            )

        return fan_out(n_kv, make)

    def deal(step):
        peer = lax.rem(me + step, n_blk)
        return pltpu.make_async_remote_copy(
            src_ref=cache_ref.at[peer],
            dst_ref=cache_in.at[step - 1],
            send_sem=cache_send.at[step - 1],
            recv_sem=cache_recv.at[step - 1],
            device_id={"blk": peer},
            device_id_type=MESH,
        )

    firsts = swap(first_ref, first_in, first_send, first_recv)
    first_in[me_kv] = first_ref[me_kv]
    for copy in firsts:
        copy.wait_recv()
    for group in range(n_kv):
        stage_a[group * rows : (group + 1) * rows, :] = first_in[group].astype(jnp.float32)
    whole[0] = stage_a[...].astype(jnp.bfloat16)

    passed = {}

    def pass_on(held, peer, slot):
        copy = pltpu.make_async_remote_copy(
            src_ref=whole.at[held],
            dst_ref=whole.at[slot],
            send_sem=send.at[slot - 1],
            recv_sem=recv.at[slot - 1],
            device_id={"blk": peer},
            device_id_type=MESH,
        )
        copy.start()
        passed[slot] = copy

    def along(step):
        return half * 8 + lax.rem(line + step, 4) * 2 + core

    across = lax.rem(me + 8, n_blk)
    sibling = me + 1 - 2 * core
    pass_on(0, across, 8)
    for step in (1, 3, 2):
        pass_on(0, along(step), 2 * step)
    pass_on(0, sibling, 1)
    seconds = swap(second_ref, second_in, second_send, second_recv)
    passed[8].wait_recv()
    for step in (1, 3, 2):
        pass_on(8, along(step), 8 + 2 * step)
    pass_on(8, sibling, 9)
    deals = fan_out(n_blk, deal)

    for base in (0, 8):
        for step in (1, 3, 2):
            slot = base + 2 * step
            passed[slot].wait_recv()
            pass_on(slot, sibling, slot + 1)
    second_in[me_kv] = second_ref[me_kv]
    for copy in seconds:
        copy.wait_recv()
    for group in range(n_kv):
        stage_b[group * rows : (group + 1) * rows, :] = second_in[group].astype(jnp.float32)
    second_out[...] = stage_b[...].astype(jnp.bfloat16)
    for base in (0, 8):
        for step in range(4):
            for other in range(2):
                slot = base + 2 * step + other
                if other:
                    passed[slot].wait_recv()
                owner = (
                    lax.rem(half + base // 8, 2) * 8
                    + lax.rem(line + 4 - step, 4) * 2
                    + lax.rem(core + other, 2)
                )
                first_out[owner] = whole[slot]
    cache_out[me] = cache_ref[me]
    for step in range(1, n_blk):
        deals[step - 1].wait_recv()
        cache_out[lax.rem(me + n_blk - step, n_blk)] = cache_in[step - 1]
    for copy in firsts + seconds + deals + list(passed.values()):
        copy.wait_send()


def regroup(n_kv, n_blk, first, second, cached):
    rows = first.shape[1]
    tall = n_kv * rows
    first_width, second_width = first.shape[2], second.shape[2]
    half = jnp.bfloat16
    dma = pltpu.SemaphoreType.DMA
    return pl.pallas_call(
        functools.partial(regroup_kernel, n_kv, n_blk),
        name="regroup",
        out_shape=(
            jax.ShapeDtypeStruct((n_blk, tall, first_width), half),
            jax.ShapeDtypeStruct((tall, second_width), half),
            jax.ShapeDtypeStruct(cached.shape, half),
        ),
        in_specs=[VMEM_SPEC] * 3,
        out_specs=(VMEM_SPEC,) * 3,
        scratch_shapes=[
            pltpu.VMEM(first.shape, half),
            pltpu.VMEM(second.shape, half),
            pltpu.VMEM((n_blk - 1,) + cached.shape[1:], half),
            pltpu.VMEM((n_blk, tall, first_width), half),
            pltpu.VMEM((tall, first_width), jnp.float32),
            pltpu.VMEM((tall, second_width), jnp.float32),
        ]
        + [dma((n_kv - 1,))] * 4
        + [dma((n_blk - 1,))] * 4,
        compiler_params=pltpu.CompilerParams(collective_id=2, has_side_effects=True),
    )(first, second, cached)


LIFT = 1.0 / math.sqrt(HD) * math.log2(math.e)


def attention_kernel(
    scalars, query_ref, own_key_ref, own_value_ref, blocks_ref, out_ref,
    keys, values, score_a, score_b, row_max, summed,
):
    slots, block = blocks_ref.shape[0], blocks_ref.shape[3]
    rows = query_ref.shape[2]
    depth = keys.shape[1]
    wide = values.shape[0]
    chunk = rows
    per_chunk = chunk // block
    chunks = slots // per_chunk
    before, live_rows = scalars[2 * slots], scalars[2 * slots + 1]

    def padded_key(part, limit):
        spots = lax.broadcasted_iota(jnp.int32, (depth - HD, block), 1)
        lines = lax.broadcasted_iota(jnp.int32, (depth - HD, block), 0)
        bias = jnp.where((lines == 0) & (spots >= limit), FLOOR_SCORE, 0.0)
        return jnp.concatenate([part.astype(jnp.float32), bias], axis=0).T.astype(jnp.bfloat16)

    @pl.when(pl.program_id(0) == 0)
    def _():
        ones = jnp.ones((wide - HD, block), jnp.bfloat16)

        def place(slot, carry):
            limit = jnp.where(
                scalars[slots + slot] > 0, before - scalars[slot] * block, 0
            )
            spot = pl.multiple_of(slot * block, block)
            keys[pl.ds(spot, block), :] = padded_key(blocks_ref[slot, 0], limit)
            values[:, pl.ds(spot, block)] = jnp.concatenate([blocks_ref[slot, 1], ones], axis=0)
            return carry

        lax.fori_loop(0, slots, place, 0)
        for part in range(rows // block):
            near = slice(part * block, (part + 1) * block)
            far = slice(slots * block + part * block, slots * block + (part + 1) * block)
            keys[far, :] = padded_key(own_key_ref[:, near], live_rows - part * block)
            values[:, far] = jnp.concatenate([own_value_ref[:, near], ones], axis=0)

    query = jnp.concatenate(
        [
            query_ref[0].astype(jnp.float32),
            jnp.ones((16, rows), jnp.float32),
            jnp.zeros((depth - HD - 16, rows), jnp.float32),
        ],
        axis=0,
    ).astype(jnp.bfloat16)

    def score(index, into):
        spot = pl.multiple_of(index * chunk, chunk)
        into[...] = jnp.dot(keys[pl.ds(spot, chunk), :], query, preferred_element_type=jnp.float32)

    def window(index, into):
        near = before + rows - WINDOW
        needed = False
        for part in range(per_chunk):
            needed |= scalars[index * per_chunk + part] * block < near

        @pl.when(needed)
        def _():
            for part in range(per_chunk):
                lines = slice(part * block, (part + 1) * block)
                place = scalars[index * per_chunk + part] * block + lax.broadcasted_iota(
                    jnp.int32, (block, rows), 0
                )
                away = before - place + lax.broadcasted_iota(jnp.int32, (block, rows), 1)
                seen = (away < WINDOW) | (place < SINKS)
                into[lines, :] = jnp.where(seen, into[lines, :], FLOOR_SCORE)

    def absorb(index, held):
        spot = pl.multiple_of(index * chunk, chunk)
        now = held[...]
        largest = jnp.maximum(row_max[...], jnp.max(now, axis=0, keepdims=True))
        fade = jnp.exp2((row_max[...] - largest) * LIFT)
        weights = jnp.exp2((now - largest) * LIFT).astype(jnp.bfloat16)
        row_max[...] = largest
        summed[...] = summed[...] * fade + jnp.dot(
            values[:, pl.ds(spot, chunk)], weights, preferred_element_type=jnp.float32
        )

    score(chunks, score_b)
    causal = lax.broadcasted_iota(jnp.int32, (rows, rows), 0) <= lax.broadcasted_iota(
        jnp.int32, (rows, rows), 1
    )
    score_b[...] = jnp.where(causal, score_b[...], FLOOR_SCORE)
    row_max[...] = jnp.full_like(row_max, FLOOR_SCORE)
    summed[...] = jnp.zeros_like(summed)
    score(0, score_a)
    absorb(chunks, score_b)
    window(0, score_a)

    def pair(step, carry):
        first = step * 2
        score(first + 1, score_b)
        absorb(first, score_a)
        window(first + 1, score_b)
        later = lax.rem(first + 2, chunks)
        score(later, score_a)
        absorb(first + 1, score_b)
        window(later, score_a)
        return carry

    lax.fori_loop(0, chunks // 2, pair, 0)
    out_ref[0] = (summed[:HD, :] / summed[HD : HD + 1, :]).astype(jnp.bfloat16)


def attend(scalars, query, own_key, own_value, blocks):
    heads, width, rows = query.shape
    slots, block = blocks.shape[0], blocks.shape[3]
    span = slots * block + rows
    whole = pl.BlockSpec(memory_space=pltpu.VMEM)
    return pl.pallas_call(
        attention_kernel,
        name="attend",
        grid=(heads,),
        out_shape=jax.ShapeDtypeStruct((heads, width, rows), jnp.bfloat16),
        in_specs=[
            pl.BlockSpec(memory_space=pltpu.SMEM),
            pl.BlockSpec((1, width, rows), lambda head: (head, 0, 0)),
            whole,
            whole,
            whole,
        ],
        out_specs=pl.BlockSpec((1, width, rows), lambda head: (head, 0, 0)),
        scratch_shapes=[
            pltpu.VMEM((span, 128), jnp.bfloat16),
            pltpu.VMEM((96, span), jnp.bfloat16),
            pltpu.VMEM((rows, rows), jnp.float32),
            pltpu.VMEM((rows, rows), jnp.float32),
            pltpu.VMEM((1, rows), jnp.float32),
            pltpu.VMEM((96, rows), jnp.float32),
        ],
        cost_estimate=pl.CostEstimate(
            flops=4 * heads * rows * span * 128,
            bytes_accessed=span * 4 * width,
            transcendentals=heads * rows * span,
        ),
    )(scalars, query, own_key, own_value, blocks)


def hail(n, me):
    barrier = pltpu.get_barrier_semaphore()
    for step in range(1, n):
        peer = lax.rem(me + step, n)
        pl.semaphore_signal(barrier, inc=1, device_id={"kv": peer}, device_id_type=MESH)
    return barrier


class Links:
    def __init__(self, send, recv):
        self.send, self.recv, self.started = send, recv, []

    def go(self, source, target, peer, index):
        copy = pltpu.make_async_remote_copy(
            src_ref=source,
            dst_ref=target,
            send_sem=self.send.at[index],
            recv_sem=self.recv.at[index],
            device_id={"kv": peer},
            device_id_type=MESH,
        )
        copy.start()
        self.started.append(copy)
        return copy

    def close(self):
        for copy in self.started:
            copy.wait_send()


def z_steps(lines):
    return sorted(range(1, lines), key=lambda step: min(step, lines - step))


def as_float(ref):
    return ref[...].astype(jnp.float32)


class Scatter(Links):
    def __init__(self, n, me, view, landings, send, recv):
        super().__init__(send, recv)
        self.land_a, self.land_b, self.stage_a, self.stage_b, self.got_a, self.got_b = landings
        self.lines, self.me, self.view = n // 2, me, view
        self.z, self.y = lax.div(me, 2), lax.rem(me, 2)
        self.partner = 2 * self.z + 1 - self.y
        self.steps = z_steps(self.lines)

    def line(self, step):
        return 2 * lax.rem(self.z + step, self.lines)

    def open(self):
        lines = self.lines
        self.along = [
            self.go(
                self.view(self.line(step) + side, 0),
                self.land_a.at[step - 1, side],
                self.line(step) + self.y,
                2 * (step - 1) + side,
            )
            for step in self.steps
            for side in range(2)
        ]
        self.across = {
            step: self.go(
                self.view(self.line(step) + 1 - self.y, 1),
                self.land_b.at[step],
                self.partner,
                2 * (lines - 1) + step,
            )
            for step in self.steps + [0]
        }

    def forward(self):
        lines = self.lines
        self.last_b = []
        for step in self.steps:
            self.across[step].wait_recv()
            self.stage_b[step - 1] = (
                as_float(self.view(self.line(step) + self.y, 1)) + as_float(self.land_b.at[step])
            ).astype(jnp.bfloat16)
            self.last_b.append(
                self.go(
                    self.stage_b.at[step - 1],
                    self.got_b.at[step - 1],
                    self.line(step) + self.y,
                    3 * lines - 2 + step - 1,
                )
            )
        for copy in self.along:
            copy.wait_recv()
        self.stage_a[...] = self.gathered(1 - self.y).astype(jnp.bfloat16)
        self.last_a = self.go(self.stage_a, self.got_a, self.partner, 4 * lines - 3)

    def gathered(self, side):
        total = as_float(self.view(2 * self.z + side, 0))
        for step in range(self.lines - 1):
            total += as_float(self.land_a.at[step, side])
        return total

    def finish_a(self):
        self.last_a.wait_recv()
        return self.gathered(self.y) + as_float(self.got_a)

    def finish_b(self):
        self.across[0].wait_recv()
        total = as_float(self.view(self.me, 1)) + as_float(self.land_b.at[0])
        for copy in self.last_b:
            copy.wait_recv()
        for step in range(self.lines - 1):
            total += as_float(self.got_b.at[step])
        return total


def scatter_scratch(n, shape, copies=1):
    lines = n // 2
    sizes = [(lines - 1, 2), (lines,), (), (lines - 1,), (), (lines - 1,)]
    lead = () if copies == 1 else (copies,)
    return [pltpu.VMEM(lead + size + shape, jnp.bfloat16) for size in sizes] + [
        pltpu.SemaphoreType.DMA(lead + (4 * lines - 2,))
    ] * 2


def middle_kernel(
    n, piece_ref, token_ref, gain_ref, middle_ref, normed_ref,
    land_a, land_b, stage_a, stage_b, got_a, got_b, send, recv, whole, share, join,
):
    me = lax.axis_index("kv")
    part = piece_ref.shape[2]
    lines = n // 2
    barrier = hail(n, me)
    terms = Scatter(
        n, me, lambda k, h: piece_ref.at[k, h],
        (land_a, land_b, stage_a, stage_b, got_a, got_b), send, recv,
    )
    links = Links(share, join)
    pl.semaphore_wait(barrier, n - 1)
    terms.open()
    terms.forward()

    def rows_of(step, side, half):
        owner = 2 * lax.rem(terms.z + lines - step, lines) + lax.rem(terms.y + side, 2)
        return pl.ds(pl.multiple_of((owner * 2 + half) * part, part), part)

    def index_of(step, side, half):
        return (step * 2 + side) * 2 + half - 2

    came = {}

    def spread(held, slot, peer):
        came[slot] = links.go(whole.at[held], whole.at[slot], peer, index_of(*slot))

    def settle(slot):
        place = rows_of(*slot)
        middle_rows = whole[slot]
        middle_ref[place, :] = middle_rows
        values = middle_rows.astype(jnp.float32)
        mean_square = jnp.mean(values * values, axis=-1, keepdims=True)
        normed_ref[place, :] = (
            values * lax.rsqrt(mean_square + EPSILON) * gain_ref[...]
        ).astype(jnp.bfloat16)

    def peer_at(step):
        return terms.line(step) + terms.y

    own_a = token_ref[rows_of(0, 0, 0), :].astype(jnp.float32)
    whole[0, 0, 0] = (own_a + terms.finish_a()).astype(jnp.bfloat16)
    for step in terms.steps:
        spread((0, 0, 0), (step, 0, 0), peer_at(step))
    spread((0, 0, 0), (0, 1, 0), terms.partner)
    own_b = token_ref[rows_of(0, 0, 1), :].astype(jnp.float32)
    whole[0, 0, 1] = (own_b + terms.finish_b()).astype(jnp.bfloat16)
    spread((0, 0, 1), (0, 1, 1), terms.partner)
    for step in terms.steps:
        spread((0, 0, 1), (step, 0, 1), peer_at(step))
    settle((0, 0, 0))
    settle((0, 0, 1))
    for step in terms.steps:
        came[step, 0, 0].wait_recv()
        spread((step, 0, 0), (step, 1, 0), terms.partner)
        if step == terms.steps[0]:
            came[0, 1, 1].wait_recv()
            for far in terms.steps:
                spread((0, 1, 1), (far, 1, 1), peer_at(far))
    settle((0, 1, 1))
    for step in terms.steps:
        settle((step, 0, 0))
    came[0, 1, 0].wait_recv()
    settle((0, 1, 0))
    for step, side, half in (
        [(step, 0, 1) for step in terms.steps]
        + [(step, 1, 0) for step in terms.steps]
        + [(step, 1, 1) for step in terms.steps]
    ):
        came[step, side, half].wait_recv()
        settle((step, side, half))
    terms.close()
    links.close()


def sum_middle(n, partial_out, tokens, mlp_gain):
    rows, width = tokens.shape
    piece = rows // n
    whole_shape = jax.ShapeDtypeStruct((rows, width), jnp.bfloat16)
    return pl.pallas_call(
        functools.partial(middle_kernel, n),
        name="sum_middle",
        cost_estimate=pl.CostEstimate(flops=0, bytes_accessed=200_000_000, transcendentals=0),
        out_shape=(whole_shape, whole_shape),
        in_specs=[VMEM_SPEC] * 3,
        out_specs=(VMEM_SPEC, VMEM_SPEC),
        scratch_shapes=scatter_scratch(n, (piece // 2, width))
        + [pltpu.VMEM((n // 2, 2, 2, piece // 2, width), jnp.bfloat16)]
        + [pltpu.SemaphoreType.DMA((2 * n - 2,))] * 2,
        compiler_params=pltpu.CompilerParams(collective_id=0, has_side_effects=True),
    )(partial_out.reshape(n, 2, piece // 2, width), tokens, mlp_gain.reshape(1, width))


def hidden_kernel(
    n, normed_ref, middle_hbm, pair_hbm, down_hbm, out_ref, pair, down, hidden, terms,
    window, turned, pair_sem, down_sem, window_sem,
    land_a, land_b, stage_a, stage_b, got_a, got_b, send, recv,
):
    me = lax.axis_index("kv")
    rows, width = normed_ref.shape
    halves, part = terms.shape[0], terms.shape[2]
    piece = width // n
    tiles = pair.shape[1] // 256
    units = down.shape[0]
    barrier = hail(n, me)

    def bring(tile):
        lanes = pl.ds(pl.multiple_of(tile * 256, 256), 256)
        return pltpu.make_async_copy(pair_hbm.at[:, lanes], pair.at[:, lanes], pair_sem.at[tile])

    for tile in range(tiles):
        bring(tile).start()
    fetch = pltpu.make_async_copy(down_hbm, down, down_sem)
    fetch.start()
    left = lax.div(me * piece, 128) * 128
    view = pltpu.make_async_copy(
        middle_hbm.at[:, pl.ds(pl.multiple_of(left, 128), window.shape[1])], window, window_sem
    )
    view.start()

    def exchange(half):
        def term(owner, side):
            start = pl.multiple_of(owner * piece + side * (piece // 2), piece // 2)
            return terms.at[half, pl.ds(start, piece // 2)]

        landings = [ref.at[half] for ref in (land_a, land_b, stage_a, stage_b, got_a, got_b)]
        return Scatter(n, me, term, landings, send.at[half], recv.at[half])

    sums = [exchange(half) for half in range(halves)]
    for half in range(halves):
        lines = slice(half * part, (half + 1) * part)

        @pl.loop(0, tiles)
        def _(tile):
            if half == 0:
                bring(tile).wait()
            lanes = pl.ds(pl.multiple_of(tile * 256, 256), 256)
            both = jnp.dot(normed_ref[lines, :], pair[:, lanes], preferred_element_type=jnp.float32)
            gate, up = both[:, :128], both[:, 128:]
            hidden[:, pl.ds(pl.multiple_of(tile * 128, 128), 128)] = (
                gate / (1.0 + jnp.exp(-gate)) * up
            ).astype(jnp.bfloat16)

        if half == 0:
            fetch.wait()

        @pl.loop(0, width // 512)
        def _(tile):
            spot = pl.ds(pl.multiple_of(tile * 512, 512), 512)
            term = jnp.dot(
                hidden[:, :units], down[:, spot], preferred_element_type=jnp.float32
            )
            terms[half, spot, :] = term.T.astype(jnp.bfloat16)

        if half == 0:
            pl.semaphore_wait(barrier, n - 1)
        sums[half].open()
    view.wait()
    turned[...] = window[...].astype(jnp.float32).T
    for half in range(halves):
        sums[half].forward()
    shift = me * piece - left
    for half in range(halves):
        lines = slice(half * part, (half + 1) * part)
        for side, finish in enumerate((sums[half].finish_a, sums[half].finish_b)):
            residual = pl.ds(pl.multiple_of(shift + side * (piece // 2), 32), piece // 2)
            place = slice(side * (piece // 2), (side + 1) * (piece // 2))
            out_ref[place, lines] = turned[residual, lines] + finish()
    for half in range(halves):
        sums[half].close()


def feed_forward(n, normed_mid, middle, w_pair, w_down):
    rows, width = normed_mid.shape
    halves = 2
    part = rows // halves
    piece = width // n
    half = jnp.bfloat16
    dma = pltpu.SemaphoreType.DMA
    any_spec = pl.BlockSpec(memory_space=pl.ANY)
    return pl.pallas_call(
        functools.partial(hidden_kernel, n),
        name="feed_forward",
        out_shape=jax.ShapeDtypeStruct((piece, rows), jnp.float32),
        in_specs=[VMEM_SPEC, any_spec, any_spec, any_spec],
        out_specs=VMEM_SPEC,
        scratch_shapes=[
            pltpu.VMEM(w_pair.shape, half),
            pltpu.VMEM(w_down.shape, half),
            pltpu.VMEM((part, w_pair.shape[1] // 2), half),
            pltpu.VMEM((halves, width, part), half),
            pltpu.VMEM((rows, piece + 64), half),
            pltpu.VMEM((piece + 64, rows), jnp.float32),
            dma((w_pair.shape[1] // 256,)),
            dma,
            dma,
        ]
        + scatter_scratch(n, (piece // 2, part), halves),
        compiler_params=pltpu.CompilerParams(
            collective_id=1, has_side_effects=True, vmem_limit_bytes=56 * 1024 * 1024
        ),
    )(normed_mid, middle, w_pair, w_down)


def pack_pairs(first, second, groups):
    rows, columns = first.shape
    units = columns // groups
    padded = -(-units // 128) * 128
    tiles = [
        jnp.pad(
            matrix.astype(jnp.bfloat16).reshape(rows, groups, units),
            ((0, 0), (0, 0), (0, padded - units)),
        ).reshape(rows, groups, -1, 1, 128)
        for matrix in (first, second)
    ]
    return jnp.transpose(jnp.concatenate(tiles, axis=3), (1, 0, 2, 3, 4)).reshape(groups, rows, -1)


def shards(
    tokens,
    attn_gain,
    mlp_gain,
    w_query,
    w_key,
    w_value,
    w_gate,
    w_up,
    w_out,
    w_down,
    cache,
    slot_prompt,
    prefix_len,
    new_len,
):
    groups = lax.axis_size("kv")
    n_blocks = lax.axis_size("blk")
    blk_index = lax.axis_index("blk")
    kv_index = lax.axis_index("kv")
    query_width = w_query.shape[1] // groups
    key_width = w_key.shape[1] // groups
    kv_local = key_width // HD
    new_rows = tokens.shape[0]
    prompts = prefix_len.shape[0]
    slots = cache.shape[1]
    prefix_here = prefix_len[blk_index]
    live_count = new_len[blk_index]
    row_ids = jnp.arange(new_rows, dtype=jnp.int32)
    positions = prefix_here + row_ids
    global_rank, local_rank = slot_ranks(slot_prompt, prompts, slots)
    own_prompts = lax.dynamic_slice_in_dim(slot_prompt, blk_index * slots, slots)
    own_ranks = lax.dynamic_slice_in_dim(local_rank, blk_index * slots, slots)
    placed = own_prompts * CAP + own_ranks
    buffer_ids = jnp.arange(prompts * CAP, dtype=jnp.int32)
    matches = placed[None, :] == buffer_ids[:, None]
    source_slot = jnp.sum(
        jnp.where(matches, jnp.arange(slots, dtype=jnp.int32)[None, :], 0), axis=1
    )
    by_slot = jnp.transpose(cache.reshape(2, slots, HD, BLOCK), (1, 0, 2, 3))
    outgoing = jnp.take(by_slot, source_slot, axis=0, mode="clip").reshape(prompts, CAP, 2, HD, BLOCK)
    w_first, w_second, arrived = regroup(
        groups,
        n_blocks,
        pack_groups((w_query, w_key, w_value), groups),
        pack_pairs(w_gate, w_up, groups),
        outgoing,
    )
    w_qkv = w_first.reshape(-1, w_first.shape[2])
    w_pair = lax.all_gather(w_second, "blk", axis=0, tiled=True)
    normed = rms_scale(tokens, attn_gain)
    projected = jnp.dot(normed, w_qkv, preferred_element_type=jnp.float32)
    queries = rotate(projected[:, :query_width].reshape(new_rows, -1, HD), positions).astype(
        jnp.bfloat16
    )
    key_new = rotate(
        projected[:, query_width : query_width + key_width].reshape(new_rows, kv_local, HD),
        positions,
    ).astype(jnp.bfloat16)
    value_new = (
        projected[:, query_width + key_width :].reshape(new_rows, kv_local, HD).astype(jnp.bfloat16)
    )
    slot_ids = jnp.arange(prompts * slots, dtype=jnp.int32)
    landing = slot_ids // slots * CAP + local_rank
    for_me = slot_prompt == blk_index
    received = (landing[None, :] == buffer_ids[:, None]) & for_me[None, :]
    block_number = jnp.sum(jnp.where(received, global_rank[None, :], 0), axis=1)
    block_live = jnp.any(received, axis=1)
    blocks = arrived.reshape(prompts * CAP, 2, HD, BLOCK)
    scalars = jnp.concatenate(
        [block_number, block_live.astype(jnp.int32), jnp.stack([prefix_here, live_count])]
    )
    attended = attend(
        scalars,
        jnp.transpose(queries, (1, 2, 0)),
        key_new.reshape(new_rows, HD).T,
        value_new.reshape(new_rows, HD).T,
        blocks,
    ).reshape(-1, new_rows)
    projected_out = lax.dot_general(
        attended, w_out, (((0,), (0,)), ((), ())), preferred_element_type=jnp.float32
    )
    partial_out = projected_out.astype(jnp.bfloat16)
    middle, normed_mid = sum_middle(groups, partial_out, tokens, mlp_gain)
    summed = feed_forward(groups, normed_mid, middle, w_pair, w_down).T
    mixed = jnp.where((row_ids < live_count)[:, None], summed, 0.0)
    return mixed.astype(jnp.bfloat16)


def solution(mesh):
    return jax.shard_map(
        shards,
        mesh=mesh,
        in_specs=(
            P("blk", None),
            P(),
            P(),
            P(("blk", "kv"), None),
            P(("blk", "kv"), None),
            P(("blk", "kv"), None),
            P(("blk", "kv"), None),
            P(("blk", "kv"), None),
            P("kv", None),
            P("kv", None),
            P(None, "blk", "kv", None, None),
            P(),
            P(),
            P(),
        ),
        out_specs=P("blk", "kv"),
        check_vma=False,
    )
```

```python
import functools
import math

import jax
import jax.numpy as jnp
from jax import lax
from jax.experimental import pallas as pl
from jax.experimental.pallas import tpu as pltpu
from jax.sharding import PartitionSpec as P

HEADS = 32
KV_HEADS = 8
HD = 80
WINDOW = 4096
SINKS = 4
BLOCK = 128
CAP = 2


FLOOR_SCORE = -1e30
EPSILON = 1e-05
ROPE_BASE = 10000.0


def rms_scale(row_data, gain_vec):
    values = row_data.astype(jnp.float32)
    mean_square = jnp.mean(values * values, axis=-1, keepdims=True)
    return (values * lax.rsqrt(mean_square + EPSILON) * gain_vec).astype(jnp.bfloat16)


def rotate(values, positions):
    head_width = values.shape[-1]
    half_width = head_width // 2
    frequency = ROPE_BASE ** (-2.0 * jnp.arange(half_width, dtype=jnp.float32) / head_width)
    angles = positions.astype(jnp.float32)[:, None] * frequency[None, :]
    cosine = jnp.cos(angles)[:, None, :]
    sine_wave = jnp.sin(angles)[:, None, :]
    first_half = values[..., :half_width]
    second_half = values[..., half_width:]
    return jnp.concatenate(
        [
            first_half * cosine - second_half * sine_wave,
            second_half * cosine + first_half * sine_wave,
        ],
        axis=-1,
    )


def slot_ranks(slot_prompt, prompts, slots):
    onehot = (slot_prompt[:, None] == jnp.arange(prompts, dtype=jnp.int32)[None, :]).astype(
        jnp.int32
    )
    running = jnp.cumsum(onehot, axis=0)
    global_rank = jnp.sum(onehot * (running - 1), axis=1)
    local_count = jnp.cumsum(onehot.reshape(-1, slots, prompts), axis=1).reshape(-1, prompts)
    local_rank = jnp.sum(onehot * (local_count - 1), axis=1)
    return (global_rank, local_rank)


def pack_groups(matrices, groups):
    rows = matrices[0].shape[0]
    pieces = [
        jnp.transpose(
            matrix.astype(jnp.bfloat16).reshape(rows, groups, matrix.shape[1] // groups), (1, 0, 2)
        )
        for matrix in matrices
    ]
    return jnp.concatenate(pieces, axis=2)


MESH = pl.DeviceIdType.MESH
VMEM_SPEC = pl.BlockSpec(memory_space=pltpu.VMEM)


def fan_out(step_count, make):
    copies = [make(step) for step in range(1, step_count)]
    for copy in copies:
        copy.start()
    return copies


def regroup_kernel(
    n_kv, n_blk, first_ref, second_ref, cache_ref, extra_ref, token_ref, gain_ref,
    projected_ref, second_out, cache_out,
    first_in, second_in, cache_in, whole, extra, normed, weights, stage_a, stage_b,
    first_send, first_recv, second_send, second_recv, cache_send, cache_recv, send, recv,
    extra_send, extra_recv,
):
    me_kv, me = lax.axis_index("kv"), lax.axis_index("blk")
    rows = first_ref.shape[1]
    half, line, core = lax.div(me, 8), lax.rem(lax.div(me, 2), 4), lax.rem(me, 2)

    barrier = pltpu.get_barrier_semaphore()
    for axis, count, mine in (("kv", n_kv, me_kv), ("blk", n_blk, me)):
        for step in range(1, count):
            pl.semaphore_signal(
                barrier, inc=1, device_id={axis: lax.rem(mine + step, count)}, device_id_type=MESH
            )
    pl.semaphore_wait(barrier, n_kv + n_blk - 2)

    def swap(source, landing, sent, got):
        def make(step):
            peer = lax.rem(me_kv + step, n_kv)
            return pltpu.make_async_remote_copy(
                src_ref=source.at[peer],
                dst_ref=landing.at[me_kv],
                send_sem=sent.at[step - 1],
                recv_sem=got.at[step - 1],
                device_id={"kv": peer},
                device_id_type=MESH,
            )

        return fan_out(n_kv, make)

    def deal(step):
        peer = lax.rem(me + step, n_blk)
        return pltpu.make_async_remote_copy(
            src_ref=cache_ref.at[peer],
            dst_ref=cache_in.at[step - 1],
            send_sem=cache_send.at[step - 1],
            recv_sem=cache_recv.at[step - 1],
            device_id={"blk": peer},
            device_id_type=MESH,
        )

    firsts = swap(first_ref, first_in, first_send, first_recv)
    first_in[me_kv] = first_ref[me_kv]
    for copy in firsts:
        copy.wait_recv()
    for group in range(n_kv):
        stage_a[group * rows : (group + 1) * rows, :] = first_in[group].astype(jnp.float32)
    whole[0] = stage_a[...].astype(jnp.bfloat16)

    extra[0] = extra_ref[...]

    passed, passed_extra = {}, {}

    def pass_extra(held, peer, slot):
        copy = pltpu.make_async_remote_copy(
            src_ref=extra.at[held],
            dst_ref=extra.at[slot],
            send_sem=extra_send.at[slot - 1],
            recv_sem=extra_recv.at[slot - 1],
            device_id={"blk": peer},
            device_id_type=MESH,
        )
        copy.start()
        passed_extra[slot] = copy

    def pass_on(held, peer, slot):
        copy = pltpu.make_async_remote_copy(
            src_ref=whole.at[held],
            dst_ref=whole.at[slot],
            send_sem=send.at[slot - 1],
            recv_sem=recv.at[slot - 1],
            device_id={"blk": peer},
            device_id_type=MESH,
        )
        copy.start()
        passed[slot] = copy

    def along(step):
        return half * 8 + lax.rem(line + step, 4) * 2 + core

    across = lax.rem(me + 8, n_blk)
    sibling = me + 1 - 2 * core
    pass_on(0, across, 8)
    for step in (1, 3, 2):
        pass_on(0, along(step), 2 * step)
    pass_on(0, sibling, 1)
    seconds = swap(second_ref, second_in, second_send, second_recv)

    @pl.loop(0, token_ref.shape[0] // 64)
    def _(part):
        lines = pl.ds(pl.multiple_of(part * 64, 64), 64)
        values = token_ref[lines, :].astype(jnp.float32)
        mean_square = jnp.mean(values * values, axis=-1, keepdims=True)
        normed[lines, :] = (
            values * lax.rsqrt(mean_square + EPSILON) * gain_ref[...]
        ).astype(jnp.bfloat16)

    passed[8].wait_recv()
    for step in (1, 3, 2):
        pass_on(8, along(step), 8 + 2 * step)
    pass_on(8, sibling, 9)
    deals = fan_out(n_blk, deal)
    pass_extra(0, across, 8)
    for step in (1, 3, 2):
        pass_extra(0, along(step), 2 * step)
    pass_extra(0, sibling, 1)

    for base in (0, 8):
        for step in (1, 3, 2):
            slot = base + 2 * step
            passed[slot].wait_recv()
            pass_on(slot, sibling, slot + 1)
    second_in[me_kv] = second_ref[me_kv]
    for copy in seconds:
        copy.wait_recv()
    for group in range(n_kv):
        stage_b[group * rows : (group + 1) * rows, :] = second_in[group].astype(jnp.float32)
    second_out[...] = stage_b[...].astype(jnp.bfloat16)
    passed_extra[8].wait_recv()
    for step in (1, 3, 2):
        pass_extra(8, along(step), 8 + 2 * step)
    pass_extra(8, sibling, 9)

    def owner_of(base, step, other):
        return (
            lax.rem(half + base // 8, 2) * 8
            + lax.rem(line + 4 - step, 4) * 2
            + lax.rem(core + other, 2)
        )

    tall = whole.shape[1]
    for base in (0, 8):
        for step in range(4):
            for other in range(2):
                slot = base + 2 * step + other
                if other:
                    passed[slot].wait_recv()
                place = pl.multiple_of(owner_of(base, step, other) * tall, tall)
                weights[pl.ds(place, tall), :] = whole[slot]

    @pl.loop(0, normed.shape[0] // 128)
    def _(part):
        lines = pl.ds(pl.multiple_of(part * 128, 128), 128)
        projected_ref[lines, :] = jnp.dot(
            normed[lines, :], weights[...], preferred_element_type=jnp.float32
        )

    for base in (0, 8):
        for step in (1, 3, 2):
            slot = base + 2 * step
            passed_extra[slot].wait_recv()
            pass_extra(slot, sibling, slot + 1)
    for base in (0, 8):
        for step in range(4):
            for other in range(2):
                slot = base + 2 * step + other
                if other:
                    passed_extra[slot].wait_recv()
                cache_out[owner_of(base, step, other), 1] = extra[slot]
    cache_out[me, 0] = cache_ref[me]
    for step in range(1, n_blk):
        deals[step - 1].wait_recv()
        cache_out[lax.rem(me + n_blk - step, n_blk), 0] = cache_in[step - 1]
    for copy in firsts + seconds + deals + [*passed.values(), *passed_extra.values()]:
        copy.wait_send()


def regroup(n_kv, n_blk, first, second, cached, extra, tokens, gain):
    rows = first.shape[1]
    tall = n_kv * rows
    first_width, second_width = first.shape[2], second.shape[2]
    half = jnp.bfloat16
    dma = pltpu.SemaphoreType.DMA
    blocks = (n_blk, 2) + cached.shape[1:]
    return pl.pallas_call(
        functools.partial(regroup_kernel, n_kv, n_blk),
        name="regroup",
        out_shape=(
            jax.ShapeDtypeStruct((tokens.shape[0], first_width), jnp.float32),
            jax.ShapeDtypeStruct((tall, second_width), half),
            jax.ShapeDtypeStruct(blocks, half),
        ),
        in_specs=[VMEM_SPEC] * 6,
        out_specs=(VMEM_SPEC,) * 3,
        scratch_shapes=[
            pltpu.VMEM(first.shape, half),
            pltpu.VMEM(second.shape, half),
            pltpu.VMEM((n_blk - 1,) + cached.shape[1:], half),
            pltpu.VMEM((n_blk, tall, first_width), half),
            pltpu.VMEM((n_blk,) + extra.shape, half),
            pltpu.VMEM(tokens.shape, half),
            pltpu.VMEM((n_blk * tall, first_width), half),
            pltpu.VMEM((tall, first_width), jnp.float32),
            pltpu.VMEM((tall, second_width), jnp.float32),
        ]
        + [dma((n_kv - 1,))] * 4
        + [dma((n_blk - 1,))] * 6,
        compiler_params=pltpu.CompilerParams(collective_id=2, has_side_effects=True),
    )(first, second, cached, extra, tokens, gain.reshape(1, -1))


LIFT = 1.0 / math.sqrt(HD) * math.log2(math.e)


def attention_kernel(
    scalars, query_ref, own_key_ref, own_value_ref, blocks_ref, out_ref,
    keys, values, score_a, score_b, row_max, summed,
):
    slots, block = blocks_ref.shape[0], blocks_ref.shape[3]
    rows = query_ref.shape[2]
    depth = keys.shape[1]
    wide = values.shape[0]
    chunk = rows
    per_chunk = chunk // block
    chunks = slots // per_chunk
    before, live_rows = scalars[2 * slots], scalars[2 * slots + 1]

    def padded_key(part, limit):
        spots = lax.broadcasted_iota(jnp.int32, (depth - HD, block), 1)
        lines = lax.broadcasted_iota(jnp.int32, (depth - HD, block), 0)
        bias = jnp.where((lines == 0) & (spots >= limit), FLOOR_SCORE, 0.0)
        return jnp.concatenate([part.astype(jnp.float32), bias], axis=0).T.astype(jnp.bfloat16)

    @pl.when(pl.program_id(0) == 0)
    def _():
        ones = jnp.ones((wide - HD, block), jnp.bfloat16)

        def place(slot, carry):
            limit = jnp.where(
                scalars[slots + slot] > 0, before - scalars[slot] * block, 0
            )
            spot = pl.multiple_of(slot * block, block)
            keys[pl.ds(spot, block), :] = padded_key(blocks_ref[slot, 0], limit)
            values[:, pl.ds(spot, block)] = jnp.concatenate([blocks_ref[slot, 1], ones], axis=0)
            return carry

        lax.fori_loop(0, slots, place, 0)
        for part in range(rows // block):
            near = slice(part * block, (part + 1) * block)
            far = slice(slots * block + part * block, slots * block + (part + 1) * block)
            keys[far, :] = padded_key(own_key_ref[:, near], live_rows - part * block)
            values[:, far] = jnp.concatenate([own_value_ref[:, near], ones], axis=0)

    query = jnp.concatenate(
        [
            query_ref[0].astype(jnp.float32),
            jnp.ones((16, rows), jnp.float32),
            jnp.zeros((depth - HD - 16, rows), jnp.float32),
        ],
        axis=0,
    ).astype(jnp.bfloat16)

    def score(index, into):
        spot = pl.multiple_of(index * chunk, chunk)
        into[...] = jnp.dot(keys[pl.ds(spot, chunk), :], query, preferred_element_type=jnp.float32)

    def window(index, into):
        near = before + rows - WINDOW
        needed = False
        for part in range(per_chunk):
            needed |= scalars[index * per_chunk + part] * block < near

        @pl.when(needed)
        def _():
            for part in range(per_chunk):
                lines = slice(part * block, (part + 1) * block)
                place = scalars[index * per_chunk + part] * block + lax.broadcasted_iota(
                    jnp.int32, (block, rows), 0
                )
                away = before - place + lax.broadcasted_iota(jnp.int32, (block, rows), 1)
                seen = (away < WINDOW) | (place < SINKS)
                into[lines, :] = jnp.where(seen, into[lines, :], FLOOR_SCORE)

    def absorb(index, held):
        spot = pl.multiple_of(index * chunk, chunk)
        now = held[...]
        largest = jnp.maximum(row_max[...], jnp.max(now, axis=0, keepdims=True))
        fade = jnp.exp2((row_max[...] - largest) * LIFT)
        weights = jnp.exp2((now - largest) * LIFT).astype(jnp.bfloat16)
        row_max[...] = largest
        summed[...] = summed[...] * fade + jnp.dot(
            values[:, pl.ds(spot, chunk)], weights, preferred_element_type=jnp.float32
        )

    score(chunks, score_b)
    causal = lax.broadcasted_iota(jnp.int32, (rows, rows), 0) <= lax.broadcasted_iota(
        jnp.int32, (rows, rows), 1
    )
    score_b[...] = jnp.where(causal, score_b[...], FLOOR_SCORE)
    row_max[...] = jnp.full_like(row_max, FLOOR_SCORE)
    summed[...] = jnp.zeros_like(summed)
    score(0, score_a)
    absorb(chunks, score_b)
    window(0, score_a)

    def pair(step, carry):
        first = step * 2
        score(first + 1, score_b)
        absorb(first, score_a)
        window(first + 1, score_b)
        later = lax.rem(first + 2, chunks)
        score(later, score_a)
        absorb(first + 1, score_b)
        window(later, score_a)
        return carry

    lax.fori_loop(0, chunks // 2, pair, 0)
    out_ref[0] = (summed[:HD, :] / summed[HD : HD + 1, :]).astype(jnp.bfloat16)


def attend(scalars, query, own_key, own_value, blocks):
    heads, width, rows = query.shape
    slots, block = blocks.shape[0], blocks.shape[3]
    span = slots * block + rows
    whole = pl.BlockSpec(memory_space=pltpu.VMEM)
    return pl.pallas_call(
        attention_kernel,
        name="attend",
        grid=(heads,),
        out_shape=jax.ShapeDtypeStruct((heads, width, rows), jnp.bfloat16),
        in_specs=[
            pl.BlockSpec(memory_space=pltpu.SMEM),
            pl.BlockSpec((1, width, rows), lambda head: (head, 0, 0)),
            whole,
            whole,
            whole,
        ],
        out_specs=pl.BlockSpec((1, width, rows), lambda head: (head, 0, 0)),
        scratch_shapes=[
            pltpu.VMEM((span, 128), jnp.bfloat16),
            pltpu.VMEM((96, span), jnp.bfloat16),
            pltpu.VMEM((rows, rows), jnp.float32),
            pltpu.VMEM((rows, rows), jnp.float32),
            pltpu.VMEM((1, rows), jnp.float32),
            pltpu.VMEM((96, rows), jnp.float32),
        ],
        cost_estimate=pl.CostEstimate(
            flops=4 * heads * rows * span * 128,
            bytes_accessed=span * 4 * width,
            transcendentals=heads * rows * span,
        ),
    )(scalars, query, own_key, own_value, blocks)


def hail(n, me):
    barrier = pltpu.get_barrier_semaphore()
    for step in range(1, n):
        peer = lax.rem(me + step, n)
        pl.semaphore_signal(barrier, inc=1, device_id={"kv": peer}, device_id_type=MESH)
    return barrier


class Links:
    def __init__(self, send, recv):
        self.send, self.recv, self.started = send, recv, []

    def go(self, source, target, peer, index):
        copy = pltpu.make_async_remote_copy(
            src_ref=source,
            dst_ref=target,
            send_sem=self.send.at[index],
            recv_sem=self.recv.at[index],
            device_id={"kv": peer},
            device_id_type=MESH,
        )
        copy.start()
        self.started.append(copy)
        return copy

    def close(self):
        for copy in self.started:
            copy.wait_send()


def z_steps(lines):
    return sorted(range(1, lines), key=lambda step: min(step, lines - step))


def as_float(ref):
    return ref[...].astype(jnp.float32)


class Scatter(Links):
    def __init__(self, n, me, view, landings, send, recv):
        super().__init__(send, recv)
        self.land_a, self.land_b, self.stage_a, self.stage_b, self.got_a, self.got_b = landings
        self.lines, self.me, self.view = n // 2, me, view
        self.z, self.y = lax.div(me, 2), lax.rem(me, 2)
        self.partner = 2 * self.z + 1 - self.y
        self.steps = z_steps(self.lines)

    def line(self, step):
        return 2 * lax.rem(self.z + step, self.lines)

    def open(self):
        lines = self.lines
        self.along = [
            self.go(
                self.view(self.line(step) + side, 0),
                self.land_a.at[step - 1, side],
                self.line(step) + self.y,
                2 * (step - 1) + side,
            )
            for step in self.steps
            for side in range(2)
        ]
        self.across = {
            step: self.go(
                self.view(self.line(step) + 1 - self.y, 1),
                self.land_b.at[step],
                self.partner,
                2 * (lines - 1) + step,
            )
            for step in self.steps + [0]
        }

    def forward(self):
        lines = self.lines
        self.last_b = []
        for step in self.steps:
            self.across[step].wait_recv()
            self.stage_b[step - 1] = (
                as_float(self.view(self.line(step) + self.y, 1)) + as_float(self.land_b.at[step])
            ).astype(jnp.bfloat16)
            self.last_b.append(
                self.go(
                    self.stage_b.at[step - 1],
                    self.got_b.at[step - 1],
                    self.line(step) + self.y,
                    3 * lines - 2 + step - 1,
                )
            )
        for copy in self.along:
            copy.wait_recv()
        self.stage_a[...] = self.gathered(1 - self.y).astype(jnp.bfloat16)
        self.last_a = self.go(self.stage_a, self.got_a, self.partner, 4 * lines - 3)

    def gathered(self, side):
        total = as_float(self.view(2 * self.z + side, 0))
        for step in range(self.lines - 1):
            total += as_float(self.land_a.at[step, side])
        return total

    def finish_a(self):
        self.last_a.wait_recv()
        return self.gathered(self.y) + as_float(self.got_a)

    def finish_b(self):
        self.across[0].wait_recv()
        total = as_float(self.view(self.me, 1)) + as_float(self.land_b.at[0])
        for copy in self.last_b:
            copy.wait_recv()
        for step in range(self.lines - 1):
            total += as_float(self.got_b.at[step])
        return total


def scatter_scratch(n, shape, copies=1):
    lines = n // 2
    sizes = [(lines - 1, 2), (lines,), (), (lines - 1,), (), (lines - 1,)]
    lead = () if copies == 1 else (copies,)
    return [pltpu.VMEM(lead + size + shape, jnp.bfloat16) for size in sizes] + [
        pltpu.SemaphoreType.DMA(lead + (4 * lines - 2,))
    ] * 2


def middle_kernel(
    n, piece_ref, token_ref, gain_ref, middle_ref, normed_ref,
    land_a, land_b, stage_a, stage_b, got_a, got_b, send, recv, whole, share, join,
):
    me = lax.axis_index("kv")
    part = piece_ref.shape[2]
    lines = n // 2
    barrier = hail(n, me)
    terms = Scatter(
        n, me, lambda k, h: piece_ref.at[k, h],
        (land_a, land_b, stage_a, stage_b, got_a, got_b), send, recv,
    )
    links = Links(share, join)
    pl.semaphore_wait(barrier, n - 1)
    terms.open()
    terms.forward()

    def rows_of(step, side, half):
        owner = 2 * lax.rem(terms.z + lines - step, lines) + lax.rem(terms.y + side, 2)
        return pl.ds(pl.multiple_of((owner * 2 + half) * part, part), part)

    def index_of(step, side, half):
        return (step * 2 + side) * 2 + half - 2

    came = {}

    def spread(held, slot, peer):
        came[slot] = links.go(whole.at[held], whole.at[slot], peer, index_of(*slot))

    def settle(slot):
        place = rows_of(*slot)
        middle_rows = whole[slot]
        middle_ref[place, :] = middle_rows
        values = middle_rows.astype(jnp.float32)
        mean_square = jnp.mean(values * values, axis=-1, keepdims=True)
        normed_ref[place, :] = (
            values * lax.rsqrt(mean_square + EPSILON) * gain_ref[...]
        ).astype(jnp.bfloat16)

    def peer_at(step):
        return terms.line(step) + terms.y

    own_a = token_ref[rows_of(0, 0, 0), :].astype(jnp.float32)
    whole[0, 0, 0] = (own_a + terms.finish_a()).astype(jnp.bfloat16)
    for step in terms.steps:
        spread((0, 0, 0), (step, 0, 0), peer_at(step))
    spread((0, 0, 0), (0, 1, 0), terms.partner)
    own_b = token_ref[rows_of(0, 0, 1), :].astype(jnp.float32)
    whole[0, 0, 1] = (own_b + terms.finish_b()).astype(jnp.bfloat16)
    spread((0, 0, 1), (0, 1, 1), terms.partner)
    for step in terms.steps:
        spread((0, 0, 1), (step, 0, 1), peer_at(step))
    settle((0, 0, 0))
    settle((0, 0, 1))
    for step in terms.steps:
        came[step, 0, 0].wait_recv()
        spread((step, 0, 0), (step, 1, 0), terms.partner)
        if step == terms.steps[0]:
            came[0, 1, 1].wait_recv()
            for far in terms.steps:
                spread((0, 1, 1), (far, 1, 1), peer_at(far))
    settle((0, 1, 1))
    for step in terms.steps:
        settle((step, 0, 0))
    came[0, 1, 0].wait_recv()
    settle((0, 1, 0))
    for step, side, half in (
        [(step, 0, 1) for step in terms.steps]
        + [(step, 1, 0) for step in terms.steps]
        + [(step, 1, 1) for step in terms.steps]
    ):
        came[step, side, half].wait_recv()
        settle((step, side, half))
    terms.close()
    links.close()


def sum_middle(n, partial_out, tokens, mlp_gain):
    rows, width = tokens.shape
    piece = rows // n
    whole_shape = jax.ShapeDtypeStruct((rows, width), jnp.bfloat16)
    return pl.pallas_call(
        functools.partial(middle_kernel, n),
        name="sum_middle",
        cost_estimate=pl.CostEstimate(flops=0, bytes_accessed=200_000_000, transcendentals=0),
        out_shape=(whole_shape, whole_shape),
        in_specs=[VMEM_SPEC] * 3,
        out_specs=(VMEM_SPEC, VMEM_SPEC),
        scratch_shapes=scatter_scratch(n, (piece // 2, width))
        + [pltpu.VMEM((n // 2, 2, 2, piece // 2, width), jnp.bfloat16)]
        + [pltpu.SemaphoreType.DMA((2 * n - 2,))] * 2,
        compiler_params=pltpu.CompilerParams(collective_id=0, has_side_effects=True),
    )(partial_out.reshape(n, 2, piece // 2, width), tokens, mlp_gain.reshape(1, width))


def hidden_kernel(
    n, normed_ref, middle_hbm, pair_hbm, down_hbm, out_ref, pair, down, hidden, terms,
    window, turned, pair_sem, down_sem, window_sem,
    land_a, land_b, stage_a, stage_b, got_a, got_b, send, recv,
):
    me = lax.axis_index("kv")
    rows, width = normed_ref.shape
    halves, part = terms.shape[0], terms.shape[2]
    piece = width // n
    tiles = pair.shape[1] // 256
    units = down.shape[0]
    barrier = hail(n, me)

    def bring(tile):
        lanes = pl.ds(pl.multiple_of(tile * 256, 256), 256)
        return pltpu.make_async_copy(pair_hbm.at[:, lanes], pair.at[:, lanes], pair_sem.at[tile])

    for tile in range(tiles):
        bring(tile).start()
    fetch = pltpu.make_async_copy(down_hbm, down, down_sem)
    fetch.start()
    left = lax.div(me * piece, 128) * 128
    view = pltpu.make_async_copy(
        middle_hbm.at[:, pl.ds(pl.multiple_of(left, 128), window.shape[1])], window, window_sem
    )
    view.start()

    def exchange(half):
        def term(owner, side):
            start = pl.multiple_of(owner * piece + side * (piece // 2), piece // 2)
            return terms.at[half, pl.ds(start, piece // 2)]

        landings = [ref.at[half] for ref in (land_a, land_b, stage_a, stage_b, got_a, got_b)]
        return Scatter(n, me, term, landings, send.at[half], recv.at[half])

    sums = [exchange(half) for half in range(halves)]
    for half in range(halves):
        lines = slice(half * part, (half + 1) * part)

        @pl.loop(0, tiles)
        def _(tile):
            if half == 0:
                bring(tile).wait()
            lanes = pl.ds(pl.multiple_of(tile * 256, 256), 256)
            both = jnp.dot(normed_ref[lines, :], pair[:, lanes], preferred_element_type=jnp.float32)
            gate, up = both[:, :128], both[:, 128:]
            hidden[:, pl.ds(pl.multiple_of(tile * 128, 128), 128)] = (
                gate / (1.0 + jnp.exp(-gate)) * up
            ).astype(jnp.bfloat16)

        if half == 0:
            fetch.wait()

        @pl.loop(0, width // 512)
        def _(tile):
            spot = pl.ds(pl.multiple_of(tile * 512, 512), 512)
            term = jnp.dot(
                hidden[:, :units], down[:, spot], preferred_element_type=jnp.float32
            )
            terms[half, spot, :] = term.T.astype(jnp.bfloat16)

        if half == 0:
            pl.semaphore_wait(barrier, n - 1)
        sums[half].open()
    view.wait()
    turned[...] = window[...].astype(jnp.float32).T
    for half in range(halves):
        sums[half].forward()
    shift = me * piece - left
    for half in range(halves):
        lines = slice(half * part, (half + 1) * part)
        for side, finish in enumerate((sums[half].finish_a, sums[half].finish_b)):
            residual = pl.ds(pl.multiple_of(shift + side * (piece // 2), 32), piece // 2)
            place = slice(side * (piece // 2), (side + 1) * (piece // 2))
            out_ref[place, lines] = turned[residual, lines] + finish()
    for half in range(halves):
        sums[half].close()


def feed_forward(n, normed_mid, middle, w_pair, w_down):
    rows, width = normed_mid.shape
    halves = 2
    part = rows // halves
    piece = width // n
    half = jnp.bfloat16
    dma = pltpu.SemaphoreType.DMA
    any_spec = pl.BlockSpec(memory_space=pl.ANY)
    return pl.pallas_call(
        functools.partial(hidden_kernel, n),
        name="feed_forward",
        out_shape=jax.ShapeDtypeStruct((piece, rows), jnp.float32),
        in_specs=[VMEM_SPEC, any_spec, any_spec, any_spec],
        out_specs=VMEM_SPEC,
        scratch_shapes=[
            pltpu.VMEM(w_pair.shape, half),
            pltpu.VMEM(w_down.shape, half),
            pltpu.VMEM((part, w_pair.shape[1] // 2), half),
            pltpu.VMEM((halves, width, part), half),
            pltpu.VMEM((rows, piece + 64), half),
            pltpu.VMEM((piece + 64, rows), jnp.float32),
            dma((w_pair.shape[1] // 256,)),
            dma,
            dma,
        ]
        + scatter_scratch(n, (piece // 2, part), halves),
        compiler_params=pltpu.CompilerParams(
            collective_id=1, has_side_effects=True, vmem_limit_bytes=56 * 1024 * 1024
        ),
    )(normed_mid, middle, w_pair, w_down)


def pack_pairs(first, second, groups):
    rows, columns = first.shape
    units = columns // groups
    padded = -(-units // 128) * 128
    tiles = [
        jnp.pad(
            matrix.astype(jnp.bfloat16).reshape(rows, groups, units),
            ((0, 0), (0, 0), (0, padded - units)),
        ).reshape(rows, groups, -1, 1, 128)
        for matrix in (first, second)
    ]
    return jnp.transpose(jnp.concatenate(tiles, axis=3), (1, 0, 2, 3, 4)).reshape(groups, rows, -1)


def shards(
    tokens,
    attn_gain,
    mlp_gain,
    w_query,
    w_key,
    w_value,
    w_gate,
    w_up,
    w_out,
    w_down,
    cache,
    slot_prompt,
    prefix_len,
    new_len,
):
    groups = lax.axis_size("kv")
    n_blocks = lax.axis_size("blk")
    blk_index = lax.axis_index("blk")
    kv_index = lax.axis_index("kv")
    query_width = w_query.shape[1] // groups
    key_width = w_key.shape[1] // groups
    kv_local = key_width // HD
    new_rows = tokens.shape[0]
    prompts = prefix_len.shape[0]
    slots = cache.shape[1]
    prefix_here = prefix_len[blk_index]
    live_count = new_len[blk_index]
    row_ids = jnp.arange(new_rows, dtype=jnp.int32)
    positions = prefix_here + row_ids
    global_rank, local_rank = slot_ranks(slot_prompt, prompts, slots)
    own_prompts = lax.dynamic_slice_in_dim(slot_prompt, blk_index * slots, slots)
    own_ranks = lax.dynamic_slice_in_dim(local_rank, blk_index * slots, slots)
    buffer_ids = jnp.arange(prompts * CAP, dtype=jnp.int32)
    own_slots = jnp.arange(slots, dtype=jnp.int32)
    wanted = jnp.arange(prompts + 1, dtype=jnp.int32)[:, None]
    matches = jnp.where(
        wanted < prompts,
        (own_prompts[None, :] == wanted) & (own_ranks[None, :] == 0),
        own_ranks[None, :] == 1,
    )
    source_slot = jnp.sum(jnp.where(matches, own_slots[None, :], 0), axis=1)
    by_slot = jnp.transpose(cache.reshape(2, slots, HD, BLOCK), (1, 0, 2, 3))
    outgoing = jnp.take(by_slot, source_slot, axis=0, mode="clip")
    projected, w_second, arrived = regroup(
        groups,
        n_blocks,
        pack_groups((w_query, w_key, w_value), groups),
        pack_pairs(w_gate, w_up, groups),
        outgoing[:prompts],
        outgoing[prompts],
        tokens,
        attn_gain,
    )
    w_pair = lax.all_gather(w_second, "blk", axis=0, tiled=True)
    queries = rotate(projected[:, :query_width].reshape(new_rows, -1, HD), positions).astype(
        jnp.bfloat16
    )
    key_new = rotate(
        projected[:, query_width : query_width + key_width].reshape(new_rows, kv_local, HD),
        positions,
    ).astype(jnp.bfloat16)
    value_new = (
        projected[:, query_width + key_width :].reshape(new_rows, kv_local, HD).astype(jnp.bfloat16)
    )
    slot_ids = jnp.arange(prompts * slots, dtype=jnp.int32)
    landing = slot_ids // slots * CAP + local_rank
    for_me = slot_prompt == blk_index
    received = (landing[None, :] == buffer_ids[:, None]) & for_me[None, :]
    block_number = jnp.sum(jnp.where(received, global_rank[None, :], 0), axis=1)
    block_live = jnp.any(received, axis=1)
    blocks = arrived.reshape(prompts * CAP, 2, HD, BLOCK)
    scalars = jnp.concatenate(
        [block_number, block_live.astype(jnp.int32), jnp.stack([prefix_here, live_count])]
    )
    attended = attend(
        scalars,
        jnp.transpose(queries, (1, 2, 0)),
        key_new.reshape(new_rows, HD).T,
        value_new.reshape(new_rows, HD).T,
        blocks,
    ).reshape(-1, new_rows)
    projected_out = lax.dot_general(
        attended, w_out, (((0,), (0,)), ((), ())), preferred_element_type=jnp.float32
    )
    partial_out = projected_out.astype(jnp.bfloat16)
    middle, normed_mid = sum_middle(groups, partial_out, tokens, mlp_gain)
    summed = feed_forward(groups, normed_mid, middle, w_pair, w_down).T
    mixed = jnp.where((row_ids < live_count)[:, None], summed, 0.0)
    return mixed.astype(jnp.bfloat16)


def solution(mesh):
    return jax.shard_map(
        shards,
        mesh=mesh,
        in_specs=(
            P("blk", None),
            P(),
            P(),
            P(("blk", "kv"), None),
            P(("blk", "kv"), None),
            P(("blk", "kv"), None),
            P(("blk", "kv"), None),
            P(("blk", "kv"), None),
            P("kv", None),
            P("kv", None),
            P(None, "blk", "kv", None, None),
            P(),
            P(),
            P(),
        ),
        out_specs=P("blk", "kv"),
        check_vma=False,
    )
```

```python
import functools
import math

import jax
import jax.numpy as jnp
from jax import lax
from jax.experimental import pallas as pl
from jax.experimental.pallas import tpu as pltpu
from jax.sharding import PartitionSpec as P

HEADS = 32
KV_HEADS = 8
HD = 80
WINDOW = 4096
SINKS = 4
BLOCK = 128
CAP = 2


FLOOR_SCORE = -1e30
EPSILON = 1e-05
ROPE_BASE = 10000.0


def rms_scale(row_data, gain_vec):
    values = row_data.astype(jnp.float32)
    mean_square = jnp.mean(values * values, axis=-1, keepdims=True)
    return (values * lax.rsqrt(mean_square + EPSILON) * gain_vec).astype(jnp.bfloat16)


def rotate(values, positions):
    head_width = values.shape[-1]
    half_width = head_width // 2
    frequency = ROPE_BASE ** (-2.0 * jnp.arange(half_width, dtype=jnp.float32) / head_width)
    angles = positions.astype(jnp.float32)[:, None] * frequency[None, :]
    cosine = jnp.cos(angles)[:, None, :]
    sine_wave = jnp.sin(angles)[:, None, :]
    first_half = values[..., :half_width]
    second_half = values[..., half_width:]
    return jnp.concatenate(
        [
            first_half * cosine - second_half * sine_wave,
            second_half * cosine + first_half * sine_wave,
        ],
        axis=-1,
    )


def slot_ranks(slot_prompt, prompts, slots):
    onehot = (slot_prompt[:, None] == jnp.arange(prompts, dtype=jnp.int32)[None, :]).astype(
        jnp.int32
    )
    running = jnp.cumsum(onehot, axis=0)
    global_rank = jnp.sum(onehot * (running - 1), axis=1)
    local_count = jnp.cumsum(onehot.reshape(-1, slots, prompts), axis=1).reshape(-1, prompts)
    local_rank = jnp.sum(onehot * (local_count - 1), axis=1)
    return (global_rank, local_rank)


def pack_groups(matrices, groups):
    rows = matrices[0].shape[0]
    pieces = [
        jnp.transpose(
            matrix.astype(jnp.bfloat16).reshape(rows, groups, matrix.shape[1] // groups), (1, 0, 2)
        )
        for matrix in matrices
    ]
    return jnp.concatenate(pieces, axis=2)


MESH = pl.DeviceIdType.MESH
VMEM_SPEC = pl.BlockSpec(memory_space=pltpu.VMEM)


def fan_out(step_count, make):
    copies = [make(step) for step in range(1, step_count)]
    for copy in copies:
        copy.start()
    return copies


def regroup_kernel(
    n_kv, n_blk, first_ref, second_ref, cache_ref, extra_ref, token_ref, gain_ref,
    projected_ref, second_out, cache_out,
    first_in, second_in, cache_in, whole, extra, normed, weights, stage_a, stage_b,
    first_send, first_recv, second_send, second_recv, cache_send, cache_recv, send, recv,
    extra_send, extra_recv,
):
    me_kv, me = lax.axis_index("kv"), lax.axis_index("blk")
    rows = first_ref.shape[1]
    half, line, core = lax.div(me, 8), lax.rem(lax.div(me, 2), 4), lax.rem(me, 2)

    barrier = pltpu.get_barrier_semaphore()
    for axis, count, mine in (("kv", n_kv, me_kv), ("blk", n_blk, me)):
        for step in range(1, count):
            pl.semaphore_signal(
                barrier, inc=1, device_id={axis: lax.rem(mine + step, count)}, device_id_type=MESH
            )
    pl.semaphore_wait(barrier, n_kv + n_blk - 2)

    def swap(source, landing, sent, got):
        def make(step):
            peer = lax.rem(me_kv + step, n_kv)
            return pltpu.make_async_remote_copy(
                src_ref=source.at[peer],
                dst_ref=landing.at[me_kv],
                send_sem=sent.at[step - 1],
                recv_sem=got.at[step - 1],
                device_id={"kv": peer},
                device_id_type=MESH,
            )

        return fan_out(n_kv, make)

    def deal(step):
        peer = lax.rem(me + step, n_blk)
        return pltpu.make_async_remote_copy(
            src_ref=cache_ref.at[peer],
            dst_ref=cache_in.at[step - 1],
            send_sem=cache_send.at[step - 1],
            recv_sem=cache_recv.at[step - 1],
            device_id={"blk": peer},
            device_id_type=MESH,
        )

    firsts = swap(first_ref, first_in, first_send, first_recv)
    first_in[me_kv] = first_ref[me_kv]
    for copy in firsts:
        copy.wait_recv()
    for group in range(n_kv):
        stage_a[group * rows : (group + 1) * rows, :] = first_in[group].astype(jnp.float32)
    whole[0] = stage_a[...].astype(jnp.bfloat16)

    extra[0] = extra_ref[...]

    passed, passed_extra = {}, {}

    def pass_extra(held, peer, slot):
        copy = pltpu.make_async_remote_copy(
            src_ref=extra.at[held],
            dst_ref=extra.at[slot],
            send_sem=extra_send.at[slot - 1],
            recv_sem=extra_recv.at[slot - 1],
            device_id={"blk": peer},
            device_id_type=MESH,
        )
        copy.start()
        passed_extra[slot] = copy

    def pass_on(held, peer, slot):
        copy = pltpu.make_async_remote_copy(
            src_ref=whole.at[held],
            dst_ref=whole.at[slot],
            send_sem=send.at[slot - 1],
            recv_sem=recv.at[slot - 1],
            device_id={"blk": peer},
            device_id_type=MESH,
        )
        copy.start()
        passed[slot] = copy

    def along(step):
        return half * 8 + lax.rem(line + step, 4) * 2 + core

    across = lax.rem(me + 8, n_blk)
    sibling = me + 1 - 2 * core
    near_rows = whole.shape[1] // 2
    relayed = []

    def relay(base):
        for part, step in enumerate((1, 3)):
            lines = pl.ds(part * near_rows, near_rows)
            index = n_blk - 1 + base // 4 + part
            passed[base + 2 * step].wait_recv()
            copy = pltpu.make_async_remote_copy(
                src_ref=whole.at[base + 2 * step, lines],
                dst_ref=whole.at[base + 4, lines],
                send_sem=send.at[index],
                recv_sem=recv.at[index],
                device_id={"blk": along(step)},
                device_id_type=MESH,
            )
            copy.start()
            relayed.append(copy)

    pass_on(0, across, 8)
    for step in (1, 3):
        pass_on(0, along(step), 2 * step)
    pass_on(0, sibling, 1)
    seconds = swap(second_ref, second_in, second_send, second_recv)

    @pl.loop(0, token_ref.shape[0] // 64)
    def _(part):
        lines = pl.ds(pl.multiple_of(part * 64, 64), 64)
        values = token_ref[lines, :].astype(jnp.float32)
        mean_square = jnp.mean(values * values, axis=-1, keepdims=True)
        normed[lines, :] = (
            values * lax.rsqrt(mean_square + EPSILON) * gain_ref[...]
        ).astype(jnp.bfloat16)

    passed[8].wait_recv()
    for step in (1, 3):
        pass_on(8, along(step), 8 + 2 * step)
    pass_on(8, sibling, 9)
    relay(0)
    for step in (1, 3):
        pass_on(2 * step, sibling, 2 * step + 1)
    relay(8)
    deals = fan_out(n_blk, deal)
    pass_extra(0, across, 8)
    for step in (1, 3, 2):
        pass_extra(0, along(step), 2 * step)
    pass_extra(0, sibling, 1)

    for step in (1, 3):
        pass_on(8 + 2 * step, sibling, 9 + 2 * step)
    for base in (0, 8):
        for copy in relayed[base // 4 : base // 4 + 2]:
            copy.wait_recv()
        pass_on(base + 4, sibling, base + 5)
    second_in[me_kv] = second_ref[me_kv]
    for copy in seconds:
        copy.wait_recv()
    for group in range(n_kv):
        stage_b[group * rows : (group + 1) * rows, :] = second_in[group].astype(jnp.float32)
    second_out[...] = stage_b[...].astype(jnp.bfloat16)
    passed_extra[8].wait_recv()
    for step in (1, 3, 2):
        pass_extra(8, along(step), 8 + 2 * step)
    pass_extra(8, sibling, 9)

    def owner_of(base, step, other):
        return (
            lax.rem(half + base // 8, 2) * 8
            + lax.rem(line + 4 - step, 4) * 2
            + lax.rem(core + other, 2)
        )

    tall = whole.shape[1]
    for base in (0, 8):
        for step in range(4):
            for other in range(2):
                slot = base + 2 * step + other
                if other:
                    passed[slot].wait_recv()
                place = pl.multiple_of(owner_of(base, step, other) * tall, tall)
                weights[pl.ds(place, tall), :] = whole[slot]

    @pl.loop(0, normed.shape[0] // 128)
    def _(part):
        lines = pl.ds(pl.multiple_of(part * 128, 128), 128)
        projected_ref[lines, :] = jnp.dot(
            normed[lines, :], weights[...], preferred_element_type=jnp.float32
        )

    for base in (0, 8):
        for step in (1, 3, 2):
            slot = base + 2 * step
            passed_extra[slot].wait_recv()
            pass_extra(slot, sibling, slot + 1)
    for base in (0, 8):
        for step in range(4):
            for other in range(2):
                slot = base + 2 * step + other
                if other:
                    passed_extra[slot].wait_recv()
                cache_out[owner_of(base, step, other), 1] = extra[slot]
    cache_out[me, 0] = cache_ref[me]
    for step in range(1, n_blk):
        deals[step - 1].wait_recv()
        cache_out[lax.rem(me + n_blk - step, n_blk), 0] = cache_in[step - 1]
    for copy in firsts + seconds + deals + [*passed.values(), *passed_extra.values()] + relayed:
        copy.wait_send()


def regroup(n_kv, n_blk, first, second, cached, extra, tokens, gain):
    rows = first.shape[1]
    tall = n_kv * rows
    first_width, second_width = first.shape[2], second.shape[2]
    half = jnp.bfloat16
    dma = pltpu.SemaphoreType.DMA
    blocks = (n_blk, 2) + cached.shape[1:]
    return pl.pallas_call(
        functools.partial(regroup_kernel, n_kv, n_blk),
        name="regroup",
        out_shape=(
            jax.ShapeDtypeStruct((tokens.shape[0], first_width), jnp.float32),
            jax.ShapeDtypeStruct((tall, second_width), half),
            jax.ShapeDtypeStruct(blocks, half),
        ),
        in_specs=[VMEM_SPEC] * 6,
        out_specs=(VMEM_SPEC,) * 3,
        scratch_shapes=[
            pltpu.VMEM(first.shape, half),
            pltpu.VMEM(second.shape, half),
            pltpu.VMEM((n_blk - 1,) + cached.shape[1:], half),
            pltpu.VMEM((n_blk, tall, first_width), half),
            pltpu.VMEM((n_blk,) + extra.shape, half),
            pltpu.VMEM(tokens.shape, half),
            pltpu.VMEM((n_blk * tall, first_width), half),
            pltpu.VMEM((tall, first_width), jnp.float32),
            pltpu.VMEM((tall, second_width), jnp.float32),
        ]
        + [dma((n_kv - 1,))] * 4
        + [dma((n_blk - 1,))] * 2
        + [dma((n_blk + 3,))] * 2
        + [dma((n_blk - 1,))] * 2,
        compiler_params=pltpu.CompilerParams(collective_id=2, has_side_effects=True),
    )(first, second, cached, extra, tokens, gain.reshape(1, -1))


LIFT = 1.0 / math.sqrt(HD) * math.log2(math.e)


def attention_kernel(
    scalars, query_ref, own_key_ref, own_value_ref, blocks_ref, out_ref,
    keys, values, score_a, score_b, row_max, summed,
):
    slots, block = blocks_ref.shape[0], blocks_ref.shape[3]
    rows = query_ref.shape[2]
    depth = keys.shape[1]
    wide = values.shape[0]
    chunk = rows
    per_chunk = chunk // block
    chunks = slots // per_chunk
    before, live_rows = scalars[2 * slots], scalars[2 * slots + 1]

    def padded_key(part, limit):
        spots = lax.broadcasted_iota(jnp.int32, (depth - HD, block), 1)
        lines = lax.broadcasted_iota(jnp.int32, (depth - HD, block), 0)
        bias = jnp.where((lines == 0) & (spots >= limit), FLOOR_SCORE, 0.0)
        return jnp.concatenate([part.astype(jnp.float32), bias], axis=0).T.astype(jnp.bfloat16)

    @pl.when(pl.program_id(0) == 0)
    def _():
        ones = jnp.ones((wide - HD, block), jnp.bfloat16)

        def place(slot, carry):
            limit = jnp.where(
                scalars[slots + slot] > 0, before - scalars[slot] * block, 0
            )
            spot = pl.multiple_of(slot * block, block)
            keys[pl.ds(spot, block), :] = padded_key(blocks_ref[slot, 0], limit)
            values[:, pl.ds(spot, block)] = jnp.concatenate([blocks_ref[slot, 1], ones], axis=0)
            return carry

        lax.fori_loop(0, slots, place, 0)
        for part in range(rows // block):
            near = slice(part * block, (part + 1) * block)
            far = slice(slots * block + part * block, slots * block + (part + 1) * block)
            keys[far, :] = padded_key(own_key_ref[:, near], live_rows - part * block)
            values[:, far] = jnp.concatenate([own_value_ref[:, near], ones], axis=0)

    query = jnp.concatenate(
        [
            query_ref[0].astype(jnp.float32),
            jnp.ones((16, rows), jnp.float32),
            jnp.zeros((depth - HD - 16, rows), jnp.float32),
        ],
        axis=0,
    ).astype(jnp.bfloat16)

    def score(index, into):
        spot = pl.multiple_of(index * chunk, chunk)
        into[...] = jnp.dot(keys[pl.ds(spot, chunk), :], query, preferred_element_type=jnp.float32)

    def window(index, into):
        near = before + rows - WINDOW
        needed = False
        for part in range(per_chunk):
            needed |= scalars[index * per_chunk + part] * block < near

        @pl.when(needed)
        def _():
            for part in range(per_chunk):
                lines = slice(part * block, (part + 1) * block)
                place = scalars[index * per_chunk + part] * block + lax.broadcasted_iota(
                    jnp.int32, (block, rows), 0
                )
                away = before - place + lax.broadcasted_iota(jnp.int32, (block, rows), 1)
                seen = (away < WINDOW) | (place < SINKS)
                into[lines, :] = jnp.where(seen, into[lines, :], FLOOR_SCORE)

    def absorb(index, held):
        spot = pl.multiple_of(index * chunk, chunk)
        now = held[...]
        largest = jnp.maximum(row_max[...], jnp.max(now, axis=0, keepdims=True))
        fade = jnp.exp2((row_max[...] - largest) * LIFT)
        weights = jnp.exp2((now - largest) * LIFT).astype(jnp.bfloat16)
        row_max[...] = largest
        summed[...] = summed[...] * fade + jnp.dot(
            values[:, pl.ds(spot, chunk)], weights, preferred_element_type=jnp.float32
        )

    score(chunks, score_b)
    causal = lax.broadcasted_iota(jnp.int32, (rows, rows), 0) <= lax.broadcasted_iota(
        jnp.int32, (rows, rows), 1
    )
    score_b[...] = jnp.where(causal, score_b[...], FLOOR_SCORE)
    row_max[...] = jnp.full_like(row_max, FLOOR_SCORE)
    summed[...] = jnp.zeros_like(summed)
    score(0, score_a)
    absorb(chunks, score_b)
    window(0, score_a)

    def pair(step, carry):
        first = step * 2
        score(first + 1, score_b)
        absorb(first, score_a)
        window(first + 1, score_b)
        later = lax.rem(first + 2, chunks)
        score(later, score_a)
        absorb(first + 1, score_b)
        window(later, score_a)
        return carry

    lax.fori_loop(0, chunks // 2, pair, 0)
    out_ref[0] = (summed[:HD, :] / summed[HD : HD + 1, :]).astype(jnp.bfloat16)


def attend(scalars, query, own_key, own_value, blocks):
    heads, width, rows = query.shape
    slots, block = blocks.shape[0], blocks.shape[3]
    span = slots * block + rows
    whole = pl.BlockSpec(memory_space=pltpu.VMEM)
    return pl.pallas_call(
        attention_kernel,
        name="attend",
        grid=(heads,),
        out_shape=jax.ShapeDtypeStruct((heads, width, rows), jnp.bfloat16),
        in_specs=[
            pl.BlockSpec(memory_space=pltpu.SMEM),
            pl.BlockSpec((1, width, rows), lambda head: (head, 0, 0)),
            whole,
            whole,
            whole,
        ],
        out_specs=pl.BlockSpec((1, width, rows), lambda head: (head, 0, 0)),
        scratch_shapes=[
            pltpu.VMEM((span, 128), jnp.bfloat16),
            pltpu.VMEM((96, span), jnp.bfloat16),
            pltpu.VMEM((rows, rows), jnp.float32),
            pltpu.VMEM((rows, rows), jnp.float32),
            pltpu.VMEM((1, rows), jnp.float32),
            pltpu.VMEM((96, rows), jnp.float32),
        ],
        cost_estimate=pl.CostEstimate(
            flops=4 * heads * rows * span * 128,
            bytes_accessed=span * 4 * width,
            transcendentals=heads * rows * span,
        ),
    )(scalars, query, own_key, own_value, blocks)


def hail(n, me):
    barrier = pltpu.get_barrier_semaphore()
    for step in range(1, n):
        peer = lax.rem(me + step, n)
        pl.semaphore_signal(barrier, inc=1, device_id={"kv": peer}, device_id_type=MESH)
    return barrier


class Links:
    def __init__(self, send, recv):
        self.send, self.recv, self.started = send, recv, []

    def go(self, source, target, peer, index):
        copy = pltpu.make_async_remote_copy(
            src_ref=source,
            dst_ref=target,
            send_sem=self.send.at[index],
            recv_sem=self.recv.at[index],
            device_id={"kv": peer},
            device_id_type=MESH,
        )
        copy.start()
        self.started.append(copy)
        return copy

    def close(self):
        for copy in self.started:
            copy.wait_send()


def z_steps(lines):
    return sorted(range(1, lines), key=lambda step: min(step, lines - step))


def as_float(ref):
    return ref[...].astype(jnp.float32)


class Scatter(Links):
    def __init__(self, n, me, view, landings, send, recv):
        super().__init__(send, recv)
        self.land_a, self.land_b, self.stage_a, self.stage_b, self.got_a, self.got_b = landings
        self.lines, self.me, self.view = n // 2, me, view
        self.z, self.y = lax.div(me, 2), lax.rem(me, 2)
        self.partner = 2 * self.z + 1 - self.y
        self.steps = z_steps(self.lines)

    def line(self, step):
        return 2 * lax.rem(self.z + step, self.lines)

    def open(self):
        lines = self.lines
        self.along = [
            self.go(
                self.view(self.line(step) + side, 0),
                self.land_a.at[step - 1, side],
                self.line(step) + self.y,
                2 * (step - 1) + side,
            )
            for step in self.steps
            for side in range(2)
        ]
        self.across = {
            step: self.go(
                self.view(self.line(step) + 1 - self.y, 1),
                self.land_b.at[step],
                self.partner,
                2 * (lines - 1) + step,
            )
            for step in self.steps + [0]
        }

    def forward(self):
        lines = self.lines
        self.last_b = []
        for step in self.steps:
            self.across[step].wait_recv()
            self.stage_b[step - 1] = (
                as_float(self.view(self.line(step) + self.y, 1)) + as_float(self.land_b.at[step])
            ).astype(jnp.bfloat16)
            self.last_b.append(
                self.go(
                    self.stage_b.at[step - 1],
                    self.got_b.at[step - 1],
                    self.line(step) + self.y,
                    3 * lines - 2 + step - 1,
                )
            )
        for copy in self.along:
            copy.wait_recv()
        self.stage_a[...] = self.gathered(1 - self.y).astype(jnp.bfloat16)
        self.last_a = self.go(self.stage_a, self.got_a, self.partner, 4 * lines - 3)

    def gathered(self, side):
        total = as_float(self.view(2 * self.z + side, 0))
        for step in range(self.lines - 1):
            total += as_float(self.land_a.at[step, side])
        return total

    def finish_a(self):
        self.last_a.wait_recv()
        return self.gathered(self.y) + as_float(self.got_a)

    def finish_b(self):
        self.across[0].wait_recv()
        total = as_float(self.view(self.me, 1)) + as_float(self.land_b.at[0])
        for copy in self.last_b:
            copy.wait_recv()
        for step in range(self.lines - 1):
            total += as_float(self.got_b.at[step])
        return total


def scatter_scratch(n, shape, copies=1):
    lines = n // 2
    sizes = [(lines - 1, 2), (lines,), (), (lines - 1,), (), (lines - 1,)]
    lead = () if copies == 1 else (copies,)
    return [pltpu.VMEM(lead + size + shape, jnp.bfloat16) for size in sizes] + [
        pltpu.SemaphoreType.DMA(lead + (4 * lines - 2,))
    ] * 2


def middle_kernel(
    n, piece_ref, token_ref, gain_ref, middle_ref, normed_ref,
    land_a, land_b, stage_a, stage_b, got_a, got_b, send, recv, whole, share, join,
):
    me = lax.axis_index("kv")
    part = piece_ref.shape[2]
    lines = n // 2
    barrier = hail(n, me)
    terms = Scatter(
        n, me, lambda k, h: piece_ref.at[k, h],
        (land_a, land_b, stage_a, stage_b, got_a, got_b), send, recv,
    )
    links = Links(share, join)
    pl.semaphore_wait(barrier, n - 1)
    terms.open()
    terms.forward()

    def rows_of(step, side, half):
        owner = 2 * lax.rem(terms.z + lines - step, lines) + lax.rem(terms.y + side, 2)
        return pl.ds(pl.multiple_of((owner * 2 + half) * part, part), part)

    def index_of(step, side, half):
        return (step * 2 + side) * 2 + half - 2

    came = {}

    def spread(held, slot, peer):
        came[slot] = [links.go(whole.at[held], whole.at[slot], peer, index_of(*slot))]

    def wait(slot):
        for copy in came[slot]:
            copy.wait_recv()

    def relay(side, half):
        came[2, side, half] = []
        for quarter, step in enumerate((1, 3)):
            held = pl.ds(quarter * (part // 2), part // 2)
            wait((step, side, half))
            came[2, side, half].append(
                links.go(
                    whole.at[step, side, half, held],
                    whole.at[2, side, half, held],
                    peer_at(step),
                    index_of(2, side, half) if quarter == 0 else 2 * n - 2 + side + half,
                )
            )

    def settle(slot):
        place = rows_of(*slot)
        middle_rows = whole[slot]
        middle_ref[place, :] = middle_rows
        values = middle_rows.astype(jnp.float32)
        mean_square = jnp.mean(values * values, axis=-1, keepdims=True)
        normed_ref[place, :] = (
            values * lax.rsqrt(mean_square + EPSILON) * gain_ref[...]
        ).astype(jnp.bfloat16)

    def peer_at(step):
        return terms.line(step) + terms.y

    own_a = token_ref[rows_of(0, 0, 0), :].astype(jnp.float32)
    whole[0, 0, 0] = (own_a + terms.finish_a()).astype(jnp.bfloat16)
    for step in (1, 3):
        spread((0, 0, 0), (step, 0, 0), peer_at(step))
    spread((0, 0, 0), (0, 1, 0), terms.partner)
    own_b = token_ref[rows_of(0, 0, 1), :].astype(jnp.float32)
    whole[0, 0, 1] = (own_b + terms.finish_b()).astype(jnp.bfloat16)
    spread((0, 0, 1), (0, 1, 1), terms.partner)
    for step in (1, 3):
        spread((0, 0, 1), (step, 0, 1), peer_at(step))
    settle((0, 0, 0))
    relay(0, 0)
    for step in (1, 3):
        spread((step, 0, 0), (step, 1, 0), terms.partner)
    wait((0, 1, 1))
    for step in (1, 3):
        spread((0, 1, 1), (step, 1, 1), peer_at(step))
    relay(0, 1)
    wait((2, 0, 0))
    spread((2, 0, 0), (2, 1, 0), terms.partner)
    settle((0, 0, 1))
    settle((0, 1, 1))
    relay(1, 1)
    for step in (1, 3, 2):
        settle((step, 0, 0))
    wait((0, 1, 0))
    settle((0, 1, 0))
    settle((1, 0, 1))
    settle((3, 0, 1))
    settle((1, 1, 1))
    settle((3, 1, 1))
    for slot in ((2, 0, 1), (1, 1, 0), (3, 1, 0), (2, 1, 1), (2, 1, 0)):
        wait(slot)
        settle(slot)
    terms.close()
    links.close()


def sum_middle(n, partial_out, tokens, mlp_gain):
    rows, width = tokens.shape
    piece = rows // n
    whole_shape = jax.ShapeDtypeStruct((rows, width), jnp.bfloat16)
    return pl.pallas_call(
        functools.partial(middle_kernel, n),
        name="sum_middle",
        cost_estimate=pl.CostEstimate(flops=0, bytes_accessed=200_000_000, transcendentals=0),
        out_shape=(whole_shape, whole_shape),
        in_specs=[VMEM_SPEC] * 3,
        out_specs=(VMEM_SPEC, VMEM_SPEC),
        scratch_shapes=scatter_scratch(n, (piece // 2, width))
        + [pltpu.VMEM((n // 2, 2, 2, piece // 2, width), jnp.bfloat16)]
        + [pltpu.SemaphoreType.DMA((2 * n + 1,))] * 2,
        compiler_params=pltpu.CompilerParams(collective_id=0, has_side_effects=True),
    )(partial_out.reshape(n, 2, piece // 2, width), tokens, mlp_gain.reshape(1, width))


def hidden_kernel(
    n, normed_ref, middle_hbm, pair_hbm, down_hbm, out_ref, pair, down, hidden, terms,
    window, turned, pair_sem, down_sem, window_sem,
    land_a, land_b, stage_a, stage_b, got_a, got_b, send, recv,
):
    me = lax.axis_index("kv")
    rows, width = normed_ref.shape
    halves, part = terms.shape[0], terms.shape[2]
    piece = width // n
    tiles = pair.shape[1] // 256
    units = down.shape[0]
    barrier = hail(n, me)

    def bring(tile):
        lanes = pl.ds(pl.multiple_of(tile * 256, 256), 256)
        return pltpu.make_async_copy(pair_hbm.at[:, lanes], pair.at[:, lanes], pair_sem.at[tile])

    for tile in range(tiles):
        bring(tile).start()
    fetch = pltpu.make_async_copy(down_hbm, down, down_sem)
    fetch.start()
    left = lax.div(me * piece, 128) * 128
    view = pltpu.make_async_copy(
        middle_hbm.at[:, pl.ds(pl.multiple_of(left, 128), window.shape[1])], window, window_sem
    )
    view.start()

    def exchange(half):
        def term(owner, side):
            start = pl.multiple_of(owner * piece + side * (piece // 2), piece // 2)
            return terms.at[half, pl.ds(start, piece // 2)]

        landings = [ref.at[half] for ref in (land_a, land_b, stage_a, stage_b, got_a, got_b)]
        return Scatter(n, me, term, landings, send.at[half], recv.at[half])

    sums = [exchange(half) for half in range(halves)]
    for half in range(halves):
        lines = slice(half * part, (half + 1) * part)

        @pl.loop(0, tiles)
        def _(tile):
            if half == 0:
                bring(tile).wait()
            lanes = pl.ds(pl.multiple_of(tile * 256, 256), 256)
            both = jnp.dot(normed_ref[lines, :], pair[:, lanes], preferred_element_type=jnp.float32)
            gate, up = both[:, :128], both[:, 128:]
            hidden[:, pl.ds(pl.multiple_of(tile * 128, 128), 128)] = (
                gate / (1.0 + jnp.exp(-gate)) * up
            ).astype(jnp.bfloat16)

        if half == 0:
            fetch.wait()

        @pl.loop(0, width // 512)
        def _(tile):
            spot = pl.ds(pl.multiple_of(tile * 512, 512), 512)
            term = jnp.dot(
                hidden[:, :units], down[:, spot], preferred_element_type=jnp.float32
            )
            terms[half, spot, :] = term.T.astype(jnp.bfloat16)

        if half == 0:
            pl.semaphore_wait(barrier, n - 1)
        sums[half].open()
    view.wait()
    turned[...] = window[...].astype(jnp.float32).T
    for half in range(halves):
        sums[half].forward()
    shift = me * piece - left
    for half in range(halves):
        lines = slice(half * part, (half + 1) * part)
        for side, finish in enumerate((sums[half].finish_a, sums[half].finish_b)):
            residual = pl.ds(pl.multiple_of(shift + side * (piece // 2), 32), piece // 2)
            place = slice(side * (piece // 2), (side + 1) * (piece // 2))
            out_ref[place, lines] = turned[residual, lines] + finish()
    for half in range(halves):
        sums[half].close()


def feed_forward(n, normed_mid, middle, w_pair, w_down):
    rows, width = normed_mid.shape
    halves = 2
    part = rows // halves
    piece = width // n
    half = jnp.bfloat16
    dma = pltpu.SemaphoreType.DMA
    any_spec = pl.BlockSpec(memory_space=pl.ANY)
    return pl.pallas_call(
        functools.partial(hidden_kernel, n),
        name="feed_forward",
        out_shape=jax.ShapeDtypeStruct((piece, rows), jnp.float32),
        in_specs=[VMEM_SPEC, any_spec, any_spec, any_spec],
        out_specs=VMEM_SPEC,
        scratch_shapes=[
            pltpu.VMEM(w_pair.shape, half),
            pltpu.VMEM(w_down.shape, half),
            pltpu.VMEM((part, w_pair.shape[1] // 2), half),
            pltpu.VMEM((halves, width, part), half),
            pltpu.VMEM((rows, piece + 64), half),
            pltpu.VMEM((piece + 64, rows), jnp.float32),
            dma((w_pair.shape[1] // 256,)),
            dma,
            dma,
        ]
        + scatter_scratch(n, (piece // 2, part), halves),
        compiler_params=pltpu.CompilerParams(
            collective_id=1, has_side_effects=True, vmem_limit_bytes=56 * 1024 * 1024
        ),
    )(normed_mid, middle, w_pair, w_down)


def pack_pairs(first, second, groups):
    rows, columns = first.shape
    units = columns // groups
    padded = -(-units // 128) * 128
    tiles = [
        jnp.pad(
            matrix.astype(jnp.bfloat16).reshape(rows, groups, units),
            ((0, 0), (0, 0), (0, padded - units)),
        ).reshape(rows, groups, -1, 1, 128)
        for matrix in (first, second)
    ]
    return jnp.transpose(jnp.concatenate(tiles, axis=3), (1, 0, 2, 3, 4)).reshape(groups, rows, -1)


def shards(
    tokens,
    attn_gain,
    mlp_gain,
    w_query,
    w_key,
    w_value,
    w_gate,
    w_up,
    w_out,
    w_down,
    cache,
    slot_prompt,
    prefix_len,
    new_len,
):
    groups = lax.axis_size("kv")
    n_blocks = lax.axis_size("blk")
    blk_index = lax.axis_index("blk")
    kv_index = lax.axis_index("kv")
    query_width = w_query.shape[1] // groups
    key_width = w_key.shape[1] // groups
    kv_local = key_width // HD
    new_rows = tokens.shape[0]
    prompts = prefix_len.shape[0]
    slots = cache.shape[1]
    prefix_here = prefix_len[blk_index]
    live_count = new_len[blk_index]
    row_ids = jnp.arange(new_rows, dtype=jnp.int32)
    positions = prefix_here + row_ids
    global_rank, local_rank = slot_ranks(slot_prompt, prompts, slots)
    own_prompts = lax.dynamic_slice_in_dim(slot_prompt, blk_index * slots, slots)
    own_ranks = lax.dynamic_slice_in_dim(local_rank, blk_index * slots, slots)
    buffer_ids = jnp.arange(prompts * CAP, dtype=jnp.int32)
    own_slots = jnp.arange(slots, dtype=jnp.int32)
    wanted = jnp.arange(prompts + 1, dtype=jnp.int32)[:, None]
    matches = jnp.where(
        wanted < prompts,
        (own_prompts[None, :] == wanted) & (own_ranks[None, :] == 0),
        own_ranks[None, :] == 1,
    )
    source_slot = jnp.sum(jnp.where(matches, own_slots[None, :], 0), axis=1)
    by_slot = jnp.transpose(cache.reshape(2, slots, HD, BLOCK), (1, 0, 2, 3))
    outgoing = jnp.take(by_slot, source_slot, axis=0, mode="clip")
    projected, w_second, arrived = regroup(
        groups,
        n_blocks,
        pack_groups((w_query, w_key, w_value), groups),
        pack_pairs(w_gate, w_up, groups),
        outgoing[:prompts],
        outgoing[prompts],
        tokens,
        attn_gain,
    )
    w_pair = lax.all_gather(w_second, "blk", axis=0, tiled=True)
    queries = rotate(projected[:, :query_width].reshape(new_rows, -1, HD), positions).astype(
        jnp.bfloat16
    )
    key_new = rotate(
        projected[:, query_width : query_width + key_width].reshape(new_rows, kv_local, HD),
        positions,
    ).astype(jnp.bfloat16)
    value_new = (
        projected[:, query_width + key_width :].reshape(new_rows, kv_local, HD).astype(jnp.bfloat16)
    )
    slot_ids = jnp.arange(prompts * slots, dtype=jnp.int32)
    landing = slot_ids // slots * CAP + local_rank
    for_me = slot_prompt == blk_index
    received = (landing[None, :] == buffer_ids[:, None]) & for_me[None, :]
    block_number = jnp.sum(jnp.where(received, global_rank[None, :], 0), axis=1)
    block_live = jnp.any(received, axis=1)
    blocks = arrived.reshape(prompts * CAP, 2, HD, BLOCK)
    scalars = jnp.concatenate(
        [block_number, block_live.astype(jnp.int32), jnp.stack([prefix_here, live_count])]
    )
    attended = attend(
        scalars,
        jnp.transpose(queries, (1, 2, 0)),
        key_new.reshape(new_rows, HD).T,
        value_new.reshape(new_rows, HD).T,
        blocks,
    ).reshape(-1, new_rows)
    projected_out = lax.dot_general(
        attended, w_out, (((0,), (0,)), ((), ())), preferred_element_type=jnp.float32
    )
    partial_out = projected_out.astype(jnp.bfloat16)
    middle, normed_mid = sum_middle(groups, partial_out, tokens, mlp_gain)
    summed = feed_forward(groups, normed_mid, middle, w_pair, w_down).T
    mixed = jnp.where((row_ids < live_count)[:, None], summed, 0.0)
    return mixed.astype(jnp.bfloat16)


def solution(mesh):
    return jax.shard_map(
        shards,
        mesh=mesh,
        in_specs=(
            P("blk", None),
            P(),
            P(),
            P(("blk", "kv"), None),
            P(("blk", "kv"), None),
            P(("blk", "kv"), None),
            P(("blk", "kv"), None),
            P(("blk", "kv"), None),
            P("kv", None),
            P("kv", None),
            P(None, "blk", "kv", None, None),
            P(),
            P(),
            P(),
        ),
        out_specs=P("blk", "kv"),
        check_vma=False,
    )
```

```python
import functools
import math

import jax
import jax.numpy as jnp
from jax import lax
from jax.experimental import pallas as pl
from jax.experimental.pallas import tpu as pltpu
from jax.sharding import PartitionSpec as P

HEADS = 32
KV_HEADS = 8
HD = 80
WINDOW = 4096
SINKS = 4
BLOCK = 128
CAP = 2


FLOOR_SCORE = -1e30
EPSILON = 1e-05
ROPE_BASE = 10000.0


def pack_groups(matrices, groups):
    rows = matrices[0].shape[0]
    pieces = [
        jnp.transpose(
            matrix.astype(jnp.bfloat16).reshape(rows, groups, matrix.shape[1] // groups), (1, 0, 2)
        )
        for matrix in matrices
    ]
    return jnp.concatenate(pieces, axis=2)


MESH = pl.DeviceIdType.MESH
VMEM_SPEC = pl.BlockSpec(memory_space=pltpu.VMEM)


def fan_out(step_count, make):
    copies = [make(step) for step in range(1, step_count)]
    for copy in copies:
        copy.start()
    return copies


def regroup_kernel(
    n_kv, n_blk, first_ref, second_ref, cache_ref, extra_ref, token_ref, gain_ref,
    projected_ref, second_out, cache_out,
    first_in, second_in, cache_in, whole, extra, normed, weights, stage_a, stage_b,
    first_send, first_recv, second_send, second_recv, cache_send, cache_recv, send, recv,
    extra_send, extra_recv,
):
    me_kv, me = lax.axis_index("kv"), lax.axis_index("blk")
    rows = first_ref.shape[1]
    half, line, core = lax.div(me, 8), lax.rem(lax.div(me, 2), 4), lax.rem(me, 2)

    barrier = pltpu.get_barrier_semaphore()
    for axis, count, mine in (("kv", n_kv, me_kv), ("blk", n_blk, me)):
        for step in range(1, count):
            pl.semaphore_signal(
                barrier, inc=1, device_id={axis: lax.rem(mine + step, count)}, device_id_type=MESH
            )
    pl.semaphore_wait(barrier, n_kv + n_blk - 2)

    def swap(source, landing, sent, got):
        def make(step):
            peer = lax.rem(me_kv + step, n_kv)
            return pltpu.make_async_remote_copy(
                src_ref=source.at[peer],
                dst_ref=landing.at[me_kv],
                send_sem=sent.at[step - 1],
                recv_sem=got.at[step - 1],
                device_id={"kv": peer},
                device_id_type=MESH,
            )

        return fan_out(n_kv, make)

    def deal(step):
        peer = lax.rem(me + step, n_blk)
        return pltpu.make_async_remote_copy(
            src_ref=cache_ref.at[peer],
            dst_ref=cache_in.at[step - 1],
            send_sem=cache_send.at[step - 1],
            recv_sem=cache_recv.at[step - 1],
            device_id={"blk": peer},
            device_id_type=MESH,
        )

    firsts = swap(first_ref, first_in, first_send, first_recv)
    first_in[me_kv] = first_ref[me_kv]
    for copy in firsts:
        copy.wait_recv()
    for group in range(n_kv):
        stage_a[group * rows : (group + 1) * rows, :] = first_in[group].astype(jnp.float32)
    whole[0] = stage_a[...].astype(jnp.bfloat16)

    extra[0] = extra_ref[...]

    passed, passed_extra = {}, {}

    def pass_extra(held, peer, slot):
        copy = pltpu.make_async_remote_copy(
            src_ref=extra.at[held],
            dst_ref=extra.at[slot],
            send_sem=extra_send.at[slot - 1],
            recv_sem=extra_recv.at[slot - 1],
            device_id={"blk": peer},
            device_id_type=MESH,
        )
        copy.start()
        passed_extra[slot] = copy

    def pass_on(held, peer, slot):
        copy = pltpu.make_async_remote_copy(
            src_ref=whole.at[held],
            dst_ref=whole.at[slot],
            send_sem=send.at[slot - 1],
            recv_sem=recv.at[slot - 1],
            device_id={"blk": peer},
            device_id_type=MESH,
        )
        copy.start()
        passed[slot] = copy

    def along(step):
        return half * 8 + lax.rem(line + step, 4) * 2 + core

    across = lax.rem(me + 8, n_blk)
    sibling = me + 1 - 2 * core
    near_rows = whole.shape[1] // 2
    relayed = []

    def relay(base):
        for part, step in enumerate((1, 3)):
            lines = pl.ds(part * near_rows, near_rows)
            index = n_blk - 1 + base // 4 + part
            passed[base + 2 * step].wait_recv()
            copy = pltpu.make_async_remote_copy(
                src_ref=whole.at[base + 2 * step, lines],
                dst_ref=whole.at[base + 4, lines],
                send_sem=send.at[index],
                recv_sem=recv.at[index],
                device_id={"blk": along(step)},
                device_id_type=MESH,
            )
            copy.start()
            relayed.append(copy)

    pass_on(0, across, 8)
    for step in (1, 3):
        pass_on(0, along(step), 2 * step)
    pass_on(0, sibling, 1)
    seconds = swap(second_ref, second_in, second_send, second_recv)

    @pl.loop(0, token_ref.shape[0] // 64)
    def _(part):
        lines = pl.ds(pl.multiple_of(part * 64, 64), 64)
        values = token_ref[lines, :].astype(jnp.float32)
        mean_square = jnp.mean(values * values, axis=-1, keepdims=True)
        normed[lines, :] = (
            values * lax.rsqrt(mean_square + EPSILON) * gain_ref[...]
        ).astype(jnp.bfloat16)

    passed[8].wait_recv()
    for step in (1, 3):
        pass_on(8, along(step), 8 + 2 * step)
    pass_on(8, sibling, 9)
    relay(0)
    for step in (1, 3):
        pass_on(2 * step, sibling, 2 * step + 1)
    relay(8)
    deals = fan_out(n_blk, deal)
    pass_extra(0, across, 8)
    for step in (1, 3, 2):
        pass_extra(0, along(step), 2 * step)
    pass_extra(0, sibling, 1)

    for step in (1, 3):
        pass_on(8 + 2 * step, sibling, 9 + 2 * step)
    for base in (0, 8):
        for copy in relayed[base // 4 : base // 4 + 2]:
            copy.wait_recv()
        pass_on(base + 4, sibling, base + 5)
    second_in[me_kv] = second_ref[me_kv]
    for copy in seconds:
        copy.wait_recv()
    for group in range(n_kv):
        stage_b[group * rows : (group + 1) * rows, :] = second_in[group].astype(jnp.float32)
    second_out[...] = stage_b[...].astype(jnp.bfloat16)
    passed_extra[8].wait_recv()
    for step in (1, 3, 2):
        pass_extra(8, along(step), 8 + 2 * step)
    pass_extra(8, sibling, 9)

    def owner_of(base, step, other):
        return (
            lax.rem(half + base // 8, 2) * 8
            + lax.rem(line + 4 - step, 4) * 2
            + lax.rem(core + other, 2)
        )

    tall = whole.shape[1]
    for base in (0, 8):
        for step in range(4):
            for other in range(2):
                slot = base + 2 * step + other
                if other:
                    passed[slot].wait_recv()
                place = pl.multiple_of(owner_of(base, step, other) * tall, tall)
                weights[pl.ds(place, tall), :] = whole[slot]

    @pl.loop(0, normed.shape[0] // 128)
    def _(part):
        lines = pl.ds(pl.multiple_of(part * 128, 128), 128)
        projected_ref[:, lines] = jnp.dot(
            normed[lines, :], weights[...], preferred_element_type=jnp.float32
        ).T

    for base in (0, 8):
        for step in (1, 3, 2):
            slot = base + 2 * step
            passed_extra[slot].wait_recv()
            pass_extra(slot, sibling, slot + 1)
    for base in (0, 8):
        for step in range(4):
            for other in range(2):
                slot = base + 2 * step + other
                if other:
                    passed_extra[slot].wait_recv()
                cache_out[owner_of(base, step, other), 1] = extra[slot]
    cache_out[me, 0] = cache_ref[me]
    for step in range(1, n_blk):
        deals[step - 1].wait_recv()
        cache_out[lax.rem(me + n_blk - step, n_blk), 0] = cache_in[step - 1]
    for copy in firsts + seconds + deals + [*passed.values(), *passed_extra.values()] + relayed:
        copy.wait_send()


def regroup(n_kv, n_blk, first, second, cached, extra, tokens, gain):
    rows = first.shape[1]
    tall = n_kv * rows
    first_width, second_width = first.shape[2], second.shape[2]
    half = jnp.bfloat16
    dma = pltpu.SemaphoreType.DMA
    blocks = (n_blk, 2) + cached.shape[1:]
    return pl.pallas_call(
        functools.partial(regroup_kernel, n_kv, n_blk),
        name="regroup",
        out_shape=(
            jax.ShapeDtypeStruct((first_width, tokens.shape[0]), jnp.float32),
            jax.ShapeDtypeStruct((tall, second_width), half),
            jax.ShapeDtypeStruct(blocks, half),
        ),
        in_specs=[VMEM_SPEC] * 6,
        out_specs=(VMEM_SPEC,) * 3,
        scratch_shapes=[
            pltpu.VMEM(first.shape, half),
            pltpu.VMEM(second.shape, half),
            pltpu.VMEM((n_blk - 1,) + cached.shape[1:], half),
            pltpu.VMEM((n_blk, tall, first_width), half),
            pltpu.VMEM((n_blk,) + extra.shape, half),
            pltpu.VMEM(tokens.shape, half),
            pltpu.VMEM((n_blk * tall, first_width), half),
            pltpu.VMEM((tall, first_width), jnp.float32),
            pltpu.VMEM((tall, second_width), jnp.float32),
        ]
        + [dma((n_kv - 1,))] * 4
        + [dma((n_blk - 1,))] * 2
        + [dma((n_blk + 3,))] * 2
        + [dma((n_blk - 1,))] * 2,
        compiler_params=pltpu.CompilerParams(collective_id=2, has_side_effects=True),
    )(first, second, cached, extra, tokens, gain.reshape(1, -1))


LIFT = 1.0 / math.sqrt(HD) * math.log2(math.e)


def attention_kernel(
    prompt_ref, prefix_ref, new_ref, projected_ref, cosine_ref, sine_ref, blocks_ref, out_ref,
    keys, values, score_a, score_b, row_max, summed, scalars,
):
    me = lax.axis_index("blk")
    slots, block = blocks_ref.shape[0], blocks_ref.shape[3]
    rows = projected_ref.shape[1]
    heads = pl.num_programs(0)
    depth = keys.shape[1]
    wide = values.shape[0]
    chunk = rows
    per_chunk = chunk // block
    chunks = slots // per_chunk
    before, live_rows = prefix_ref[me], new_ref[me]

    def rotated(index):
        start = pl.multiple_of(index * HD, HD)
        first = projected_ref[pl.ds(start, HD // 2), :]
        second = projected_ref[pl.ds(start + HD // 2, HD // 2), :]
        cosine, sine = cosine_ref[...], sine_ref[...]
        return jnp.concatenate(
            [first * cosine - second * sine, second * cosine + first * sine], axis=0
        )

    def padded_key(part, limit):
        spots = lax.broadcasted_iota(jnp.int32, (depth - HD, block), 1)
        lines = lax.broadcasted_iota(jnp.int32, (depth - HD, block), 0)
        bias = jnp.where((lines == 0) & (spots >= limit), FLOOR_SCORE, 0.0)
        return jnp.concatenate([part.astype(jnp.float32), bias], axis=0).T.astype(jnp.bfloat16)

    @pl.when(pl.program_id(0) == 0)
    def _():
        ones = jnp.ones((wide - HD, block), jnp.bfloat16)

        def clear(spot, carry):
            scalars[spot] = 0
            return carry

        lax.fori_loop(0, 2 * slots, clear, 0)
        sources = slots // CAP
        each = prompt_ref.shape[0] // sources

        def find(source, count):
            rank = jnp.int32(0)
            for spot in range(each):
                mine = prompt_ref[source * each + spot] == me
                target = source * CAP + jnp.minimum(rank, CAP - 1)

                @pl.when(mine)
                def _(target=target, count=count):
                    scalars[target] = count
                    scalars[slots + target] = 1

                rank = rank + mine.astype(jnp.int32)
                count = count + mine.astype(jnp.int32)
            return count

        lax.fori_loop(0, sources, find, jnp.int32(0))
        own_key = rotated(heads)
        own_value = projected_ref[(heads + 1) * HD : (heads + 2) * HD, :].astype(jnp.bfloat16)

        def place(slot, carry):
            limit = jnp.where(
                scalars[slots + slot] > 0, before - scalars[slot] * block, 0
            )
            spot = pl.multiple_of(slot * block, block)
            keys[pl.ds(spot, block), :] = padded_key(blocks_ref[slot, 0], limit)
            values[:, pl.ds(spot, block)] = jnp.concatenate([blocks_ref[slot, 1], ones], axis=0)
            return carry

        lax.fori_loop(0, slots, place, 0)
        for part in range(rows // block):
            near = slice(part * block, (part + 1) * block)
            far = slice(slots * block + part * block, slots * block + (part + 1) * block)
            keys[far, :] = padded_key(own_key[:, near], live_rows - part * block)
            values[:, far] = jnp.concatenate([own_value[:, near], ones], axis=0)

    query = jnp.concatenate(
        [
            rotated(pl.program_id(0)),
            jnp.ones((16, rows), jnp.float32),
            jnp.zeros((depth - HD - 16, rows), jnp.float32),
        ],
        axis=0,
    ).astype(jnp.bfloat16)

    def score(index, into):
        spot = pl.multiple_of(index * chunk, chunk)
        into[...] = jnp.dot(keys[pl.ds(spot, chunk), :], query, preferred_element_type=jnp.float32)

    def window(index, into):
        near = before + rows - WINDOW
        needed = False
        for part in range(per_chunk):
            needed |= scalars[index * per_chunk + part] * block < near

        @pl.when(needed)
        def _():
            for part in range(per_chunk):
                lines = slice(part * block, (part + 1) * block)
                place = scalars[index * per_chunk + part] * block + lax.broadcasted_iota(
                    jnp.int32, (block, rows), 0
                )
                away = before - place + lax.broadcasted_iota(jnp.int32, (block, rows), 1)
                seen = (away < WINDOW) | (place < SINKS)
                into[lines, :] = jnp.where(seen, into[lines, :], FLOOR_SCORE)

    def absorb(index, held):
        spot = pl.multiple_of(index * chunk, chunk)
        now = held[...]
        largest = jnp.maximum(row_max[...], jnp.max(now, axis=0, keepdims=True))
        fade = jnp.exp2((row_max[...] - largest) * LIFT)
        weights = jnp.exp2((now - largest) * LIFT).astype(jnp.bfloat16)
        row_max[...] = largest
        summed[...] = summed[...] * fade + jnp.dot(
            values[:, pl.ds(spot, chunk)], weights, preferred_element_type=jnp.float32
        )

    score(chunks, score_b)
    causal = lax.broadcasted_iota(jnp.int32, (rows, rows), 0) <= lax.broadcasted_iota(
        jnp.int32, (rows, rows), 1
    )
    score_b[...] = jnp.where(causal, score_b[...], FLOOR_SCORE)
    row_max[...] = jnp.full_like(row_max, FLOOR_SCORE)
    summed[...] = jnp.zeros_like(summed)
    score(0, score_a)
    absorb(chunks, score_b)
    window(0, score_a)

    def pair(step, carry):
        first = step * 2
        score(first + 1, score_b)
        absorb(first, score_a)
        window(first + 1, score_b)
        later = lax.rem(first + 2, chunks)
        score(later, score_a)
        absorb(first + 1, score_b)
        window(later, score_a)
        return carry

    lax.fori_loop(0, chunks // 2, pair, 0)
    out_ref[0] = (summed[:HD, :] / summed[HD : HD + 1, :]).astype(jnp.bfloat16)


def attend(heads, slot_prompt, prefix_len, new_len, projected, cosine, sine, blocks):
    rows = projected.shape[1]
    slots, _, width, block = blocks.shape
    span = slots * block + rows
    smem = pl.BlockSpec(memory_space=pltpu.SMEM)
    return pl.pallas_call(
        attention_kernel,
        name="attend",
        grid=(heads,),
        out_shape=jax.ShapeDtypeStruct((heads, width, rows), jnp.bfloat16),
        in_specs=[smem, smem, smem] + [VMEM_SPEC] * 4,
        out_specs=pl.BlockSpec((1, width, rows), lambda head: (head, 0, 0)),
        scratch_shapes=[
            pltpu.VMEM((span, 128), jnp.bfloat16),
            pltpu.VMEM((96, span), jnp.bfloat16),
            pltpu.VMEM((rows, rows), jnp.float32),
            pltpu.VMEM((rows, rows), jnp.float32),
            pltpu.VMEM((1, rows), jnp.float32),
            pltpu.VMEM((96, rows), jnp.float32),
            pltpu.SMEM((2 * slots,), jnp.int32),
        ],
        cost_estimate=pl.CostEstimate(
            flops=4 * heads * rows * span * 128,
            bytes_accessed=span * 4 * width,
            transcendentals=heads * rows * span,
        ),
    )(slot_prompt, prefix_len, new_len, projected, cosine, sine, blocks)


def hail(n, me):
    barrier = pltpu.get_barrier_semaphore()
    for step in range(1, n):
        peer = lax.rem(me + step, n)
        pl.semaphore_signal(barrier, inc=1, device_id={"kv": peer}, device_id_type=MESH)
    return barrier


class Links:
    def __init__(self, send, recv):
        self.send, self.recv, self.started = send, recv, []

    def go(self, source, target, peer, index):
        copy = pltpu.make_async_remote_copy(
            src_ref=source,
            dst_ref=target,
            send_sem=self.send.at[index],
            recv_sem=self.recv.at[index],
            device_id={"kv": peer},
            device_id_type=MESH,
        )
        copy.start()
        self.started.append(copy)
        return copy

    def close(self):
        for copy in self.started:
            copy.wait_send()


def z_steps(lines):
    return sorted(range(1, lines), key=lambda step: min(step, lines - step))


def as_float(ref):
    return ref[...].astype(jnp.float32)


class Scatter(Links):
    def __init__(self, n, me, view, landings, send, recv):
        super().__init__(send, recv)
        self.land_a, self.land_b, self.stage_a, self.stage_b, self.got_a, self.got_b = landings
        self.lines, self.me, self.view = n // 2, me, view
        self.z, self.y = lax.div(me, 2), lax.rem(me, 2)
        self.partner = 2 * self.z + 1 - self.y
        self.steps = z_steps(self.lines)

    def line(self, step):
        return 2 * lax.rem(self.z + step, self.lines)

    def open(self):
        lines = self.lines
        self.along = [
            self.go(
                self.view(self.line(step) + side, 0),
                self.land_a.at[step - 1, side],
                self.line(step) + self.y,
                2 * (step - 1) + side,
            )
            for step in self.steps
            for side in range(2)
        ]
        self.across = {
            step: self.go(
                self.view(self.line(step) + 1 - self.y, 1),
                self.land_b.at[step],
                self.partner,
                2 * (lines - 1) + step,
            )
            for step in self.steps + [0]
        }

    def forward(self):
        lines = self.lines
        self.last_b = []
        for step in self.steps:
            self.across[step].wait_recv()
            self.stage_b[step - 1] = (
                as_float(self.view(self.line(step) + self.y, 1)) + as_float(self.land_b.at[step])
            ).astype(jnp.bfloat16)
            self.last_b.append(
                self.go(
                    self.stage_b.at[step - 1],
                    self.got_b.at[step - 1],
                    self.line(step) + self.y,
                    3 * lines - 2 + step - 1,
                )
            )
        for copy in self.along:
            copy.wait_recv()
        self.stage_a[...] = self.gathered(1 - self.y).astype(jnp.bfloat16)
        self.last_a = self.go(self.stage_a, self.got_a, self.partner, 4 * lines - 3)

    def gathered(self, side):
        total = as_float(self.view(2 * self.z + side, 0))
        for step in range(self.lines - 1):
            total += as_float(self.land_a.at[step, side])
        return total

    def finish_a(self):
        self.last_a.wait_recv()
        return self.gathered(self.y) + as_float(self.got_a)

    def finish_b(self):
        self.across[0].wait_recv()
        total = as_float(self.view(self.me, 1)) + as_float(self.land_b.at[0])
        for copy in self.last_b:
            copy.wait_recv()
        for step in range(self.lines - 1):
            total += as_float(self.got_b.at[step])
        return total


def scatter_scratch(n, shape, copies=1):
    lines = n // 2
    sizes = [(lines - 1, 2), (lines,), (), (lines - 1,), (), (lines - 1,)]
    lead = () if copies == 1 else (copies,)
    return [pltpu.VMEM(lead + size + shape, jnp.bfloat16) for size in sizes] + [
        pltpu.SemaphoreType.DMA(lead + (4 * lines - 2,))
    ] * 2


def middle_kernel(
    n, piece_ref, token_ref, gain_ref, middle_ref, normed_ref,
    land_a, land_b, stage_a, stage_b, got_a, got_b, send, recv, whole, share, join,
):
    me = lax.axis_index("kv")
    part = piece_ref.shape[2]
    lines = n // 2
    barrier = hail(n, me)
    terms = Scatter(
        n, me, lambda k, h: piece_ref.at[k, h],
        (land_a, land_b, stage_a, stage_b, got_a, got_b), send, recv,
    )
    links = Links(share, join)
    pl.semaphore_wait(barrier, n - 1)
    terms.open()
    terms.forward()

    def rows_of(step, side, half):
        owner = 2 * lax.rem(terms.z + lines - step, lines) + lax.rem(terms.y + side, 2)
        return pl.ds(pl.multiple_of((owner * 2 + half) * part, part), part)

    def index_of(step, side, half):
        return (step * 2 + side) * 2 + half - 2

    came = {}

    def spread(held, slot, peer):
        came[slot] = [links.go(whole.at[held], whole.at[slot], peer, index_of(*slot))]

    def wait(slot):
        for copy in came[slot]:
            copy.wait_recv()

    def relay(side, half):
        came[2, side, half] = []
        for quarter, step in enumerate((1, 3)):
            held = pl.ds(quarter * (part // 2), part // 2)
            wait((step, side, half))
            came[2, side, half].append(
                links.go(
                    whole.at[step, side, half, held],
                    whole.at[2, side, half, held],
                    peer_at(step),
                    index_of(2, side, half) if quarter == 0 else 2 * n - 2 + side + half,
                )
            )

    def settle(slot):
        place = rows_of(*slot)
        middle_rows = whole[slot]
        middle_ref[place, :] = middle_rows
        values = middle_rows.astype(jnp.float32)
        mean_square = jnp.mean(values * values, axis=-1, keepdims=True)
        normed_ref[place, :] = (
            values * lax.rsqrt(mean_square + EPSILON) * gain_ref[...]
        ).astype(jnp.bfloat16)

    def peer_at(step):
        return terms.line(step) + terms.y

    own_a = token_ref[rows_of(0, 0, 0), :].astype(jnp.float32)
    whole[0, 0, 0] = (own_a + terms.finish_a()).astype(jnp.bfloat16)
    for step in (1, 3):
        spread((0, 0, 0), (step, 0, 0), peer_at(step))
    spread((0, 0, 0), (0, 1, 0), terms.partner)
    own_b = token_ref[rows_of(0, 0, 1), :].astype(jnp.float32)
    whole[0, 0, 1] = (own_b + terms.finish_b()).astype(jnp.bfloat16)
    spread((0, 0, 1), (0, 1, 1), terms.partner)
    for step in (1, 3):
        spread((0, 0, 1), (step, 0, 1), peer_at(step))
    settle((0, 0, 0))
    relay(0, 0)
    for step in (1, 3):
        spread((step, 0, 0), (step, 1, 0), terms.partner)
    wait((0, 1, 1))
    for step in (1, 3):
        spread((0, 1, 1), (step, 1, 1), peer_at(step))
    relay(0, 1)
    wait((2, 0, 0))
    spread((2, 0, 0), (2, 1, 0), terms.partner)
    settle((0, 0, 1))
    settle((0, 1, 1))
    relay(1, 1)
    for step in (1, 3, 2):
        settle((step, 0, 0))
    wait((0, 1, 0))
    settle((0, 1, 0))
    settle((1, 0, 1))
    settle((3, 0, 1))
    settle((1, 1, 1))
    settle((3, 1, 1))
    for slot in ((2, 0, 1), (1, 1, 0), (3, 1, 0), (2, 1, 1), (2, 1, 0)):
        wait(slot)
        settle(slot)
    terms.close()
    links.close()


def sum_middle(n, partial_out, tokens, mlp_gain):
    rows, width = tokens.shape
    piece = rows // n
    whole_shape = jax.ShapeDtypeStruct((rows, width), jnp.bfloat16)
    return pl.pallas_call(
        functools.partial(middle_kernel, n),
        name="sum_middle",
        cost_estimate=pl.CostEstimate(flops=0, bytes_accessed=200_000_000, transcendentals=0),
        out_shape=(whole_shape, whole_shape),
        in_specs=[VMEM_SPEC] * 3,
        out_specs=(VMEM_SPEC, VMEM_SPEC),
        scratch_shapes=scatter_scratch(n, (piece // 2, width))
        + [pltpu.VMEM((n // 2, 2, 2, piece // 2, width), jnp.bfloat16)]
        + [pltpu.SemaphoreType.DMA((2 * n + 1,))] * 2,
        compiler_params=pltpu.CompilerParams(collective_id=0, has_side_effects=True),
    )(partial_out.reshape(n, 2, piece // 2, width), tokens, mlp_gain.reshape(1, width))


def hidden_kernel(
    n, normed_ref, middle_hbm, pair_hbm, down_hbm, out_ref, pair, down, hidden, terms,
    window, turned, pair_sem, down_sem, window_sem,
    land_a, land_b, stage_a, stage_b, got_a, got_b, send, recv,
):
    me = lax.axis_index("kv")
    rows, width = normed_ref.shape
    halves, part = terms.shape[0], terms.shape[2]
    piece = width // n
    tiles = pair.shape[1] // 256
    units = down.shape[0]
    barrier = hail(n, me)

    def bring(tile):
        lanes = pl.ds(pl.multiple_of(tile * 256, 256), 256)
        return pltpu.make_async_copy(pair_hbm.at[:, lanes], pair.at[:, lanes], pair_sem.at[tile])

    for tile in range(tiles):
        bring(tile).start()
    fetch = pltpu.make_async_copy(down_hbm, down, down_sem)
    fetch.start()
    left = lax.div(me * piece, 128) * 128
    view = pltpu.make_async_copy(
        middle_hbm.at[:, pl.ds(pl.multiple_of(left, 128), window.shape[1])], window, window_sem
    )
    view.start()

    def exchange(half):
        def term(owner, side):
            start = pl.multiple_of(owner * piece + side * (piece // 2), piece // 2)
            return terms.at[half, pl.ds(start, piece // 2)]

        landings = [ref.at[half] for ref in (land_a, land_b, stage_a, stage_b, got_a, got_b)]
        return Scatter(n, me, term, landings, send.at[half], recv.at[half])

    sums = [exchange(half) for half in range(halves)]
    for half in range(halves):
        lines = slice(half * part, (half + 1) * part)

        @pl.loop(0, tiles)
        def _(tile):
            if half == 0:
                bring(tile).wait()
            lanes = pl.ds(pl.multiple_of(tile * 256, 256), 256)
            both = jnp.dot(normed_ref[lines, :], pair[:, lanes], preferred_element_type=jnp.float32)
            gate, up = both[:, :128], both[:, 128:]
            hidden[:, pl.ds(pl.multiple_of(tile * 128, 128), 128)] = (
                gate / (1.0 + jnp.exp(-gate)) * up
            ).astype(jnp.bfloat16)

        if half == 0:
            fetch.wait()

        @pl.loop(0, width // 512)
        def _(tile):
            spot = pl.ds(pl.multiple_of(tile * 512, 512), 512)
            term = jnp.dot(
                hidden[:, :units], down[:, spot], preferred_element_type=jnp.float32
            )
            terms[half, spot, :] = term.T.astype(jnp.bfloat16)

        if half == 0:
            pl.semaphore_wait(barrier, n - 1)
        sums[half].open()
    view.wait()
    turned[...] = window[...].astype(jnp.float32).T
    for half in range(halves):
        sums[half].forward()
    shift = me * piece - left
    for half in range(halves):
        lines = slice(half * part, (half + 1) * part)
        for side, finish in enumerate((sums[half].finish_a, sums[half].finish_b)):
            residual = pl.ds(pl.multiple_of(shift + side * (piece // 2), 32), piece // 2)
            place = slice(side * (piece // 2), (side + 1) * (piece // 2))
            out_ref[place, lines] = turned[residual, lines] + finish()
    for half in range(halves):
        sums[half].close()


def feed_forward(n, normed_mid, middle, w_pair, w_down):
    rows, width = normed_mid.shape
    halves = 2
    part = rows // halves
    piece = width // n
    half = jnp.bfloat16
    dma = pltpu.SemaphoreType.DMA
    any_spec = pl.BlockSpec(memory_space=pl.ANY)
    return pl.pallas_call(
        functools.partial(hidden_kernel, n),
        name="feed_forward",
        out_shape=jax.ShapeDtypeStruct((piece, rows), jnp.float32),
        in_specs=[VMEM_SPEC, any_spec, any_spec, any_spec],
        out_specs=VMEM_SPEC,
        scratch_shapes=[
            pltpu.VMEM(w_pair.shape, half),
            pltpu.VMEM(w_down.shape, half),
            pltpu.VMEM((part, w_pair.shape[1] // 2), half),
            pltpu.VMEM((halves, width, part), half),
            pltpu.VMEM((rows, piece + 64), half),
            pltpu.VMEM((piece + 64, rows), jnp.float32),
            dma((w_pair.shape[1] // 256,)),
            dma,
            dma,
        ]
        + scatter_scratch(n, (piece // 2, part), halves),
        compiler_params=pltpu.CompilerParams(
            collective_id=1, has_side_effects=True, vmem_limit_bytes=56 * 1024 * 1024
        ),
    )(normed_mid, middle, w_pair, w_down)


def pack_pairs(first, second, groups):
    rows, columns = first.shape
    units = columns // groups
    padded = -(-units // 128) * 128
    tiles = [
        jnp.pad(
            matrix.astype(jnp.bfloat16).reshape(rows, groups, units),
            ((0, 0), (0, 0), (0, padded - units)),
        ).reshape(rows, groups, -1, 1, 128)
        for matrix in (first, second)
    ]
    return jnp.transpose(jnp.concatenate(tiles, axis=3), (1, 0, 2, 3, 4)).reshape(groups, rows, -1)


def shards(
    tokens,
    attn_gain,
    mlp_gain,
    w_query,
    w_key,
    w_value,
    w_gate,
    w_up,
    w_out,
    w_down,
    cache,
    slot_prompt,
    prefix_len,
    new_len,
):
    groups = lax.axis_size("kv")
    n_blocks = lax.axis_size("blk")
    blk_index = lax.axis_index("blk")
    new_rows = tokens.shape[0]
    prompts = prefix_len.shape[0]
    slots = cache.shape[1]
    row_ids = jnp.arange(new_rows, dtype=jnp.int32)
    frequency = ROPE_BASE ** (-2.0 * jnp.arange(HD // 2, dtype=jnp.float32) / HD)
    positions = (prefix_len[blk_index] + row_ids).astype(jnp.float32)
    angles = positions[None, :] * frequency[:, None]
    own_prompts = lax.dynamic_slice_in_dim(slot_prompt, blk_index * slots, slots)
    earlier = jnp.tri(slots, k=-1, dtype=jnp.bool_)
    own_ranks = jnp.sum(
        ((own_prompts[:, None] == own_prompts[None, :]) & earlier).astype(jnp.int32), axis=1
    )
    own_slots = jnp.arange(slots, dtype=jnp.int32)
    wanted = jnp.arange(prompts + 1, dtype=jnp.int32)[:, None]
    matches = jnp.where(
        wanted < prompts,
        (own_prompts[None, :] == wanted) & (own_ranks[None, :] == 0),
        own_ranks[None, :] == 1,
    )
    source_slot = jnp.sum(jnp.where(matches, own_slots[None, :], 0), axis=1)
    by_slot = jnp.transpose(cache.reshape(2, slots, HD, BLOCK), (1, 0, 2, 3))
    outgoing = jnp.take(by_slot, source_slot, axis=0, mode="clip")
    projected, w_second, arrived = regroup(
        groups,
        n_blocks,
        pack_groups((w_query, w_key, w_value), groups),
        pack_pairs(w_gate, w_up, groups),
        outgoing[:prompts],
        outgoing[prompts],
        tokens,
        attn_gain,
    )
    w_pair = lax.all_gather(w_second, "blk", axis=0, tiled=True)
    attended = attend(
        HEADS // groups,
        slot_prompt,
        prefix_len,
        new_len,
        projected,
        jnp.cos(angles),
        jnp.sin(angles),
        arrived.reshape(prompts * CAP, 2, HD, BLOCK),
    ).reshape(-1, new_rows)
    projected_out = lax.dot_general(
        attended, w_out, (((0,), (0,)), ((), ())), preferred_element_type=jnp.float32
    )
    partial_out = projected_out.astype(jnp.bfloat16)
    middle, normed_mid = sum_middle(groups, partial_out, tokens, mlp_gain)
    summed = feed_forward(groups, normed_mid, middle, w_pair, w_down).T
    mixed = jnp.where((row_ids < new_len[blk_index])[:, None], summed, 0.0)
    return mixed.astype(jnp.bfloat16)


def solution(mesh):
    return jax.shard_map(
        shards,
        mesh=mesh,
        in_specs=(
            P("blk", None),
            P(),
            P(),
            P(("blk", "kv"), None),
            P(("blk", "kv"), None),
            P(("blk", "kv"), None),
            P(("blk", "kv"), None),
            P(("blk", "kv"), None),
            P("kv", None),
            P("kv", None),
            P(None, "blk", "kv", None, None),
            P(),
            P(),
            P(),
        ),
        out_specs=P("blk", "kv"),
        check_vma=False,
    )
```

```python
import functools
import math

import jax
import jax.numpy as jnp
from jax import lax
from jax.experimental import pallas as pl
from jax.experimental.pallas import tpu as pltpu
from jax.sharding import PartitionSpec as P

HEADS = 32
KV_HEADS = 8
HD = 80
WINDOW = 4096
SINKS = 4
BLOCK = 128
CAP = 2


FLOOR_SCORE = -1e30
EPSILON = 1e-05
ROPE_BASE = 10000.0


def pack_groups(matrices, groups):
    rows = matrices[0].shape[0]
    pieces = [
        jnp.transpose(
            matrix.astype(jnp.bfloat16).reshape(rows, groups, matrix.shape[1] // groups), (1, 0, 2)
        )
        for matrix in matrices
    ]
    return jnp.concatenate(pieces, axis=2)


MESH = pl.DeviceIdType.MESH
VMEM_SPEC = pl.BlockSpec(memory_space=pltpu.VMEM)


def fan_out(step_count, make):
    copies = [make(step) for step in range(1, step_count)]
    for copy in copies:
        copy.start()
    return copies


def regroup_kernel(
    n_kv, n_blk, first_ref, second_ref, cache_ref, extra_ref, token_ref, gain_ref,
    projected_ref, second_out, cache_out,
    first_in, second_in, cache_in, whole, extra, normed, weights, stage_a, stage_b,
    first_send, first_recv, second_send, second_recv, cache_send, cache_recv, send, recv,
    extra_send, extra_recv,
):
    me_kv, me = lax.axis_index("kv"), lax.axis_index("blk")
    rows = first_ref.shape[1]
    half, line, core = lax.div(me, 8), lax.rem(lax.div(me, 2), 4), lax.rem(me, 2)

    barrier = pltpu.get_barrier_semaphore()
    for axis, count, mine in (("kv", n_kv, me_kv), ("blk", n_blk, me)):
        for step in range(1, count):
            pl.semaphore_signal(
                barrier, inc=1, device_id={axis: lax.rem(mine + step, count)}, device_id_type=MESH
            )
    pl.semaphore_wait(barrier, n_kv + n_blk - 2)

    def swap(source, landing, sent, got):
        def make(step):
            peer = lax.rem(me_kv + step, n_kv)
            return pltpu.make_async_remote_copy(
                src_ref=source.at[peer],
                dst_ref=landing.at[me_kv],
                send_sem=sent.at[step - 1],
                recv_sem=got.at[step - 1],
                device_id={"kv": peer},
                device_id_type=MESH,
            )

        return fan_out(n_kv, make)

    def deal(step):
        peer = lax.rem(me + step, n_blk)
        return pltpu.make_async_remote_copy(
            src_ref=cache_ref.at[peer],
            dst_ref=cache_in.at[step - 1],
            send_sem=cache_send.at[step - 1],
            recv_sem=cache_recv.at[step - 1],
            device_id={"blk": peer},
            device_id_type=MESH,
        )

    firsts = swap(first_ref, first_in, first_send, first_recv)
    first_in[me_kv] = first_ref[me_kv]
    for copy in firsts:
        copy.wait_recv()
    for group in range(n_kv):
        stage_a[group * rows : (group + 1) * rows, :] = first_in[group].astype(jnp.float32)
    whole[0] = stage_a[...].astype(jnp.bfloat16)

    extra[0] = extra_ref[...]

    passed, passed_extra = {}, {}

    def pass_extra(held, peer, slot):
        copy = pltpu.make_async_remote_copy(
            src_ref=extra.at[held],
            dst_ref=extra.at[slot],
            send_sem=extra_send.at[slot - 1],
            recv_sem=extra_recv.at[slot - 1],
            device_id={"blk": peer},
            device_id_type=MESH,
        )
        copy.start()
        passed_extra[slot] = copy

    def pass_on(held, peer, slot):
        copy = pltpu.make_async_remote_copy(
            src_ref=whole.at[held],
            dst_ref=whole.at[slot],
            send_sem=send.at[slot - 1],
            recv_sem=recv.at[slot - 1],
            device_id={"blk": peer},
            device_id_type=MESH,
        )
        copy.start()
        passed[slot] = copy

    def along(step):
        return half * 8 + lax.rem(line + step, 4) * 2 + core

    across = lax.rem(me + 8, n_blk)
    sibling = me + 1 - 2 * core
    near_rows = whole.shape[1] // 2
    relayed = []

    def relay(base):
        for part, step in enumerate((1, 3)):
            lines = pl.ds(part * near_rows, near_rows)
            index = n_blk - 1 + base // 4 + part
            passed[base + 2 * step].wait_recv()
            copy = pltpu.make_async_remote_copy(
                src_ref=whole.at[base + 2 * step, lines],
                dst_ref=whole.at[base + 4, lines],
                send_sem=send.at[index],
                recv_sem=recv.at[index],
                device_id={"blk": along(step)},
                device_id_type=MESH,
            )
            copy.start()
            relayed.append(copy)

    pass_on(0, across, 8)
    for step in (1, 3):
        pass_on(0, along(step), 2 * step)
    pass_on(0, sibling, 1)
    seconds = swap(second_ref, second_in, second_send, second_recv)

    @pl.loop(0, token_ref.shape[0] // 64)
    def _(part):
        lines = pl.ds(pl.multiple_of(part * 64, 64), 64)
        values = token_ref[lines, :].astype(jnp.float32)
        mean_square = jnp.mean(values * values, axis=-1, keepdims=True)
        normed[lines, :] = (
            values * lax.rsqrt(mean_square + EPSILON) * gain_ref[...]
        ).astype(jnp.bfloat16)

    passed[8].wait_recv()
    for step in (1, 3):
        pass_on(8, along(step), 8 + 2 * step)
    pass_on(8, sibling, 9)
    relay(0)
    for step in (1, 3):
        pass_on(2 * step, sibling, 2 * step + 1)
    relay(8)
    deals = fan_out(n_blk, deal)
    pass_extra(0, across, 8)
    for step in (1, 3, 2):
        pass_extra(0, along(step), 2 * step)
    pass_extra(0, sibling, 1)

    for step in (1, 3):
        pass_on(8 + 2 * step, sibling, 9 + 2 * step)
    for base in (0, 8):
        for copy in relayed[base // 4 : base // 4 + 2]:
            copy.wait_recv()
        pass_on(base + 4, sibling, base + 5)
    second_in[me_kv] = second_ref[me_kv]
    for copy in seconds:
        copy.wait_recv()
    for group in range(n_kv):
        stage_b[group * rows : (group + 1) * rows, :] = second_in[group].astype(jnp.float32)
    second_out[...] = stage_b[...].astype(jnp.bfloat16)
    passed_extra[8].wait_recv()
    for step in (1, 3, 2):
        pass_extra(8, along(step), 8 + 2 * step)
    pass_extra(8, sibling, 9)

    def owner_of(base, step, other):
        return (
            lax.rem(half + base // 8, 2) * 8
            + lax.rem(line + 4 - step, 4) * 2
            + lax.rem(core + other, 2)
        )

    tall = whole.shape[1]
    for base in (0, 8):
        for step in range(4):
            for other in range(2):
                slot = base + 2 * step + other
                if other:
                    passed[slot].wait_recv()
                place = pl.multiple_of(owner_of(base, step, other) * tall, tall)
                weights[pl.ds(place, tall), :] = whole[slot]

    @pl.loop(0, normed.shape[0] // 128)
    def _(part):
        lines = pl.ds(pl.multiple_of(part * 128, 128), 128)
        projected_ref[:, lines] = jnp.dot(
            normed[lines, :], weights[...], preferred_element_type=jnp.float32
        ).T

    for base in (0, 8):
        for step in (1, 3, 2):
            slot = base + 2 * step
            passed_extra[slot].wait_recv()
            pass_extra(slot, sibling, slot + 1)
    for base in (0, 8):
        for step in range(4):
            for other in range(2):
                slot = base + 2 * step + other
                if other:
                    passed_extra[slot].wait_recv()
                cache_out[owner_of(base, step, other), 1] = extra[slot]
    cache_out[me, 0] = cache_ref[me]
    for step in range(1, n_blk):
        deals[step - 1].wait_recv()
        cache_out[lax.rem(me + n_blk - step, n_blk), 0] = cache_in[step - 1]
    for copy in firsts + seconds + deals + [*passed.values(), *passed_extra.values()] + relayed:
        copy.wait_send()


def regroup(n_kv, n_blk, first, second, cached, extra, tokens, gain):
    rows = first.shape[1]
    tall = n_kv * rows
    first_width, second_width = first.shape[2], second.shape[2]
    half = jnp.bfloat16
    dma = pltpu.SemaphoreType.DMA
    blocks = (n_blk, 2) + cached.shape[1:]
    return pl.pallas_call(
        functools.partial(regroup_kernel, n_kv, n_blk),
        name="regroup",
        out_shape=(
            jax.ShapeDtypeStruct((first_width, tokens.shape[0]), jnp.float32),
            jax.ShapeDtypeStruct((tall, second_width), half),
            jax.ShapeDtypeStruct(blocks, half),
        ),
        in_specs=[VMEM_SPEC] * 6,
        out_specs=(VMEM_SPEC,) * 3,
        scratch_shapes=[
            pltpu.VMEM(first.shape, half),
            pltpu.VMEM(second.shape, half),
            pltpu.VMEM((n_blk - 1,) + cached.shape[1:], half),
            pltpu.VMEM((n_blk, tall, first_width), half),
            pltpu.VMEM((n_blk,) + extra.shape, half),
            pltpu.VMEM(tokens.shape, half),
            pltpu.VMEM((n_blk * tall, first_width), half),
            pltpu.VMEM((tall, first_width), jnp.float32),
            pltpu.VMEM((tall, second_width), jnp.float32),
        ]
        + [dma((n_kv - 1,))] * 4
        + [dma((n_blk - 1,))] * 2
        + [dma((n_blk + 3,))] * 2
        + [dma((n_blk - 1,))] * 2,
        compiler_params=pltpu.CompilerParams(collective_id=2, has_side_effects=True),
    )(first, second, cached, extra, tokens, gain.reshape(1, -1))


LIFT = 1.0 / math.sqrt(HD) * math.log2(math.e)


def attention_kernel(
    prompt_ref, prefix_ref, new_ref, projected_ref, cosine_ref, sine_ref, blocks_ref, out_ref,
    keys, values, score_a, score_b, row_max, summed, scalars,
):
    me = lax.axis_index("blk")
    slots, block = blocks_ref.shape[0], blocks_ref.shape[3]
    rows = projected_ref.shape[1]
    heads = pl.num_programs(0)
    depth = keys.shape[1]
    wide = values.shape[0]
    chunk = rows
    per_chunk = chunk // block
    chunks = slots // per_chunk
    before, live_rows = prefix_ref[me], new_ref[me]

    def rotated(index):
        start = pl.multiple_of(index * HD, HD)
        first = projected_ref[pl.ds(start, HD // 2), :]
        second = projected_ref[pl.ds(start + HD // 2, HD // 2), :]
        cosine, sine = cosine_ref[...], sine_ref[...]
        return jnp.concatenate(
            [first * cosine - second * sine, second * cosine + first * sine], axis=0
        )

    def padded_key(part, limit):
        spots = lax.broadcasted_iota(jnp.int32, (depth - HD, block), 1)
        lines = lax.broadcasted_iota(jnp.int32, (depth - HD, block), 0)
        bias = jnp.where((lines == 0) & (spots >= limit), FLOOR_SCORE, 0.0)
        return jnp.concatenate([part.astype(jnp.float32), bias], axis=0).T.astype(jnp.bfloat16)

    @pl.when(pl.program_id(0) == 0)
    def _():
        ones = jnp.ones((wide - HD, block), jnp.bfloat16)

        def clear(spot, carry):
            scalars[spot] = 0
            return carry

        lax.fori_loop(0, 2 * slots, clear, 0)
        sources = slots // CAP
        each = prompt_ref.shape[0] // sources

        def find(source, count):
            rank = jnp.int32(0)
            for spot in range(each):
                mine = prompt_ref[source * each + spot] == me
                target = source * CAP + jnp.minimum(rank, CAP - 1)

                @pl.when(mine)
                def _(target=target, count=count):
                    scalars[target] = count
                    scalars[slots + target] = 1

                rank = rank + mine.astype(jnp.int32)
                count = count + mine.astype(jnp.int32)
            return count

        lax.fori_loop(0, sources, find, jnp.int32(0))
        own_key = rotated(heads)
        own_value = projected_ref[(heads + 1) * HD : (heads + 2) * HD, :].astype(jnp.bfloat16)

        def place(slot, carry):
            limit = jnp.where(
                scalars[slots + slot] > 0, before - scalars[slot] * block, 0
            )
            spot = pl.multiple_of(slot * block, block)
            keys[pl.ds(spot, block), :] = padded_key(blocks_ref[slot, 0], limit)
            values[:, pl.ds(spot, block)] = jnp.concatenate([blocks_ref[slot, 1], ones], axis=0)
            return carry

        lax.fori_loop(0, slots, place, 0)
        for part in range(rows // block):
            near = slice(part * block, (part + 1) * block)
            far = slice(slots * block + part * block, slots * block + (part + 1) * block)
            keys[far, :] = padded_key(own_key[:, near], live_rows - part * block)
            values[:, far] = jnp.concatenate([own_value[:, near], ones], axis=0)

    query = jnp.concatenate(
        [
            rotated(pl.program_id(0)),
            jnp.ones((16, rows), jnp.float32),
            jnp.zeros((depth - HD - 16, rows), jnp.float32),
        ],
        axis=0,
    ).astype(jnp.bfloat16)

    def score(index, into):
        spot = pl.multiple_of(index * chunk, chunk)
        into[...] = jnp.dot(keys[pl.ds(spot, chunk), :], query, preferred_element_type=jnp.float32)

    def window(index, into):
        near = before + rows - WINDOW
        needed = False
        for part in range(per_chunk):
            needed |= scalars[index * per_chunk + part] * block < near

        @pl.when(needed)
        def _():
            for part in range(per_chunk):
                lines = slice(part * block, (part + 1) * block)
                place = scalars[index * per_chunk + part] * block + lax.broadcasted_iota(
                    jnp.int32, (block, rows), 0
                )
                away = before - place + lax.broadcasted_iota(jnp.int32, (block, rows), 1)
                seen = (away < WINDOW) | (place < SINKS)
                into[lines, :] = jnp.where(seen, into[lines, :], FLOOR_SCORE)

    def absorb(index, held):
        spot = pl.multiple_of(index * chunk, chunk)
        now = held[...]
        largest = jnp.maximum(row_max[...], jnp.max(now, axis=0, keepdims=True))
        fade = jnp.exp2((row_max[...] - largest) * LIFT)
        weights = jnp.exp2((now - largest) * LIFT).astype(jnp.bfloat16)
        row_max[...] = largest
        summed[...] = summed[...] * fade + jnp.dot(
            values[:, pl.ds(spot, chunk)], weights, preferred_element_type=jnp.float32
        )

    score(chunks, score_b)
    causal = lax.broadcasted_iota(jnp.int32, (rows, rows), 0) <= lax.broadcasted_iota(
        jnp.int32, (rows, rows), 1
    )
    score_b[...] = jnp.where(causal, score_b[...], FLOOR_SCORE)
    row_max[...] = jnp.full_like(row_max, FLOOR_SCORE)
    summed[...] = jnp.zeros_like(summed)
    score(0, score_a)
    absorb(chunks, score_b)
    window(0, score_a)

    def pair(step, carry):
        first = step * 2
        score(first + 1, score_b)
        absorb(first, score_a)
        window(first + 1, score_b)
        later = lax.rem(first + 2, chunks)
        score(later, score_a)
        absorb(first + 1, score_b)
        window(later, score_a)
        return carry

    lax.fori_loop(0, chunks // 2, pair, 0)
    out_ref[0] = (summed[:HD, :] / summed[HD : HD + 1, :]).astype(jnp.bfloat16)


def attend(heads, slot_prompt, prefix_len, new_len, projected, cosine, sine, blocks):
    rows = projected.shape[1]
    slots, _, width, block = blocks.shape
    span = slots * block + rows
    smem = pl.BlockSpec(memory_space=pltpu.SMEM)
    return pl.pallas_call(
        attention_kernel,
        name="attend",
        grid=(heads,),
        out_shape=jax.ShapeDtypeStruct((heads, width, rows), jnp.bfloat16),
        in_specs=[smem, smem, smem] + [VMEM_SPEC] * 4,
        out_specs=pl.BlockSpec((1, width, rows), lambda head: (head, 0, 0)),
        scratch_shapes=[
            pltpu.VMEM((span, 128), jnp.bfloat16),
            pltpu.VMEM((96, span), jnp.bfloat16),
            pltpu.VMEM((rows, rows), jnp.float32),
            pltpu.VMEM((rows, rows), jnp.float32),
            pltpu.VMEM((1, rows), jnp.float32),
            pltpu.VMEM((96, rows), jnp.float32),
            pltpu.SMEM((2 * slots,), jnp.int32),
        ],
        cost_estimate=pl.CostEstimate(
            flops=4 * heads * rows * span * 128,
            bytes_accessed=span * 4 * width,
            transcendentals=heads * rows * span,
        ),
    )(slot_prompt, prefix_len, new_len, projected, cosine, sine, blocks)


def hail(n, me):
    barrier = pltpu.get_barrier_semaphore()
    for step in range(1, n):
        peer = lax.rem(me + step, n)
        pl.semaphore_signal(barrier, inc=1, device_id={"kv": peer}, device_id_type=MESH)
    return barrier


class Links:
    def __init__(self, send, recv):
        self.send, self.recv, self.started = send, recv, []

    def go(self, source, target, peer, index):
        copy = pltpu.make_async_remote_copy(
            src_ref=source,
            dst_ref=target,
            send_sem=self.send.at[index],
            recv_sem=self.recv.at[index],
            device_id={"kv": peer},
            device_id_type=MESH,
        )
        copy.start()
        self.started.append(copy)
        return copy

    def close(self):
        for copy in self.started:
            copy.wait_send()


def z_steps(lines):
    return sorted(range(1, lines), key=lambda step: min(step, lines - step))


def as_float(ref):
    return ref[...].astype(jnp.float32)


class Scatter(Links):
    def __init__(self, n, me, view, landings, send, recv):
        super().__init__(send, recv)
        self.land_a, self.land_b, self.stage_a, self.stage_b, self.got_a, self.got_b = landings
        self.lines, self.me, self.view = n // 2, me, view
        self.z, self.y = lax.div(me, 2), lax.rem(me, 2)
        self.partner = 2 * self.z + 1 - self.y
        self.steps = z_steps(self.lines)

    def line(self, step):
        return 2 * lax.rem(self.z + step, self.lines)

    def open(self):
        lines = self.lines
        self.along = [
            self.go(
                self.view(self.line(step) + side, 0),
                self.land_a.at[step - 1, side],
                self.line(step) + self.y,
                2 * (step - 1) + side,
            )
            for step in self.steps
            for side in range(2)
        ]
        self.across = {
            step: self.go(
                self.view(self.line(step) + 1 - self.y, 1),
                self.land_b.at[step],
                self.partner,
                2 * (lines - 1) + step,
            )
            for step in self.steps + [0]
        }

    def forward(self):
        lines = self.lines
        self.last_b = []
        for step in self.steps:
            self.across[step].wait_recv()
            self.stage_b[step - 1] = (
                as_float(self.view(self.line(step) + self.y, 1)) + as_float(self.land_b.at[step])
            ).astype(jnp.bfloat16)
            self.last_b.append(
                self.go(
                    self.stage_b.at[step - 1],
                    self.got_b.at[step - 1],
                    self.line(step) + self.y,
                    3 * lines - 2 + step - 1,
                )
            )
        for copy in self.along:
            copy.wait_recv()
        self.stage_a[...] = self.gathered(1 - self.y).astype(jnp.bfloat16)
        self.last_a = self.go(self.stage_a, self.got_a, self.partner, 4 * lines - 3)

    def gathered(self, side):
        total = as_float(self.view(2 * self.z + side, 0))
        for step in range(self.lines - 1):
            total += as_float(self.land_a.at[step, side])
        return total

    def finish_a(self):
        self.last_a.wait_recv()
        return self.gathered(self.y) + as_float(self.got_a)

    def finish_b(self):
        self.across[0].wait_recv()
        total = as_float(self.view(self.me, 1)) + as_float(self.land_b.at[0])
        for copy in self.last_b:
            copy.wait_recv()
        for step in range(self.lines - 1):
            total += as_float(self.got_b.at[step])
        return total


def scatter_scratch(n, shape, copies=1):
    lines = n // 2
    sizes = [(lines - 1, 2), (lines,), (), (lines - 1,), (), (lines - 1,)]
    lead = () if copies == 1 else (copies,)
    return [pltpu.VMEM(lead + size + shape, jnp.bfloat16) for size in sizes] + [
        pltpu.SemaphoreType.DMA(lead + (4 * lines - 2,))
    ] * 2


def middle_kernel(
    n, piece_ref, token_ref, gain_ref, middle_ref, normed_ref,
    land_a, land_b, stage_a, stage_b, got_a, got_b, send, recv, whole, share, join,
):
    me = lax.axis_index("kv")
    part = piece_ref.shape[2]
    lines = n // 2
    barrier = hail(n, me)
    terms = Scatter(
        n, me, lambda k, h: piece_ref.at[k, h],
        (land_a, land_b, stage_a, stage_b, got_a, got_b), send, recv,
    )
    links = Links(share, join)
    pl.semaphore_wait(barrier, n - 1)
    terms.open()
    terms.forward()

    def rows_of(step, side, half):
        owner = 2 * lax.rem(terms.z + lines - step, lines) + lax.rem(terms.y + side, 2)
        return pl.ds(pl.multiple_of((owner * 2 + half) * part, part), part)

    def index_of(step, side, half):
        return (step * 2 + side) * 2 + half - 2

    came = {}

    def spread(held, slot, peer):
        came[slot] = [links.go(whole.at[held], whole.at[slot], peer, index_of(*slot))]

    def wait(slot):
        for copy in came[slot]:
            copy.wait_recv()

    def relay(side, half):
        came[2, side, half] = []
        for quarter, step in enumerate((1, 3)):
            held = pl.ds(quarter * (part // 2), part // 2)
            wait((step, side, half))
            came[2, side, half].append(
                links.go(
                    whole.at[step, side, half, held],
                    whole.at[2, side, half, held],
                    peer_at(step),
                    index_of(2, side, half) if quarter == 0 else 2 * n - 2 + side + half,
                )
            )

    def settle(slot):
        place = rows_of(*slot)
        middle_rows = whole[slot]
        middle_ref[place, :] = middle_rows
        values = middle_rows.astype(jnp.float32)
        mean_square = jnp.mean(values * values, axis=-1, keepdims=True)
        normed_ref[place, :] = (
            values * lax.rsqrt(mean_square + EPSILON) * gain_ref[...]
        ).astype(jnp.bfloat16)

    def peer_at(step):
        return terms.line(step) + terms.y

    own_a = token_ref[rows_of(0, 0, 0), :].astype(jnp.float32)
    whole[0, 0, 0] = (own_a + terms.finish_a()).astype(jnp.bfloat16)
    for step in (1, 3):
        spread((0, 0, 0), (step, 0, 0), peer_at(step))
    spread((0, 0, 0), (0, 1, 0), terms.partner)
    own_b = token_ref[rows_of(0, 0, 1), :].astype(jnp.float32)
    whole[0, 0, 1] = (own_b + terms.finish_b()).astype(jnp.bfloat16)
    spread((0, 0, 1), (0, 1, 1), terms.partner)
    for step in (1, 3):
        spread((0, 0, 1), (step, 0, 1), peer_at(step))
    settle((0, 0, 0))
    relay(0, 0)
    for step in (1, 3):
        spread((step, 0, 0), (step, 1, 0), terms.partner)
    wait((0, 1, 1))
    for step in (1, 3):
        spread((0, 1, 1), (step, 1, 1), peer_at(step))
    relay(0, 1)
    wait((2, 0, 0))
    spread((2, 0, 0), (2, 1, 0), terms.partner)
    settle((0, 0, 1))
    settle((0, 1, 1))
    relay(1, 1)
    for step in (1, 3, 2):
        settle((step, 0, 0))
    wait((0, 1, 0))
    settle((0, 1, 0))
    settle((1, 0, 1))
    settle((3, 0, 1))
    settle((1, 1, 1))
    settle((3, 1, 1))
    for slot in ((2, 0, 1), (1, 1, 0), (3, 1, 0), (2, 1, 1), (2, 1, 0)):
        wait(slot)
        settle(slot)
    terms.close()
    links.close()


def sum_middle(n, partial_out, tokens, mlp_gain):
    rows, width = tokens.shape
    piece = rows // n
    whole_shape = jax.ShapeDtypeStruct((rows, width), jnp.bfloat16)
    return pl.pallas_call(
        functools.partial(middle_kernel, n),
        name="sum_middle",
        cost_estimate=pl.CostEstimate(flops=0, bytes_accessed=200_000_000, transcendentals=0),
        out_shape=(whole_shape, whole_shape),
        in_specs=[VMEM_SPEC] * 3,
        out_specs=(VMEM_SPEC, VMEM_SPEC),
        scratch_shapes=scatter_scratch(n, (piece // 2, width))
        + [pltpu.VMEM((n // 2, 2, 2, piece // 2, width), jnp.bfloat16)]
        + [pltpu.SemaphoreType.DMA((2 * n + 1,))] * 2,
        compiler_params=pltpu.CompilerParams(collective_id=0, has_side_effects=True),
    )(partial_out.reshape(n, 2, piece // 2, width), tokens, mlp_gain.reshape(1, width))


def hidden_kernel(
    n, normed_ref, middle_hbm, pair_hbm, down_hbm, out_ref, pair, down, hidden, terms,
    window, turned, pair_sem, swap_send, swap_recv, down_sem, window_sem,
    land_a, land_b, stage_a, stage_b, got_a, got_b, send, recv,
):
    me = lax.axis_index("kv")
    rows, width = normed_ref.shape
    halves, part = terms.shape[0], terms.shape[2]
    piece = width // n
    tiles = pair.shape[3] // 256
    blk = lax.axis_index("blk")
    core = lax.rem(blk, 2)
    sibling = blk + 1 - 2 * core
    units = down.shape[0]
    barrier = hail(n, me)
    pl.semaphore_signal(barrier, inc=1, device_id={"blk": sibling}, device_id_type=MESH)

    def bring(tile):
        lanes = pl.ds(pl.multiple_of(tile * 256, 256), 256)
        return pltpu.make_async_copy(
            pair_hbm.at[:, :, lanes], pair.at[:, core, :, lanes], pair_sem.at[tile]
        )

    def swap(tile):
        lanes = pl.ds(pl.multiple_of(tile * 256, 256), 256)
        return pltpu.make_async_remote_copy(
            src_ref=pair_hbm.at[:, :, lanes],
            dst_ref=pair.at[:, core, :, lanes],
            send_sem=swap_send.at[tile],
            recv_sem=swap_recv.at[tile],
            device_id={"blk": sibling},
            device_id_type=MESH,
        )

    for tile in range(tiles):
        bring(tile).start()
    pl.semaphore_wait(barrier, n)
    for tile in range(tiles):
        swap(tile).start()
    fetch = pltpu.make_async_copy(down_hbm, down, down_sem)
    fetch.start()
    left = lax.div(me * piece, 128) * 128
    view = pltpu.make_async_copy(
        middle_hbm.at[:, pl.ds(pl.multiple_of(left, 128), window.shape[1])], window, window_sem
    )
    view.start()

    def exchange(half):
        def term(owner, side):
            start = pl.multiple_of(owner * piece + side * (piece // 2), piece // 2)
            return terms.at[half, pl.ds(start, piece // 2)]

        landings = [ref.at[half] for ref in (land_a, land_b, stage_a, stage_b, got_a, got_b)]
        return Scatter(n, me, term, landings, send.at[half], recv.at[half])

    sums = [exchange(half) for half in range(halves)]
    for half in range(halves):
        lines = slice(half * part, (half + 1) * part)

        @pl.loop(0, tiles)
        def _(tile):
            if half == 0:
                bring(tile).wait()
                swap(tile).wait()
            lanes = pl.ds(pl.multiple_of(tile * 256, 256), 256)
            both = jnp.dot(
                normed_ref[lines, :],
                pair[:, :, :, lanes].reshape(width, 256),
                preferred_element_type=jnp.float32,
            )
            gate, up = both[:, :128], both[:, 128:]
            hidden[:, pl.ds(pl.multiple_of(tile * 128, 128), 128)] = (
                gate / (1.0 + jnp.exp(-gate)) * up
            ).astype(jnp.bfloat16)

        if half == 0:
            fetch.wait()

        @pl.loop(0, width // 512)
        def _(tile):
            spot = pl.ds(pl.multiple_of(tile * 512, 512), 512)
            term = jnp.dot(
                hidden[:, :units], down[:, spot], preferred_element_type=jnp.float32
            )
            terms[half, spot, :] = term.T.astype(jnp.bfloat16)

        sums[half].open()
    view.wait()
    turned[...] = window[...].astype(jnp.float32).T
    for half in range(halves):
        sums[half].forward()
    shift = me * piece - left
    for half in range(halves):
        lines = slice(half * part, (half + 1) * part)
        for side, finish in enumerate((sums[half].finish_a, sums[half].finish_b)):
            residual = pl.ds(pl.multiple_of(shift + side * (piece // 2), 32), piece // 2)
            place = slice(side * (piece // 2), (side + 1) * (piece // 2))
            out_ref[place, lines] = turned[residual, lines] + finish()
    for half in range(halves):
        sums[half].close()


def feed_forward(n, normed_mid, middle, w_pair, w_down):
    rows, width = normed_mid.shape
    halves = 2
    part = rows // halves
    piece = width // n
    half = jnp.bfloat16
    dma = pltpu.SemaphoreType.DMA
    any_spec = pl.BlockSpec(memory_space=pl.ANY)
    return pl.pallas_call(
        functools.partial(hidden_kernel, n),
        name="feed_forward",
        out_shape=jax.ShapeDtypeStruct((piece, rows), jnp.float32),
        in_specs=[VMEM_SPEC, any_spec, any_spec, any_spec],
        out_specs=VMEM_SPEC,
        scratch_shapes=[
            pltpu.VMEM((w_pair.shape[0], 2) + w_pair.shape[1:], half),
            pltpu.VMEM(w_down.shape, half),
            pltpu.VMEM((part, w_pair.shape[2] // 2), half),
            pltpu.VMEM((halves, width, part), half),
            pltpu.VMEM((rows, piece + 64), half),
            pltpu.VMEM((piece + 64, rows), jnp.float32),
            dma((w_pair.shape[2] // 256,)),
            dma((w_pair.shape[2] // 256,)),
            dma((w_pair.shape[2] // 256,)),
            dma,
            dma,
        ]
        + scatter_scratch(n, (piece // 2, part), halves),
        compiler_params=pltpu.CompilerParams(
            collective_id=1, has_side_effects=True, vmem_limit_bytes=56 * 1024 * 1024
        ),
    )(normed_mid, middle, w_pair, w_down)


def pack_pairs(first, second, groups):
    rows, columns = first.shape
    units = columns // groups
    padded = -(-units // 128) * 128
    tiles = [
        jnp.pad(
            matrix.astype(jnp.bfloat16).reshape(rows, groups, units),
            ((0, 0), (0, 0), (0, padded - units)),
        ).reshape(rows, groups, -1, 1, 128)
        for matrix in (first, second)
    ]
    return jnp.transpose(jnp.concatenate(tiles, axis=3), (1, 0, 2, 3, 4)).reshape(groups, rows, -1)


def shards(
    tokens,
    attn_gain,
    mlp_gain,
    w_query,
    w_key,
    w_value,
    w_gate,
    w_up,
    w_out,
    w_down,
    cache,
    slot_prompt,
    prefix_len,
    new_len,
):
    groups = lax.axis_size("kv")
    n_blocks = lax.axis_size("blk")
    blk_index = lax.axis_index("blk")
    new_rows = tokens.shape[0]
    prompts = prefix_len.shape[0]
    slots = cache.shape[1]
    row_ids = jnp.arange(new_rows, dtype=jnp.int32)
    frequency = ROPE_BASE ** (-2.0 * jnp.arange(HD // 2, dtype=jnp.float32) / HD)
    positions = (prefix_len[blk_index] + row_ids).astype(jnp.float32)
    angles = positions[None, :] * frequency[:, None]
    own_prompts = lax.dynamic_slice_in_dim(slot_prompt, blk_index * slots, slots)
    earlier = jnp.tri(slots, k=-1, dtype=jnp.bool_)
    own_ranks = jnp.sum(
        ((own_prompts[:, None] == own_prompts[None, :]) & earlier).astype(jnp.int32), axis=1
    )
    own_slots = jnp.arange(slots, dtype=jnp.int32)
    wanted = jnp.arange(prompts + 1, dtype=jnp.int32)[:, None]
    matches = jnp.where(
        wanted < prompts,
        (own_prompts[None, :] == wanted) & (own_ranks[None, :] == 0),
        own_ranks[None, :] == 1,
    )
    source_slot = jnp.sum(jnp.where(matches, own_slots[None, :], 0), axis=1)
    by_slot = jnp.transpose(cache.reshape(2, slots, HD, BLOCK), (1, 0, 2, 3))
    outgoing = jnp.take(by_slot, source_slot, axis=0, mode="clip")
    projected, w_second, arrived = regroup(
        groups,
        n_blocks,
        pack_groups((w_query, w_key, w_value), groups),
        pack_pairs(w_gate, w_up, groups),
        outgoing[:prompts],
        outgoing[prompts],
        tokens,
        attn_gain,
    )
    same_core = [list(range(core, n_blocks, 2)) for core in range(2)]
    w_pair = lax.all_gather(w_second, "blk", axis=0, axis_index_groups=same_core)
    attended = attend(
        HEADS // groups,
        slot_prompt,
        prefix_len,
        new_len,
        projected,
        jnp.cos(angles),
        jnp.sin(angles),
        arrived.reshape(prompts * CAP, 2, HD, BLOCK),
    ).reshape(-1, new_rows)
    projected_out = lax.dot_general(
        attended, w_out, (((0,), (0,)), ((), ())), preferred_element_type=jnp.float32
    )
    partial_out = projected_out.astype(jnp.bfloat16)
    middle, normed_mid = sum_middle(groups, partial_out, tokens, mlp_gain)
    summed = feed_forward(groups, normed_mid, middle, w_pair, w_down).T
    mixed = jnp.where((row_ids < new_len[blk_index])[:, None], summed, 0.0)
    return mixed.astype(jnp.bfloat16)


def solution(mesh):
    return jax.shard_map(
        shards,
        mesh=mesh,
        in_specs=(
            P("blk", None),
            P(),
            P(),
            P(("blk", "kv"), None),
            P(("blk", "kv"), None),
            P(("blk", "kv"), None),
            P(("blk", "kv"), None),
            P(("blk", "kv"), None),
            P("kv", None),
            P("kv", None),
            P(None, "blk", "kv", None, None),
            P(),
            P(),
            P(),
        ),
        out_specs=P("blk", "kv"),
        check_vma=False,
    )
```

```python
import functools
import math

import jax
import jax.numpy as jnp
from jax import lax
from jax.experimental import pallas as pl
from jax.experimental.pallas import tpu as pltpu
from jax.sharding import PartitionSpec as P

HEADS = 32
KV_HEADS = 8
HD = 80
WINDOW = 4096
SINKS = 4
BLOCK = 128
CAP = 2


FLOOR_SCORE = -1e30
EPSILON = 1e-05
ROPE_BASE = 10000.0


def pack_groups(matrices, groups):
    rows = matrices[0].shape[0]
    pieces = [
        jnp.transpose(
            matrix.astype(jnp.bfloat16).reshape(rows, groups, matrix.shape[1] // groups), (1, 0, 2)
        )
        for matrix in matrices
    ]
    return jnp.concatenate(pieces, axis=2)


MESH = pl.DeviceIdType.MESH
VMEM_SPEC = pl.BlockSpec(memory_space=pltpu.VMEM)


def fan_out(step_count, make):
    copies = [make(step) for step in range(1, step_count)]
    for copy in copies:
        copy.start()
    return copies


def regroup_kernel(
    n_kv, n_blk, first_ref, second_ref, cache_ref, extra_ref, token_ref, gain_ref,
    projected_ref, second_out, cache_out,
    first_in, second_in, cache_in, whole, extra, normed, weights, stage_a, stage_b,
    first_send, first_recv, second_send, second_recv, cache_send, cache_recv, send, recv,
    extra_send, extra_recv,
):
    me_kv, me = lax.axis_index("kv"), lax.axis_index("blk")
    rows = first_ref.shape[1]
    half, line, core = lax.div(me, 8), lax.rem(lax.div(me, 2), 4), lax.rem(me, 2)

    barrier = pltpu.get_barrier_semaphore()
    for axis, count, mine in (("kv", n_kv, me_kv), ("blk", n_blk, me)):
        for step in range(1, count):
            pl.semaphore_signal(
                barrier, inc=1, device_id={axis: lax.rem(mine + step, count)}, device_id_type=MESH
            )
    pl.semaphore_wait(barrier, n_kv + n_blk - 2)

    def swap(source, landing, sent, got):
        def make(step):
            peer = lax.rem(me_kv + step, n_kv)
            return pltpu.make_async_remote_copy(
                src_ref=source.at[peer],
                dst_ref=landing.at[me_kv],
                send_sem=sent.at[step - 1],
                recv_sem=got.at[step - 1],
                device_id={"kv": peer},
                device_id_type=MESH,
            )

        return fan_out(n_kv, make)

    def deal(step):
        peer = lax.rem(me + step, n_blk)
        return pltpu.make_async_remote_copy(
            src_ref=cache_ref.at[peer],
            dst_ref=cache_in.at[step - 1],
            send_sem=cache_send.at[step - 1],
            recv_sem=cache_recv.at[step - 1],
            device_id={"blk": peer},
            device_id_type=MESH,
        )

    firsts = swap(first_ref, first_in, first_send, first_recv)
    first_in[me_kv] = first_ref[me_kv]
    for copy in firsts:
        copy.wait_recv()
    for group in range(n_kv):
        stage_a[group * rows : (group + 1) * rows, :] = first_in[group].astype(jnp.float32)
    whole[0] = stage_a[...].astype(jnp.bfloat16)

    extra[0] = extra_ref[...]

    passed, passed_extra = {}, {}

    def pass_extra(held, peer, slot):
        copy = pltpu.make_async_remote_copy(
            src_ref=extra.at[held],
            dst_ref=extra.at[slot],
            send_sem=extra_send.at[slot - 1],
            recv_sem=extra_recv.at[slot - 1],
            device_id={"blk": peer},
            device_id_type=MESH,
        )
        copy.start()
        passed_extra[slot] = copy

    def pass_on(held, peer, slot):
        copy = pltpu.make_async_remote_copy(
            src_ref=whole.at[held],
            dst_ref=whole.at[slot],
            send_sem=send.at[slot - 1],
            recv_sem=recv.at[slot - 1],
            device_id={"blk": peer},
            device_id_type=MESH,
        )
        copy.start()
        passed[slot] = copy

    def along(step):
        return half * 8 + lax.rem(line + step, 4) * 2 + core

    across = lax.rem(me + 8, n_blk)
    sibling = me + 1 - 2 * core
    near_rows = whole.shape[1] // 2
    relayed = []

    def relay(base):
        for part, step in enumerate((1, 3)):
            lines = pl.ds(part * near_rows, near_rows)
            index = n_blk - 1 + base // 4 + part
            passed[base + 2 * step].wait_recv()
            copy = pltpu.make_async_remote_copy(
                src_ref=whole.at[base + 2 * step, lines],
                dst_ref=whole.at[base + 4, lines],
                send_sem=send.at[index],
                recv_sem=recv.at[index],
                device_id={"blk": along(step)},
                device_id_type=MESH,
            )
            copy.start()
            relayed.append(copy)

    pass_on(0, across, 8)
    for step in (1, 3):
        pass_on(0, along(step), 2 * step)
    pass_on(0, sibling, 1)
    seconds = swap(second_ref, second_in, second_send, second_recv)

    @pl.loop(0, token_ref.shape[0] // 64)
    def _(part):
        lines = pl.ds(pl.multiple_of(part * 64, 64), 64)
        values = token_ref[lines, :].astype(jnp.float32)
        mean_square = jnp.mean(values * values, axis=-1, keepdims=True)
        normed[lines, :] = (
            values * lax.rsqrt(mean_square + EPSILON) * gain_ref[...]
        ).astype(jnp.bfloat16)

    passed[8].wait_recv()
    for step in (1, 3):
        pass_on(8, along(step), 8 + 2 * step)
    pass_on(8, sibling, 9)
    relay(0)
    for step in (1, 3):
        pass_on(2 * step, sibling, 2 * step + 1)
    relay(8)
    deals = fan_out(n_blk, deal)
    pass_extra(0, across, 8)
    for step in (1, 3, 2):
        pass_extra(0, along(step), 2 * step)
    pass_extra(0, sibling, 1)

    for step in (1, 3):
        pass_on(8 + 2 * step, sibling, 9 + 2 * step)
    for base in (0, 8):
        for copy in relayed[base // 4 : base // 4 + 2]:
            copy.wait_recv()
        pass_on(base + 4, sibling, base + 5)
    second_in[me_kv] = second_ref[me_kv]
    for copy in seconds:
        copy.wait_recv()
    for group in range(n_kv):
        stage_b[group * rows : (group + 1) * rows, :] = second_in[group].astype(jnp.float32)
    second_out[...] = stage_b[...].astype(jnp.bfloat16)
    passed_extra[8].wait_recv()
    for step in (1, 3, 2):
        pass_extra(8, along(step), 8 + 2 * step)
    pass_extra(8, sibling, 9)

    def owner_of(base, step, other):
        return (
            lax.rem(half + base // 8, 2) * 8
            + lax.rem(line + 4 - step, 4) * 2
            + lax.rem(core + other, 2)
        )

    tall = whole.shape[1]
    for base in (0, 8):
        for step in range(4):
            for other in range(2):
                slot = base + 2 * step + other
                if other:
                    passed[slot].wait_recv()
                place = pl.multiple_of(owner_of(base, step, other) * tall, tall)
                weights[pl.ds(place, tall), :] = whole[slot]

    @pl.loop(0, normed.shape[0] // 128)
    def _(part):
        lines = pl.ds(pl.multiple_of(part * 128, 128), 128)
        projected_ref[:, lines] = jnp.dot(
            normed[lines, :], weights[...], preferred_element_type=jnp.float32
        ).T

    for base in (0, 8):
        for step in (1, 3, 2):
            slot = base + 2 * step
            passed_extra[slot].wait_recv()
            pass_extra(slot, sibling, slot + 1)
    for base in (0, 8):
        for step in range(4):
            for other in range(2):
                slot = base + 2 * step + other
                if other:
                    passed_extra[slot].wait_recv()
                cache_out[owner_of(base, step, other), 1] = extra[slot]
    cache_out[me, 0] = cache_ref[me]
    for step in range(1, n_blk):
        deals[step - 1].wait_recv()
        cache_out[lax.rem(me + n_blk - step, n_blk), 0] = cache_in[step - 1]
    for copy in firsts + seconds + deals + [*passed.values(), *passed_extra.values()] + relayed:
        copy.wait_send()


def regroup(n_kv, n_blk, first, second, cached, extra, tokens, gain):
    rows = first.shape[1]
    tall = n_kv * rows
    first_width, second_width = first.shape[2], second.shape[2]
    half = jnp.bfloat16
    dma = pltpu.SemaphoreType.DMA
    blocks = (n_blk, 2) + cached.shape[1:]
    return pl.pallas_call(
        functools.partial(regroup_kernel, n_kv, n_blk),
        name="regroup",
        out_shape=(
            jax.ShapeDtypeStruct((first_width, tokens.shape[0]), jnp.float32),
            jax.ShapeDtypeStruct((tall, second_width), half),
            jax.ShapeDtypeStruct(blocks, half),
        ),
        in_specs=[VMEM_SPEC] * 6,
        out_specs=(VMEM_SPEC,) * 3,
        scratch_shapes=[
            pltpu.VMEM(first.shape, half),
            pltpu.VMEM(second.shape, half),
            pltpu.VMEM((n_blk - 1,) + cached.shape[1:], half),
            pltpu.VMEM((n_blk, tall, first_width), half),
            pltpu.VMEM((n_blk,) + extra.shape, half),
            pltpu.VMEM(tokens.shape, half),
            pltpu.VMEM((n_blk * tall, first_width), half),
            pltpu.VMEM((tall, first_width), jnp.float32),
            pltpu.VMEM((tall, second_width), jnp.float32),
        ]
        + [dma((n_kv - 1,))] * 4
        + [dma((n_blk - 1,))] * 2
        + [dma((n_blk + 3,))] * 2
        + [dma((n_blk - 1,))] * 2,
        compiler_params=pltpu.CompilerParams(collective_id=2, has_side_effects=True),
    )(first, second, cached, extra, tokens, gain.reshape(1, -1))


LIFT = 1.0 / math.sqrt(HD) * math.log2(math.e)


def attention_kernel(
    prompt_ref, prefix_ref, new_ref, projected_ref, cosine_ref, sine_ref, blocks_ref, out_ref,
    keys, values, score_a, score_b, row_max, summed, scalars,
):
    me = lax.axis_index("blk")
    slots, block = blocks_ref.shape[0], blocks_ref.shape[3]
    rows = projected_ref.shape[1]
    heads = pl.num_programs(0)
    depth = keys.shape[1]
    wide = values.shape[0]
    chunk = rows
    per_chunk = chunk // block
    chunks = slots // per_chunk
    before, live_rows = prefix_ref[me], new_ref[me]

    def rotated(index):
        start = pl.multiple_of(index * HD, HD)
        first = projected_ref[pl.ds(start, HD // 2), :]
        second = projected_ref[pl.ds(start + HD // 2, HD // 2), :]
        cosine, sine = cosine_ref[...], sine_ref[...]
        return jnp.concatenate(
            [first * cosine - second * sine, second * cosine + first * sine], axis=0
        )

    def padded_key(part, limit):
        spots = lax.broadcasted_iota(jnp.int32, (depth - HD, block), 1)
        lines = lax.broadcasted_iota(jnp.int32, (depth - HD, block), 0)
        bias = jnp.where((lines == 0) & (spots >= limit), FLOOR_SCORE, 0.0)
        return jnp.concatenate([part.astype(jnp.float32), bias], axis=0).T.astype(jnp.bfloat16)

    @pl.when(pl.program_id(0) == 0)
    def _():
        ones = jnp.ones((wide - HD, block), jnp.bfloat16)

        def clear(spot, carry):
            scalars[spot] = 0
            return carry

        lax.fori_loop(0, 2 * slots, clear, 0)
        sources = slots // CAP
        each = prompt_ref.shape[0] // sources

        def find(source, count):
            rank = jnp.int32(0)
            for spot in range(each):
                mine = prompt_ref[source * each + spot] == me
                target = source * CAP + jnp.minimum(rank, CAP - 1)

                @pl.when(mine)
                def _(target=target, count=count):
                    scalars[target] = count
                    scalars[slots + target] = 1

                rank = rank + mine.astype(jnp.int32)
                count = count + mine.astype(jnp.int32)
            return count

        lax.fori_loop(0, sources, find, jnp.int32(0))
        own_key = rotated(heads)
        own_value = projected_ref[(heads + 1) * HD : (heads + 2) * HD, :].astype(jnp.bfloat16)

        def place(slot, carry):
            limit = jnp.where(
                scalars[slots + slot] > 0, before - scalars[slot] * block, 0
            )
            spot = pl.multiple_of(slot * block, block)
            keys[pl.ds(spot, block), :] = padded_key(blocks_ref[slot, 0], limit)
            values[:, pl.ds(spot, block)] = jnp.concatenate([blocks_ref[slot, 1], ones], axis=0)
            return carry

        lax.fori_loop(0, slots, place, 0)
        for part in range(rows // block):
            near = slice(part * block, (part + 1) * block)
            far = slice(slots * block + part * block, slots * block + (part + 1) * block)
            keys[far, :] = padded_key(own_key[:, near], live_rows - part * block)
            values[:, far] = jnp.concatenate([own_value[:, near], ones], axis=0)

    query = jnp.concatenate(
        [
            rotated(pl.program_id(0)),
            jnp.ones((16, rows), jnp.float32),
            jnp.zeros((depth - HD - 16, rows), jnp.float32),
        ],
        axis=0,
    ).astype(jnp.bfloat16)

    def score(index, into):
        spot = pl.multiple_of(index * chunk, chunk)
        into[...] = jnp.dot(keys[pl.ds(spot, chunk), :], query, preferred_element_type=jnp.float32)

    def window(index, into):
        near = before + rows - WINDOW
        needed = False
        for part in range(per_chunk):
            needed |= scalars[index * per_chunk + part] * block < near

        @pl.when(needed)
        def _():
            for part in range(per_chunk):
                lines = slice(part * block, (part + 1) * block)
                place = scalars[index * per_chunk + part] * block + lax.broadcasted_iota(
                    jnp.int32, (block, rows), 0
                )
                away = before - place + lax.broadcasted_iota(jnp.int32, (block, rows), 1)
                seen = (away < WINDOW) | (place < SINKS)
                into[lines, :] = jnp.where(seen, into[lines, :], FLOOR_SCORE)

    def absorb(index, held):
        spot = pl.multiple_of(index * chunk, chunk)
        now = held[...]
        largest = jnp.maximum(row_max[...], jnp.max(now, axis=0, keepdims=True))
        fade = jnp.exp2((row_max[...] - largest) * LIFT)
        weights = jnp.exp2((now - largest) * LIFT).astype(jnp.bfloat16)
        row_max[...] = largest
        summed[...] = summed[...] * fade + jnp.dot(
            values[:, pl.ds(spot, chunk)], weights, preferred_element_type=jnp.float32
        )

    score(chunks, score_b)
    causal = lax.broadcasted_iota(jnp.int32, (rows, rows), 0) <= lax.broadcasted_iota(
        jnp.int32, (rows, rows), 1
    )
    score_b[...] = jnp.where(causal, score_b[...], FLOOR_SCORE)
    row_max[...] = jnp.full_like(row_max, FLOOR_SCORE)
    summed[...] = jnp.zeros_like(summed)
    score(0, score_a)
    absorb(chunks, score_b)
    window(0, score_a)

    def pair(step, carry):
        first = step * 2
        score(first + 1, score_b)
        absorb(first, score_a)
        window(first + 1, score_b)
        later = lax.rem(first + 2, chunks)
        score(later, score_a)
        absorb(first + 1, score_b)
        window(later, score_a)
        return carry

    lax.fori_loop(0, chunks // 2, pair, 0)
    out_ref[0] = (summed[:HD, :] / summed[HD : HD + 1, :]).astype(jnp.bfloat16)


def attend(heads, slot_prompt, prefix_len, new_len, projected, cosine, sine, blocks):
    rows = projected.shape[1]
    slots, _, width, block = blocks.shape
    span = slots * block + rows
    smem = pl.BlockSpec(memory_space=pltpu.SMEM)
    return pl.pallas_call(
        attention_kernel,
        name="attend",
        grid=(heads,),
        out_shape=jax.ShapeDtypeStruct((heads, width, rows), jnp.bfloat16),
        in_specs=[smem, smem, smem] + [VMEM_SPEC] * 4,
        out_specs=pl.BlockSpec((1, width, rows), lambda head: (head, 0, 0)),
        scratch_shapes=[
            pltpu.VMEM((span, 128), jnp.bfloat16),
            pltpu.VMEM((96, span), jnp.bfloat16),
            pltpu.VMEM((rows, rows), jnp.float32),
            pltpu.VMEM((rows, rows), jnp.float32),
            pltpu.VMEM((1, rows), jnp.float32),
            pltpu.VMEM((96, rows), jnp.float32),
            pltpu.SMEM((2 * slots,), jnp.int32),
        ],
        cost_estimate=pl.CostEstimate(
            flops=4 * heads * rows * span * 128,
            bytes_accessed=span * 4 * width,
            transcendentals=heads * rows * span,
        ),
    )(slot_prompt, prefix_len, new_len, projected, cosine, sine, blocks)


def hail(n, me):
    barrier = pltpu.get_barrier_semaphore()
    for step in range(1, n):
        peer = lax.rem(me + step, n)
        pl.semaphore_signal(barrier, inc=1, device_id={"kv": peer}, device_id_type=MESH)
    return barrier


class Links:
    def __init__(self, send, recv):
        self.send, self.recv, self.started = send, recv, []

    def go(self, source, target, peer, index):
        copy = pltpu.make_async_remote_copy(
            src_ref=source,
            dst_ref=target,
            send_sem=self.send.at[index],
            recv_sem=self.recv.at[index],
            device_id={"kv": peer},
            device_id_type=MESH,
        )
        copy.start()
        self.started.append(copy)
        return copy

    def close(self):
        for copy in self.started:
            copy.wait_send()


def z_steps(lines):
    return sorted(range(1, lines), key=lambda step: min(step, lines - step))


def as_float(ref):
    return ref[...].astype(jnp.float32)


class Scatter(Links):
    def __init__(self, n, me, view, landings, send, recv):
        super().__init__(send, recv)
        self.land_a, self.land_b, self.stage_a, self.stage_b, self.got_a, self.got_b = landings
        self.lines, self.me, self.view = n // 2, me, view
        self.z, self.y = lax.div(me, 2), lax.rem(me, 2)
        self.partner = 2 * self.z + 1 - self.y
        self.steps = z_steps(self.lines)

    def line(self, step):
        return 2 * lax.rem(self.z + step, self.lines)

    def open(self):
        lines = self.lines
        self.along = [
            self.go(
                self.view(self.line(step) + side, 0),
                self.land_a.at[step - 1, side],
                self.line(step) + self.y,
                2 * (step - 1) + side,
            )
            for step in self.steps
            for side in range(2)
        ]
        self.across = {
            step: self.go(
                self.view(self.line(step) + 1 - self.y, 1),
                self.land_b.at[step],
                self.partner,
                2 * (lines - 1) + step,
            )
            for step in self.steps + [0]
        }

    def forward(self):
        lines = self.lines
        self.last_b = []
        for step in self.steps:
            self.across[step].wait_recv()
            self.stage_b[step - 1] = (
                as_float(self.view(self.line(step) + self.y, 1)) + as_float(self.land_b.at[step])
            ).astype(jnp.bfloat16)
            self.last_b.append(
                self.go(
                    self.stage_b.at[step - 1],
                    self.got_b.at[step - 1],
                    self.line(step) + self.y,
                    3 * lines - 2 + step - 1,
                )
            )
        for copy in self.along:
            copy.wait_recv()
        self.stage_a[...] = self.gathered(1 - self.y).astype(jnp.bfloat16)
        self.last_a = self.go(self.stage_a, self.got_a, self.partner, 4 * lines - 3)

    def gathered(self, side):
        total = as_float(self.view(2 * self.z + side, 0))
        for step in range(self.lines - 1):
            total += as_float(self.land_a.at[step, side])
        return total

    def finish_a(self):
        self.last_a.wait_recv()
        return self.gathered(self.y) + as_float(self.got_a)

    def finish_b(self):
        self.across[0].wait_recv()
        total = as_float(self.view(self.me, 1)) + as_float(self.land_b.at[0])
        for copy in self.last_b:
            copy.wait_recv()
        for step in range(self.lines - 1):
            total += as_float(self.got_b.at[step])
        return total


def scatter_scratch(n, shape, copies=1):
    lines = n // 2
    sizes = [(lines - 1, 2), (lines,), (), (lines - 1,), (), (lines - 1,)]
    lead = () if copies == 1 else (copies,)
    return [pltpu.VMEM(lead + size + shape, jnp.bfloat16) for size in sizes] + [
        pltpu.SemaphoreType.DMA(lead + (4 * lines - 2,))
    ] * 2


def middle_kernel(
    n, piece_ref, token_ref, gain_ref, middle_ref, normed_ref,
    land_a, land_b, stage_a, stage_b, got_a, got_b, send, recv, whole, share, join,
):
    me = lax.axis_index("kv")
    part = piece_ref.shape[2]
    lines = n // 2
    barrier = hail(n, me)
    terms = Scatter(
        n, me, lambda k, h: piece_ref.at[k, h],
        (land_a, land_b, stage_a, stage_b, got_a, got_b), send, recv,
    )
    links = Links(share, join)
    pl.semaphore_wait(barrier, n - 1)
    terms.open()
    terms.forward()

    def rows_of(step, side, half):
        owner = 2 * lax.rem(terms.z + lines - step, lines) + lax.rem(terms.y + side, 2)
        return pl.ds(pl.multiple_of((owner * 2 + half) * part, part), part)

    def index_of(step, side, half):
        return (step * 2 + side) * 2 + half - 2

    came = {}

    def spread(held, slot, peer):
        came[slot] = [links.go(whole.at[held], whole.at[slot], peer, index_of(*slot))]

    def wait(slot):
        for copy in came[slot]:
            copy.wait_recv()

    def relay(side, half):
        came[2, side, half] = []
        for quarter, step in enumerate((1, 3)):
            held = pl.ds(quarter * (part // 2), part // 2)
            wait((step, side, half))
            came[2, side, half].append(
                links.go(
                    whole.at[step, side, half, held],
                    whole.at[2, side, half, held],
                    peer_at(step),
                    index_of(2, side, half) if quarter == 0 else 2 * n - 2 + side + half,
                )
            )

    def settle(slot):
        place = rows_of(*slot)
        middle_rows = whole[slot]
        middle_ref[place, :] = middle_rows
        values = middle_rows.astype(jnp.float32)
        mean_square = jnp.mean(values * values, axis=-1, keepdims=True)
        normed_ref[place, :] = (
            values * lax.rsqrt(mean_square + EPSILON) * gain_ref[...]
        ).astype(jnp.bfloat16)

    def peer_at(step):
        return terms.line(step) + terms.y

    own_a = token_ref[rows_of(0, 0, 0), :].astype(jnp.float32)
    whole[0, 0, 0] = (own_a + terms.finish_a()).astype(jnp.bfloat16)
    for step in (1, 3):
        spread((0, 0, 0), (step, 0, 0), peer_at(step))
    spread((0, 0, 0), (0, 1, 0), terms.partner)
    own_b = token_ref[rows_of(0, 0, 1), :].astype(jnp.float32)
    whole[0, 0, 1] = (own_b + terms.finish_b()).astype(jnp.bfloat16)
    spread((0, 0, 1), (0, 1, 1), terms.partner)
    for step in (1, 3):
        spread((0, 0, 1), (step, 0, 1), peer_at(step))
    settle((0, 0, 0))
    relay(0, 0)
    for step in (1, 3):
        spread((step, 0, 0), (step, 1, 0), terms.partner)
    wait((0, 1, 1))
    for step in (1, 3):
        spread((0, 1, 1), (step, 1, 1), peer_at(step))
    relay(0, 1)
    wait((2, 0, 0))
    spread((2, 0, 0), (2, 1, 0), terms.partner)
    settle((0, 0, 1))
    settle((0, 1, 1))
    relay(1, 1)
    for step in (1, 3, 2):
        settle((step, 0, 0))
    wait((0, 1, 0))
    settle((0, 1, 0))
    settle((1, 0, 1))
    settle((3, 0, 1))
    settle((1, 1, 1))
    settle((3, 1, 1))
    for slot in ((2, 0, 1), (1, 1, 0), (3, 1, 0), (2, 1, 1), (2, 1, 0)):
        wait(slot)
        settle(slot)
    terms.close()
    links.close()


def sum_middle(n, partial_out, tokens, mlp_gain):
    rows, width = tokens.shape
    piece = rows // n
    whole_shape = jax.ShapeDtypeStruct((rows, width), jnp.bfloat16)
    return pl.pallas_call(
        functools.partial(middle_kernel, n),
        name="sum_middle",
        cost_estimate=pl.CostEstimate(flops=0, bytes_accessed=200_000_000, transcendentals=0),
        out_shape=(whole_shape, whole_shape),
        in_specs=[VMEM_SPEC] * 3,
        out_specs=(VMEM_SPEC, VMEM_SPEC),
        scratch_shapes=scatter_scratch(n, (piece // 2, width))
        + [pltpu.VMEM((n // 2, 2, 2, piece // 2, width), jnp.bfloat16)]
        + [pltpu.SemaphoreType.DMA((2 * n + 1,))] * 2,
        compiler_params=pltpu.CompilerParams(collective_id=0, has_side_effects=True),
    )(partial_out.reshape(n, 2, piece // 2, width), tokens, mlp_gain.reshape(1, width))


def hidden_kernel(
    n, normed_ref, middle_hbm, pair_hbm, down_hbm, out_ref, pair, down, hidden, terms,
    window, turned, pair_sem, down_sem, window_sem,
    land_a, land_b, stage_a, stage_b, got_a, got_b, send, recv,
):
    me = lax.axis_index("kv")
    rows, width = normed_ref.shape
    halves, part = terms.shape[0], terms.shape[2]
    piece = width // n
    tiles = pair.shape[3] // 256
    units = down.shape[0]
    barrier = hail(n, me)

    def bring(tile):
        lanes = pl.ds(pl.multiple_of(tile * 256, 256), 256)
        return [
            pltpu.make_async_copy(
                pair_hbm.at[:, side, :, lanes], pair.at[side, :, :, lanes], pair_sem.at[tile, side]
            )
            for side in range(2)
        ]

    for tile in range(tiles):
        for copy in bring(tile):
            copy.start()
    fetch = pltpu.make_async_copy(down_hbm, down, down_sem)
    fetch.start()
    left = lax.div(me * piece, 128) * 128
    view = pltpu.make_async_copy(
        middle_hbm.at[:, pl.ds(pl.multiple_of(left, 128), window.shape[1])], window, window_sem
    )
    view.start()

    def exchange(half):
        def term(owner, side):
            start = pl.multiple_of(owner * piece + side * (piece // 2), piece // 2)
            return terms.at[half, pl.ds(start, piece // 2)]

        landings = [ref.at[half] for ref in (land_a, land_b, stage_a, stage_b, got_a, got_b)]
        return Scatter(n, me, term, landings, send.at[half], recv.at[half])

    sums = [exchange(half) for half in range(halves)]
    for half in range(halves):
        lines = slice(half * part, (half + 1) * part)

        @pl.loop(0, tiles)
        def _(tile):
            if half == 0:
                for copy in bring(tile):
                    copy.wait()
            lanes = pl.ds(pl.multiple_of(tile * 256, 256), 256)
            both = jnp.dot(
                normed_ref[lines, :],
                pair[:, :, :, lanes].reshape(width, 256),
                preferred_element_type=jnp.float32,
            )
            gate, up = both[:, :128], both[:, 128:]
            hidden[:, pl.ds(pl.multiple_of(tile * 128, 128), 128)] = (
                gate / (1.0 + jnp.exp(-gate)) * up
            ).astype(jnp.bfloat16)

        if half == 0:
            fetch.wait()

        @pl.loop(0, width // 512)
        def _(tile):
            spot = pl.ds(pl.multiple_of(tile * 512, 512), 512)
            term = jnp.dot(
                hidden[:, :units], down[:, spot], preferred_element_type=jnp.float32
            )
            terms[half, spot, :] = term.T.astype(jnp.bfloat16)

        if half == 0:
            pl.semaphore_wait(barrier, n - 1)
        sums[half].open()
    view.wait()
    turned[...] = window[...].astype(jnp.float32).T
    for half in range(halves):
        sums[half].forward()
    shift = me * piece - left
    for half in range(halves):
        lines = slice(half * part, (half + 1) * part)
        for side, finish in enumerate((sums[half].finish_a, sums[half].finish_b)):
            residual = pl.ds(pl.multiple_of(shift + side * (piece // 2), 32), piece // 2)
            place = slice(side * (piece // 2), (side + 1) * (piece // 2))
            out_ref[place, lines] = turned[residual, lines] + finish()
    for half in range(halves):
        sums[half].close()


def feed_forward(n, normed_mid, middle, w_pair, w_down):
    rows, width = normed_mid.shape
    halves = 2
    part = rows // halves
    piece = width // n
    half = jnp.bfloat16
    dma = pltpu.SemaphoreType.DMA
    any_spec = pl.BlockSpec(memory_space=pl.ANY)
    return pl.pallas_call(
        functools.partial(hidden_kernel, n),
        name="feed_forward",
        out_shape=jax.ShapeDtypeStruct((piece, rows), jnp.float32),
        in_specs=[VMEM_SPEC, any_spec, any_spec, any_spec],
        out_specs=VMEM_SPEC,
        scratch_shapes=[
            pltpu.VMEM((2, w_pair.shape[0]) + w_pair.shape[2:], half),
            pltpu.VMEM(w_down.shape, half),
            pltpu.VMEM((part, w_pair.shape[3] // 2), half),
            pltpu.VMEM((halves, width, part), half),
            pltpu.VMEM((rows, piece + 64), half),
            pltpu.VMEM((piece + 64, rows), jnp.float32),
            dma((w_pair.shape[3] // 256, 2)),
            dma,
            dma,
        ]
        + scatter_scratch(n, (piece // 2, part), halves),
        compiler_params=pltpu.CompilerParams(
            collective_id=1, has_side_effects=True, vmem_limit_bytes=56 * 1024 * 1024
        ),
    )(normed_mid, middle, w_pair, w_down)


def pack_pairs(first, second, groups):
    rows, columns = first.shape
    units = columns // groups
    padded = -(-units // 128) * 128
    tiles = [
        jnp.pad(
            matrix.astype(jnp.bfloat16).reshape(rows, groups, units),
            ((0, 0), (0, 0), (0, padded - units)),
        ).reshape(rows, groups, -1, 1, 128)
        for matrix in (first, second)
    ]
    return jnp.transpose(jnp.concatenate(tiles, axis=3), (1, 0, 2, 3, 4)).reshape(groups, rows, -1)


def shards(
    tokens,
    attn_gain,
    mlp_gain,
    w_query,
    w_key,
    w_value,
    w_gate,
    w_up,
    w_out,
    w_down,
    cache,
    slot_prompt,
    prefix_len,
    new_len,
):
    groups = lax.axis_size("kv")
    n_blocks = lax.axis_size("blk")
    blk_index = lax.axis_index("blk")
    new_rows = tokens.shape[0]
    prompts = prefix_len.shape[0]
    slots = cache.shape[1]
    row_ids = jnp.arange(new_rows, dtype=jnp.int32)
    frequency = ROPE_BASE ** (-2.0 * jnp.arange(HD // 2, dtype=jnp.float32) / HD)
    positions = (prefix_len[blk_index] + row_ids).astype(jnp.float32)
    angles = positions[None, :] * frequency[:, None]
    own_prompts = lax.dynamic_slice_in_dim(slot_prompt, blk_index * slots, slots)
    earlier = jnp.tri(slots, k=-1, dtype=jnp.bool_)
    own_ranks = jnp.sum(
        ((own_prompts[:, None] == own_prompts[None, :]) & earlier).astype(jnp.int32), axis=1
    )
    own_slots = jnp.arange(slots, dtype=jnp.int32)
    wanted = jnp.arange(prompts + 1, dtype=jnp.int32)[:, None]
    matches = jnp.where(
        wanted < prompts,
        (own_prompts[None, :] == wanted) & (own_ranks[None, :] == 0),
        own_ranks[None, :] == 1,
    )
    source_slot = jnp.sum(jnp.where(matches, own_slots[None, :], 0), axis=1)
    by_slot = jnp.transpose(cache.reshape(2, slots, HD, BLOCK), (1, 0, 2, 3))
    outgoing = jnp.take(by_slot, source_slot, axis=0, mode="clip")
    projected, w_second, arrived = regroup(
        groups,
        n_blocks,
        pack_groups((w_query, w_key, w_value), groups),
        pack_pairs(w_gate, w_up, groups),
        outgoing[:prompts],
        outgoing[prompts],
        tokens,
        attn_gain,
    )
    line = n_blocks // 2
    facing = [[spot, spot + line] for spot in range(line)]
    sides = [list(range(line)), list(range(line, n_blocks))]
    w_both = lax.all_gather(w_second, "blk", axis=0, axis_index_groups=facing)
    attended = attend(
        HEADS // groups,
        slot_prompt,
        prefix_len,
        new_len,
        projected,
        jnp.cos(angles),
        jnp.sin(angles),
        arrived.reshape(prompts * CAP, 2, HD, BLOCK),
    ).reshape(-1, new_rows)
    attended, w_both = lax.optimization_barrier((attended, w_both))
    w_pair = lax.all_gather(w_both, "blk", axis=0, axis_index_groups=sides)
    projected_out = lax.dot_general(
        attended, w_out, (((0,), (0,)), ((), ())), preferred_element_type=jnp.float32
    )
    partial_out = projected_out.astype(jnp.bfloat16)
    middle, normed_mid = sum_middle(groups, partial_out, tokens, mlp_gain)
    summed = feed_forward(groups, normed_mid, middle, w_pair, w_down).T
    mixed = jnp.where((row_ids < new_len[blk_index])[:, None], summed, 0.0)
    return mixed.astype(jnp.bfloat16)


def solution(mesh):
    return jax.shard_map(
        shards,
        mesh=mesh,
        in_specs=(
            P("blk", None),
            P(),
            P(),
            P(("blk", "kv"), None),
            P(("blk", "kv"), None),
            P(("blk", "kv"), None),
            P(("blk", "kv"), None),
            P(("blk", "kv"), None),
            P("kv", None),
            P("kv", None),
            P(None, "blk", "kv", None, None),
            P(),
            P(),
            P(),
        ),
        out_specs=P("blk", "kv"),
        check_vma=False,
    )
```
